32 devices in a mesh: groups: 2 (over y), seq: 4 (over z), head: 2 (over x), sub: 2 (over core).
Axes of the slice: x: 2, y: 2, z: 4, core: 2. Of those that a mesh axis runs over, the one named last changes fastest.
Arguments:
- token_values: bfloat16 [16384, 5120], P(('groups', 'seq', 'sub'), 'head'), parts along dimension 0, may hold values from -6 to 6
- gate_values: bfloat16 [16384, 5120], P(('groups', 'seq', 'sub'), 'head'), parts along dimension 0, may hold values from -80 to 80
- state_input: bfloat16 [16384, 128], P(('groups', 'seq', 'sub')), parts along dimension 0, may hold values from -6 to 6
- state_readout: bfloat16 [16384, 128], P(('groups', 'seq', 'sub')), parts along dimension 0, may hold values from -6 to 6
- step_raw: float32 [80, 8192], P('head', ('seq', 'sub')), may hold values from -3 to 16
- step_bias: float32 [80], P('head'), may hold values from -16 to -3
- decay_log: float32 [80], P('head'), may hold values from 0 to 2.78
- skip_gain: float32 [80], P('head'), may hold values from 0.5 to 2
- norm_gain: float32 [5120], P('head'), may hold values from 0.5 to 1.5
- document_ids: int32 [16384], P(('groups', 'seq', 'sub')), parts along dimension 0, may hold values from 0 to 8191, as said below
- live_blocks: int32 [16], P(('groups', 'seq', 'sub')), parts along dimension 0, may hold values from 1 to 4, as said below
Outputs:
- normalized: bfloat16 [16384, 5120], P(('groups', 'seq', 'sub'), 'head'), parts along dimension 0
The draws below stay inside these ranges and needn't reach their ends.
There are 2 independent parts, one for each index of `groups`. The reference program is written for one: setup_inputs(seed, part) draws one part's arguments, and reference() takes and returns one part's arrays. A program takes and returns all parts, laid end to end along the dimension named above; an argument that names none is the same for every part. Nothing has to cross between parts.
Inputs may be any that keep to these rules, and one draw needn't show every extreme that they name: `document_ids`: never falling along the sequence, 0 at the first position, 8191 at the last, and unchanged over the padding positions that follow a shard's live blocks. `live_blocks`: the number of live blocks of 256 positions at the start of each shard of 1024 positions; the rest of a shard is padding; some shard has 4 and some has 1.
All inputs are finite; a program needn't handle non-finite values.
Results may differ from the reference program's by a relative error of at most 0.003.
Values sent between devices are 32-bit elements; how exact they have to be, the bound alone decides.
No kernel may reach another device: no remote copies, remote signals or barrier semaphores. Data moves between devices by JAX's collectives and lax.ppermute only.
A program may use at most 192 MiB of HBM per device.

```python
import math
import jax
import jax.numpy as jnp
from jax import lax

HEADS = 80
STATE = 128
BLOCK = 256
SHARD_BLOCKS = 4
TOK_DEV = 1024
SEQUENCE_SHARDS = 8
TOKENS = 8192
CHANNELS = 5120


def head_plan(key):
    layout_key = jax.random.fold_in(key, 7001)
    key_slow, key_rate, key_long, key_short = jax.random.split(layout_key, 4)
    share = 5
    slow_flag = jax.random.randint(key_slow, (HEADS,), 0, 10) < share
    rate_scale = jnp.exp(jax.random.uniform(key_rate, (HEADS,), jnp.float32, 0.0, math.log(16.0)))
    long_base = jnp.exp(jax.random.uniform(key_long, (HEADS,), jnp.float32, math.log(0.15), math.log(0.5))) / (rate_scale * TOKENS)
    short_base = jnp.exp(jax.random.uniform(key_short, (HEADS,), jnp.float32, math.log(0.02), math.log(0.04))) / rate_scale
    base_step = jnp.where(slow_flag, long_base, short_base)
    return (rate_scale, jnp.log(jnp.expm1(base_step)))


def draw_decay_log(key, part):
    rate_scale, bias_amount = head_plan(key)
    return jnp.log(rate_scale).astype(jnp.float32)


def draw_step_bias(key, part):
    rate_scale, bias_amount = head_plan(key)
    return bias_amount.astype(jnp.float32)


def draw_step_raw(key, part):
    rate_scale, bias_amount = head_plan(key)
    raw_key = jax.random.fold_in(key, 7002)
    key_noise, key_offset, key_spot, key_frac = jax.random.split(raw_key, 4)
    jitter_values = jnp.clip(0.5 * jax.random.normal(key_noise, (HEADS, TOKENS), jnp.float32), -2.0, 2.0)
    offsets = jax.random.uniform(key_offset, (HEADS, TOKENS // BLOCK), jnp.float32, -0.7, 0.7)
    smoothing_factor = jnp.repeat(offsets, BLOCK, axis=1)
    spots = jax.random.randint(key_spot, (HEADS, 3), 0, TOKENS)
    fractions = jax.random.uniform(key_frac, (HEADS, 3), jnp.float32, 0.2, 0.4)
    desired_total = -jnp.log1p(-fractions) / rate_scale[:, None]
    spike_unscaled = jnp.log(jnp.expm1(desired_total)) - bias_amount[:, None]
    match_total = jnp.arange(TOKENS, dtype=jnp.int32)[None, :, None] == spots[:, None, :]
    spike_amount = jnp.sum(jnp.where(match_total, spike_unscaled[:, None, :], 0.0), axis=2)
    return jnp.where(jnp.any(match_total, axis=2), spike_amount, jitter_values + smoothing_factor).astype(jnp.float32)


def draw_gate_values(key, part):
    gate_key = jax.random.fold_in(key, 7201)
    key_base, key_scale = jax.random.split(gate_key, 2)
    channel_pos = jnp.arange(CHANNELS, dtype=jnp.float32) / (CHANNELS - 1)
    base_values = jnp.clip(jax.random.normal(key_base, (TOKENS, CHANNELS), jnp.float32), -4.0, 4.0)
    rising = 1.0 + 2.0 * channel_pos
    token_scale = jnp.exp(jax.random.uniform(key_scale, (TOKENS, 1), jnp.float32, math.log(0.5), math.log(5.0)))
    return (base_values * token_scale * rising[None, :]).astype(jnp.bfloat16)


def pack_plan(key):
    layout_key = jax.random.fold_in(key, 7101)
    key_tally, key_complete, key_lone, key_extra, key_limit = jax.random.split(layout_key, 5)
    extra_flag = jax.random.randint(key_extra, (SEQUENCE_SHARDS,), 0, 3) == 0
    tally_values = 1 + jnp.where(extra_flag, jax.random.randint(key_tally, (SEQUENCE_SHARDS,), 0, SHARD_BLOCKS), 0)
    full_at = jax.random.randint(key_complete, (), 0, SEQUENCE_SHARDS)
    single_at = (full_at + 1 + jax.random.randint(key_lone, (), 0, SEQUENCE_SHARDS - 1)) % SEQUENCE_SHARDS
    tally_values = tally_values.at[full_at].set(SHARD_BLOCKS).at[single_at].set(1)
    positions = jnp.arange(TOKENS, dtype=jnp.int32)
    is_live = positions % TOK_DEV < BLOCK * tally_values[positions // TOK_DEV]
    starts = (jax.random.randint(key_limit, (TOKENS,), 0, 4 * BLOCK) == 0) & is_live & (positions > 0)
    starts = starts | (positions == BLOCK // 2)
    doc_number = jnp.cumsum(starts.astype(jnp.int32))
    doc_number = jnp.where(doc_number == doc_number[-1], TOKENS - 1, doc_number)
    return (tally_values.astype(jnp.int32), doc_number.astype(jnp.int32))


def draw_document_ids(key, part):
    tally_values, doc_number = pack_plan(key)
    return doc_number


def draw_live_blocks(key, part):
    tally_values, doc_number = pack_plan(key)
    return tally_values


def shard_levels(key, shape, shards, least, high):
    def one(axis_at, shards_of):
        heights = jax.random.uniform(jax.random.fold_in(jax.random.fold_in(key, 6), axis_at), (shards_of,), jnp.float32, least / len(shards), high / len(shards))
        return jnp.repeat(jnp.exp(heights), shape[axis_at] // shards_of).reshape((-1,) + (1,) * (len(shape) - axis_at - 1))

    factor_of = one(*shards[0])
    for cut in shards[1:]:
        factor_of = factor_of * one(*cut)
    return factor_of


def bell_draw(key, extent, deviation, most, cuts=(), kind=jnp.bfloat16):
    level = shard_levels(key, extent, cuts, -0.22, 0.18) if cuts else 1.0
    drawn = jax.random.normal(key, extent, jnp.float32) * deviation * level
    return jnp.minimum(jnp.maximum(drawn, -most), most).astype(kind)


def setup_inputs(seed: int = 0, part: int = 0) -> dict:
    key_of = jax.random.split(jax.random.key(seed), 12)
    part_keys = jax.random.split(jax.random.fold_in(key_of[11], part), 12)
    token_values = bell_draw(part_keys[0], (TOKENS, CHANNELS), 1.0, 6.0, ((0, 8), (1, 2)))
    gate_values = draw_gate_values(jax.random.fold_in(jax.random.fold_in(key_of[11], part), 71), part)
    state_input = bell_draw(part_keys[2], (TOKENS, STATE), 1.0, 6.0, ((0, 8),))
    state_readout = bell_draw(part_keys[3], (TOKENS, STATE), 1.0, 6.0, ((0, 8),))
    step_raw = draw_step_raw(jax.random.fold_in(key_of[11], 71), part)
    step_bias = draw_step_bias(jax.random.fold_in(key_of[11], 71), part)
    decay_log = draw_decay_log(jax.random.fold_in(key_of[11], 71), part)
    skip_gain = jnp.clip(0.5 + 1.5 * jax.random.uniform(key_of[7], (HEADS,), jnp.float32) ** shard_levels(key_of[7], (HEADS,), ((0, 2),), -0.2, 0.2), 0.5, 2.0)
    norm_gain = jnp.clip(1.0 + 0.1 * jax.random.normal(key_of[8], (CHANNELS,), jnp.float32), 0.5, 1.5)
    document_ids = draw_document_ids(jax.random.fold_in(jax.random.fold_in(key_of[11], part), 71), part)
    live_blocks = draw_live_blocks(jax.random.fold_in(jax.random.fold_in(key_of[11], part), 71), part)
    return {"token_values": token_values, "gate_values": gate_values, "state_input": state_input, "state_readout": state_readout, "step_raw": step_raw, "step_bias": step_bias, "decay_log": decay_log, "skip_gain": skip_gain, "norm_gain": norm_gain, "document_ids": document_ids, "live_blocks": live_blocks}


def block_terms(values, inputs, readout, doc_here, prior_doc, cum_here, steps_here):
    affinity = jnp.dot(readout, inputs.T, preferred_element_type=jnp.float32)
    block_positions = jnp.arange(readout.shape[0], dtype=jnp.int32)
    allowed = (block_positions[:, None] >= block_positions[None, :]) & (doc_here[:, None] == doc_here[None, :])
    spread = cum_here[:, :, None] - cum_here[:, None, :]
    decayed = jnp.where(allowed[None], jnp.exp(jnp.minimum(spread, 0.0)), 0.0)
    weights = (affinity[None] * decayed * steps_here[:, None, :]).astype(jnp.bfloat16)
    inner_out = jnp.einsum('hts,shp->thp', weights.astype(jnp.float32), values.astype(jnp.float32))
    to_end = steps_here * jnp.exp(cum_here[:, -1:] - cum_here) * (doc_here == doc_here[-1]).astype(jnp.float32)[None, :]
    scaled = (inputs.astype(jnp.float32)[None] * to_end[:, :, None]).astype(jnp.bfloat16)
    block_state = jnp.einsum('shp,hsn->hpn', values.astype(jnp.float32), scaled.astype(jnp.float32))
    entry_rate = jnp.exp(cum_here) * (doc_here == prior_doc).astype(jnp.float32)[None, :]
    return (inner_out, block_state, entry_rate)

def reference(token_values, gate_values, state_input, state_readout, step_raw, step_bias, decay_log, skip_gain, norm_gain, document_ids, live_blocks):
    total_len = token_values.shape[0]
    num_heads = step_raw.shape[0]
    head_width = token_values.shape[1] // num_heads
    state_width = state_input.shape[1]
    num_blocks = total_len // BLOCK
    positions = jnp.arange(total_len, dtype=jnp.int32)
    is_live = positions % TOK_DEV < BLOCK * live_blocks[positions // TOK_DEV]
    step_size = jnp.where(is_live[None, :], jax.nn.softplus(step_raw + step_bias[:, None]), 0.0)
    log_rate = -jnp.exp(decay_log)[:, None] * step_size
    cumulated = jnp.cumsum(log_rate.reshape(num_heads, num_blocks, BLOCK), axis=2).transpose(1, 0, 2)
    step_blocks = step_size.reshape(num_heads, num_blocks, BLOCK).transpose(1, 0, 2)
    items = (token_values.reshape(num_blocks, BLOCK, num_heads, head_width), state_input.reshape(num_blocks, BLOCK, state_width), state_readout.reshape(num_blocks, BLOCK, state_width), document_ids.reshape(num_blocks, BLOCK), cumulated, step_blocks)

    def advance(carried, item):
        state_now, prior_doc = carried
        values, inputs, readout, doc_here, cum_here, steps_here = item
        inner_out, block_state, entry_rate = block_terms(values, inputs, readout, doc_here, prior_doc, cum_here, steps_here)
        outer = jnp.einsum('tn,hpn->thp', readout.astype(jnp.float32), state_now, precision=lax.Precision.HIGHEST) * entry_rate.T[:, :, None]
        new_state = entry_rate[:, -1][:, None, None] * state_now + block_state
        return ((new_state, doc_here[-1]), inner_out + outer)
    start_state = jnp.zeros((num_heads, head_width, state_width), jnp.float32)
    scan_rest, mixed = lax.scan(advance, (start_state, document_ids[0]), items)
    mixed = mixed.reshape(total_len, num_heads, head_width)
    mixed = mixed + skip_gain[None, :, None] * token_values.reshape(total_len, num_heads, head_width).astype(jnp.float32)
    mixed = jnp.where(is_live[:, None, None], mixed, 0.0).reshape(total_len, num_heads * head_width)
    gated = mixed * jax.nn.silu(gate_values.astype(jnp.float32))
    scale_row = lax.rsqrt(lax.optimization_barrier(jnp.mean(gated * gated, axis=1)) + 1e-05)
    return (gated * norm_gain * scale_row[:, None]).astype(jnp.bfloat16)
```

```python
import functools
import math

import jax
import jax.numpy as jnp
from jax import lax
from jax.experimental import pallas as pl
from jax.experimental.pallas import tpu as pltpu
from jax.sharding import PartitionSpec as P

BLOCK = 256
LANES = 128
LOG2E = math.log2(math.e)
F32 = jnp.float32
BF16 = jnp.bfloat16


def dot(a, b, contract=((1,), (0,))):
    return lax.dot_general(a, b, (contract, ((), ())), preferred_element_type=F32)


def two_parts(value):
    high = value.astype(BF16)
    low = (value - high.astype(F32)).astype(BF16)
    return high, low


def pick_row(ref, base, count, k, cols):
    row = ref[base : base + 1, cols]
    for j in range(1, count):
        row = jnp.where(k == j, ref[base + j : base + j + 1, cols], row)
    return row


def softplus(v):
    u = jnp.exp(-jnp.abs(v))
    s = u / (2.0 + u)
    q = s * s
    series = jnp.full_like(q, 1.0 / 17.0)
    for odd in (15, 13, 11, 9, 7, 5, 3, 1):
        series = series * q + 1.0 / odd
    return jnp.maximum(v, 0.0) + 2.0 * s * series


def state_kernel(
    heads,
    width,
    live_ref,
    docs_ref,
    raw_ref,
    par_ref,
    doc_row_ref,
    skip_ref,
    x_ref,
    b_ref,
    g_ref,
    col_ref,
    enter_ref,
    sum_ref,
    row_ref,
    pack,
    decay_col,
    spread,
    state,
    scal,
):
    k = pl.program_id(0)
    blocks = pl.num_programs(0)
    length = raw_ref.shape[1]
    count = length // BLOCK
    channels = x_ref.shape[1]
    tiles = channels // LANES
    ends = [docs_ref[j * BLOCK + BLOCK - 1] for j in range(count)]

    @pl.when(k == 0)
    def _():
        rows = raw_ref.shape[0]
        lane = lax.broadcasted_iota(jnp.int32, (1, length), 1)
        step = softplus(raw_ref[...] + par_ref[:, 0:1])
        step = jnp.where(lane < live_ref[0] * BLOCK, step, 0.0)
        cum = (-LOG2E * jnp.exp(par_ref[:, 1:2])) * step
        within = jnp.bitwise_and(lane, BLOCK - 1)
        shift = 1
        while shift < BLOCK:
            cum = cum + jnp.where(within >= shift, pltpu.roll(cum, shift, 1), 0.0)
            shift *= 2
        g_ref[...] = cum - jnp.where(step > 0.0, LOG2E * jnp.log(step), -1e30)
        pack[...] = jnp.zeros_like(pack)
        pack[0:rows, :] = cum
        pack[LANES - 1 : LANES, :] = doc_row_ref[...].astype(F32)
        col_ref[...] = pack[...].T
        pack[LANES - 1 : LANES, :] = jnp.zeros((1, length), F32)
        for j in range(count):
            piece = slice(j * BLOCK, (j + 1) * BLOCK)
            last = cum[:, (j + 1) * BLOCK - 1 : (j + 1) * BLOCK]
            same = doc_row_ref[:, piece] == ends[j]
            pack[0:rows, piece] = jnp.where(
                same, step[:, piece] * jnp.exp2(last - cum[:, piece]), 0.0
            )
        high, low = two_parts(pack[...].T)
        decay_col[:, 0:LANES] = high
        decay_col[:, LANES:] = low
        first = lax.broadcasted_iota(jnp.int32, (LANES, channels), 0) * width
        chan = lax.broadcasted_iota(jnp.int32, (LANES, channels), 1)
        hot = jnp.where((chan >= first) & (chan < first + width), 1.0, 0.0).astype(BF16)
        spread[0:LANES, :] = hot
        spread[LANES:, :] = hot
        head_lane = lax.broadcasted_iota(jnp.int32, (1, LANES), 1) < heads
        before = jnp.zeros((1, LANES), F32)
        scal[...] = jnp.zeros_like(scal)
        for j in range(count):
            end = jnp.where(head_lane, col_ref[(j + 1) * BLOCK - 1 : (j + 1) * BLOCK, :], 0.0)
            scal[j : j + 1, :] = jnp.where(head_lane, jnp.exp2(end), 0.0)
            scal[count + j : count + j + 1, :] = jnp.where(head_lane, jnp.exp2(before), 0.0)
            before = before + end
        scal[2 * count : 2 * count + 1, :] = jnp.where(head_lane, jnp.exp2(before), 0.0)
        scal[2 * count + 1 : 2 * count + 2, :] = skip_ref[...]
        high, low = two_parts(scal[...])
        row_ref[...] = dot(jnp.concatenate([high, low], axis=1), spread[...])
        state[...] = jnp.zeros_like(state)

    start = pl.multiple_of(k * BLOCK, BLOCK)
    end_doc = docs_ref[k * BLOCK + BLOCK - 1]
    prior_doc = docs_ref[jnp.maximum(k * BLOCK - 1, 0)]
    link = jnp.where(end_doc == prior_doc, 1.0, 0.0)
    decay = decay_col[pl.ds(start, BLOCK), :]
    inputs_t = b_ref[...].T
    wide = LANES * math.gcd(tiles, 5)
    for c in range(0, channels, wide):
        cols = slice(c, c + wide)
        old = state[:, cols]
        high, low = two_parts(old)
        enter_ref[0, 0 : state.shape[0], cols] = high
        enter_ref[0, state.shape[0] :, cols] = low
        scaled = (x_ref[:, cols].astype(F32) * dot(decay, spread[:, cols])).astype(BF16)
        passage = pick_row(row_ref, 0, count, k, cols) * link
        state[:, cols] = passage * old + dot(inputs_t, scaled)

    @pl.when(k == blocks - 1)
    def _():
        half = state.shape[0] // 2
        whole = jnp.where(ends[count - 1] == docs_ref[0], 1.0, 0.0)
        for side in range(2):
            for j in range(tiles):
                sum_ref[side, j * half : (j + 1) * half, :] = state[
                    side * half : (side + 1) * half, j * LANES : (j + 1) * LANES
                ]
                sum_ref[side, tiles * half + j : tiles * half + j + 1, :] = (
                    row_ref[2 * count : 2 * count + 1, j * LANES : (j + 1) * LANES] * whole
                )
            base = tiles * half + tiles
            sum_ref[side, base : base + 1, :] = jnp.full((1, LANES), docs_ref[0].astype(F32))
            sum_ref[side, base + 1 : base + 2, :] = jnp.full(
                (1, LANES), docs_ref[length - 1].astype(F32)
            )


def inner_kernel(
    width,
    first_tile,
    count,
    live_ref,
    docs_ref,
    x_ref,
    z_ref,
    b_ref,
    c_ref,
    g_ref,
    col_ref,
    doc_row_ref,
    enter_ref,
    row_ref,
    y_ref,
    f_ref,
):
    k = pl.program_id(0)
    half = BLOCK // 2
    per_tile = LANES // width

    @pl.when(k >= live_ref[0])
    def _():
        y_ref[...] = jnp.zeros_like(y_ref)
        f_ref[...] = jnp.zeros_like(f_ref)

    @pl.when(k < live_ref[0])
    def _():
        readout = c_ref[...]
        affinity = dot(readout, b_ref[...], ((1,), (1,)))
        doc_col = col_ref[:, LANES - 1 : LANES]
        doc_row = doc_row_ref[...].astype(F32)
        t = lax.broadcasted_iota(jnp.int32, (BLOCK, BLOCK), 0)
        s = lax.broadcasted_iota(jnp.int32, (BLOCK, BLOCK), 1)
        affinity = jnp.where((t >= s) & (doc_col == doc_row), affinity, 0.0)
        prior_doc = docs_ref[jnp.maximum(k * BLOCK - 1, 0)].astype(F32)
        first_doc = docs_ref[0].astype(F32)
        link = jnp.broadcast_to(jnp.where(doc_col == prior_doc, 1.0, 0.0), (BLOCK, LANES))
        link_first = jnp.broadcast_to(jnp.where(doc_col == first_doc, 1.0, 0.0), (BLOCK, LANES))
        lane = lax.broadcasted_iota(jnp.int32, (1, LANES), 1)
        twice = jnp.concatenate([readout, readout], axis=1)
        for j in range(x_ref.shape[1] // LANES):
            cols = slice(j * LANES, (j + 1) * LANES)
            x = x_ref[:, cols]
            tops, bottoms, masked = [], [], []
            exponent = None
            for i in range(per_tile):
                h = (first_tile + j) * per_tile + i
                cum = jnp.broadcast_to(col_ref[:, h : h + 1], (BLOCK, LANES))
                g = g_ref[h : h + 1, :]
                wide = jnp.concatenate([cum[half:], cum[half:]], axis=1)
                top = jnp.exp2(jnp.minimum(cum[:half] - g[:, :half], 64.0))
                bottom = jnp.exp2(jnp.minimum(wide - g, 64.0))
                tops.append((top * affinity[:half, :half]).astype(BF16))
                bottoms.append((bottom * affinity[half:, :]).astype(BF16))
                mine = (lane >= i * width) & (lane < (i + 1) * width)
                masked.append(x * jnp.where(mine, 1.0, 0.0).astype(BF16))
                exponent = cum if exponent is None else jnp.where(mine, cum, exponent)
            upper = dot(
                jnp.concatenate(tops, axis=1),
                jnp.concatenate([m[:half] for m in masked], axis=0),
            )
            lower = dot(jnp.concatenate(bottoms, axis=1), jnp.concatenate(masked, axis=0))
            inner = jnp.concatenate([upper, lower], axis=0)
            enter = jnp.exp2(exponent)
            outer = dot(twice, enter_ref[0, :, cols])
            skip = row_ref[2 * count + 1 : 2 * count + 2, cols]
            y = inner + enter * link * outer + skip * x.astype(F32)
            z = z_ref[:, cols].astype(F32)
            gate = z / (1.0 + jnp.exp2(-LOG2E * z))
            y_ref[:, cols] = y * gate
            f_ref[:, cols] = enter * pick_row(row_ref, count, count, k, cols) * (link_first * gate)


def join_kernel(sub_ref, own_ref, other_ref, c_ref, *refs):
    pieces = (len(refs) - 3) // 2
    y_refs, f_refs = refs[:pieces], refs[pieces : 2 * pieces]
    gated_ref, square_ref, carry = refs[2 * pieces :]
    tiles, half = own_ref.shape[0], own_ref.shape[1]

    @pl.when(pl.program_id(0) == 0)
    def _():
        mine = pl.multiple_of(sub_ref[0] * half, half)
        theirs = pl.multiple_of((1 - sub_ref[0]) * half, half)
        for j in range(tiles):
            cols = slice(j * LANES, (j + 1) * LANES)
            high, low = two_parts(own_ref[j])
            carry[pl.ds(mine, half), cols] = high
            carry[pl.ds(2 * half + mine, half), cols] = low
            high, low = two_parts(other_ref[j])
            carry[pl.ds(theirs, half), cols] = high
            carry[pl.ds(2 * half + theirs, half), cols] = low

    twice = jnp.concatenate([c_ref[...], c_ref[...]], axis=1)
    total = jnp.zeros((c_ref.shape[0], LANES), F32)
    at = 0
    for y_ref, f_ref in zip(y_refs, f_refs):
        for j in range(y_ref.shape[1] // LANES):
            here = slice(j * LANES, (j + 1) * LANES)
            cols = slice(at, at + LANES)
            gated = y_ref[:, here] + f_ref[:, here] * dot(twice, carry[:, cols])
            gated_ref[:, cols] = gated
            total = total + gated * gated
            at += LANES
    square_ref[0] = jnp.sum(total.T, axis=0, keepdims=True)


def norm_kernel(channels_all, square_ref, gain_ref, gated_ref, out_ref):
    rows = gated_ref.shape[0]
    scale = lax.rsqrt(square_ref[0] / channels_all + 1e-05)
    scale = jnp.broadcast_to(scale, (LANES, rows)).T
    for j in range(gated_ref.shape[1] // LANES):
        cols = slice(j * LANES, (j + 1) * LANES)
        out_ref[:, cols] = (gated_ref[:, cols] * gain_ref[:, cols] * scale).astype(BF16)


def whole(shape):
    return pl.BlockSpec(shape, lambda k, *_: (0,) * len(shape))


SMEM = pl.BlockSpec(memory_space=pltpu.SMEM)


def on_device(
    token_values,
    gate_values,
    state_input,
    state_readout,
    step_raw,
    step_bias,
    decay_log,
    skip_gain,
    norm_gain,
    document_ids,
    live_blocks,
):
    length, channels = token_values.shape
    heads = step_raw.shape[0]
    width = channels // heads
    states = state_input.shape[1]
    half = states // 2
    count = length // BLOCK
    tiles = channels // LANES
    rows = -(-heads // 8) * 8
    scalars = -(-(2 * count + 2) // 16) * 16
    extra = -(-(tiles + 2) // 8) * 8
    assert lax.axis_size("sub") == 2 and heads < LANES and 2 * half == states

    params = jnp.stack([step_bias, decay_log], axis=1)
    raw = step_raw
    if rows != heads:
        params = jnp.pad(params, ((0, rows - heads), (0, 0)))
        raw = jnp.pad(raw, ((0, rows - heads), (0, 0)))
    skip_row = jnp.pad(skip_gain, (0, LANES - heads)).reshape(1, LANES)
    doc_row = document_ids.reshape(1, length)

    g, col, enter, sums, row = pl.pallas_call(
        functools.partial(state_kernel, heads, width),
        grid=(count,),
        in_specs=[
            SMEM,
            SMEM,
            whole((rows, length)),
            whole((rows, 2)),
            whole((1, length)),
            whole((1, LANES)),
            pl.BlockSpec((BLOCK, channels), lambda k: (k, 0)),
            pl.BlockSpec((BLOCK, states), lambda k: (k, 0)),
        ],
        out_specs=[
            whole((rows, length)),
            whole((length, LANES)),
            pl.BlockSpec((1, 2 * states, channels), lambda k: (k, 0, 0)),
            whole((2, tiles * half + extra, LANES)),
            whole((scalars, channels)),
        ],
        out_shape=[
            jax.ShapeDtypeStruct((rows, length), F32),
            jax.ShapeDtypeStruct((length, LANES), F32),
            jax.ShapeDtypeStruct((count, 2 * states, channels), BF16),
            jax.ShapeDtypeStruct((2, tiles * half + extra, LANES), F32),
            jax.ShapeDtypeStruct((scalars, channels), F32),
        ],
        scratch_shapes=[
            pltpu.VMEM((LANES, length), F32),
            pltpu.VMEM((length, 2 * LANES), BF16),
            pltpu.VMEM((2 * LANES, channels), BF16),
            pltpu.VMEM((states, channels), F32),
            pltpu.VMEM((scalars, LANES), F32),
        ],
        name="shard_state",
    )(live_blocks, document_ids, raw, params, doc_row, skip_row, token_values, state_input)

    pieces = 4 if tiles % 4 == 0 else 1
    wide = channels // pieces
    ys, fs = [], []
    for q in range(pieces):
        y, f = pl.pallas_call(
            functools.partial(inner_kernel, width, q * wide // LANES, count),
            grid=(count,),
            in_specs=[
                SMEM,
                SMEM,
                pl.BlockSpec((BLOCK, wide), lambda k, q=q: (k, q)),
                pl.BlockSpec((BLOCK, wide), lambda k, q=q: (k, q)),
                pl.BlockSpec((BLOCK, states), lambda k: (k, 0)),
                pl.BlockSpec((BLOCK, states), lambda k: (k, 0)),
                pl.BlockSpec((rows, BLOCK), lambda k: (0, k)),
                pl.BlockSpec((BLOCK, LANES), lambda k: (k, 0)),
                pl.BlockSpec((1, BLOCK), lambda k: (0, k)),
                pl.BlockSpec((1, 2 * states, wide), lambda k, q=q: (k, 0, q)),
                pl.BlockSpec((scalars, wide), lambda k, q=q: (0, q)),
            ],
            out_specs=[pl.BlockSpec((BLOCK, wide), lambda k: (k, 0))] * 2,
            out_shape=[jax.ShapeDtypeStruct((length, wide), F32)] * 2,
            cost_estimate=pl.CostEstimate(
                flops=length * wide * 1200, bytes_accessed=length * wide * 12, transcendentals=0
            ),
            name="inner_" + str(q),
        )(
            live_blocks,
            document_ids,
            token_values,
            gate_values,
            state_input,
            state_readout,
            g,
            col,
            doc_row,
            enter,
            row,
        )
        ys.append(y)
        fs.append(f)

    own, other = carry_in(sums, tiles, half)

    gated, squares = pl.pallas_call(
        join_kernel,
        grid=(count,),
        in_specs=[SMEM, whole((tiles, half, LANES)), whole((tiles, half, LANES))]
        + [pl.BlockSpec((BLOCK, states), lambda k: (k, 0))]
        + [pl.BlockSpec((BLOCK, wide), lambda k: (k, 0))] * (2 * pieces),
        out_specs=[
            pl.BlockSpec((BLOCK, channels), lambda k: (k, 0)),
            pl.BlockSpec((1, 1, BLOCK), lambda k: (k, 0, 0)),
        ],
        out_shape=[
            jax.ShapeDtypeStruct((length, channels), F32),
            jax.ShapeDtypeStruct((count, 1, BLOCK), F32),
        ],
        scratch_shapes=[pltpu.VMEM((2 * states, channels), BF16)],
        name="join",
    )(lax.axis_index("sub").astype(jnp.int32).reshape(1), own, other, state_readout, *ys, *fs)

    squares = lax.psum(squares, "head")
    return pl.pallas_call(
        functools.partial(norm_kernel, channels * lax.axis_size("head")),
        grid=(count,),
        in_specs=[
            pl.BlockSpec((1, 1, BLOCK), lambda k: (k, 0, 0)),
            whole((1, channels)),
            pl.BlockSpec((BLOCK, channels), lambda k: (k, 0)),
        ],
        out_specs=pl.BlockSpec((BLOCK, channels), lambda k: (k, 0)),
        out_shape=jax.ShapeDtypeStruct((length, channels), BF16),
        name="norm",
    )(squares, norm_gain.reshape(1, channels), gated)


def carry_in(sums, tiles, half):
    body = tiles * half
    sub = lax.axis_index("sub")
    place, chips = lax.axis_index("seq"), lax.axis_size("seq")
    second = sub == 1
    mine = lax.dynamic_index_in_dim(sums, sub, 0, keepdims=False)
    sent = lax.dynamic_index_in_dim(sums, 1 - sub, 0, keepdims=False)
    got = lax.ppermute(sent, "sub", [(0, 1), (1, 0)])

    def parts(block):
        return (
            block[:body].reshape(tiles, half, LANES),
            block[body : body + tiles].reshape(tiles, 1, LANES),
            block[body + tiles, 0],
            block[body + tiles + 1, 0],
        )

    mine, got = parts(mine), parts(got)
    early = tuple(jnp.where(second, b, a) for a, b in zip(mine, got))
    late = tuple(jnp.where(second, a, b) for a, b in zip(mine, got))
    link = jnp.where(early[3] == late[2], 1.0, 0.0)
    late_decay = late[1] * link
    chip_state = late_decay * early[0] + late[0]
    chip_decay = late_decay * early[1]
    first, last = early[2], late[3]

    chunks = 2 if tiles % 2 == 0 else 1
    size = tiles // chunks
    rows = size * half

    def at(array, index):
        return lax.dynamic_slice_in_dim(array, index * size, size, 0)

    got = jnp.zeros((rows + 8, LANES), F32)
    history = [jnp.zeros((size, half, LANES), F32)]
    for t in range(chunks + chips - 2):
        index = jnp.clip(t - place, 0, chunks - 1)
        joined = jnp.where(got[rows, 0] == first, 1.0, 0.0)
        carry = joined * got[:rows].reshape(size, half, LANES)
        send = at(chip_decay, index) * carry + at(chip_state, index)
        send = jnp.concatenate([send.reshape(rows, LANES), jnp.full((8, LANES), last)], axis=0)
        pairs = [(z, z + 1) for z in range(chips - 1) if 0 <= t - z < chunks]
        got = lax.ppermute(send, "seq", pairs)
        joined = jnp.where(got[rows, 0] == first, 1.0, 0.0)
        history.append(joined * got[:rows].reshape(size, half, LANES))
    entering = lax.dynamic_slice_in_dim(jnp.stack(history), place, chunks, 0)
    entering = entering.reshape(tiles, half, LANES)
    onward = link * (early[1] * entering + early[0])
    own = jnp.where(second, onward, entering)
    other = lax.ppermute(jnp.where(second, entering, onward), "sub", [(0, 1), (1, 0)])
    return own, other


def solution(mesh):
    placed = (
        P(("groups", "seq", "sub"), "head"),
        P(("groups", "seq", "sub"), "head"),
        P(("groups", "seq", "sub"), None),
        P(("groups", "seq", "sub"), None),
        P("head", ("seq", "sub")),
        P("head"),
        P("head"),
        P("head"),
        P("head"),
        P(("groups", "seq", "sub")),
        P(("groups", "seq", "sub")),
    )
    return jax.shard_map(
        on_device,
        mesh=mesh,
        in_specs=placed,
        out_specs=P(("groups", "seq", "sub"), "head"),
        check_vma=False,
    )
```

```python
import functools
import math

import jax
import jax.numpy as jnp
import numpy as np
from jax import lax
from jax.experimental import pallas as pl
from jax.experimental.pallas import tpu as pltpu
from jax.sharding import PartitionSpec as P

BLOCK = 256
LANES = 128
LOG2E = math.log2(math.e)
F32 = jnp.float32
BF16 = jnp.bfloat16


def dot(a, b, contract=((1,), (0,))):
    return lax.dot_general(a, b, (contract, ((), ())), preferred_element_type=F32)


def two_parts(value):
    high = value.astype(BF16)
    low = (value - high.astype(F32)).astype(BF16)
    return high, low


def pick_row(ref, base, count, k, cols):
    row = ref[base : base + 1, cols]
    for j in range(1, count):
        row = jnp.where(k == j, ref[base + j : base + j + 1, cols], row)
    return row


def softplus(v):
    u = jnp.exp(-jnp.abs(v))
    s = u / (2.0 + u)
    q = s * s
    series = jnp.full_like(q, 1.0 / 17.0)
    for odd in (15, 13, 11, 9, 7, 5, 3, 1):
        series = series * q + 1.0 / odd
    return jnp.maximum(v, 0.0) + 2.0 * s * series


def state_kernel(
    heads,
    live_ref,
    docs_ref,
    sub_ref,
    raw_ref,
    par_ref,
    doc_row_ref,
    skip_ref,
    hot_ref,
    x_ref,
    b_ref,
    g_ref,
    col_ref,
    enter_ref,
    own_ref,
    aux_ref,
    sent_ref,
    row_ref,
    pack,
    decay_col,
    state,
    scal,
):
    k = pl.program_id(0)
    length = raw_ref.shape[1]
    count = length // BLOCK
    channels = x_ref.shape[1]
    tiles = channels // LANES
    ends = [docs_ref[j * BLOCK + BLOCK - 1] for j in range(count)]

    @pl.when(k == 0)
    def _():
        rows = raw_ref.shape[0]
        lane = lax.broadcasted_iota(jnp.int32, (1, length), 1)
        step = softplus(raw_ref[...] + par_ref[:, 0:1])
        step = jnp.where(lane < live_ref[0] * BLOCK, step, 0.0)
        cum = (-LOG2E * jnp.exp(par_ref[:, 1:2])) * step
        within = jnp.bitwise_and(lane, BLOCK - 1)
        shift = 1
        while shift < BLOCK:
            cum = cum + jnp.where(within >= shift, pltpu.roll(cum, shift, 1), 0.0)
            shift *= 2
        g = cum - jnp.where(step > 0.0, LOG2E * jnp.log(step), -1e30)
        for h in range(rows):
            g_ref[h] = g[h : h + 1, :]
        pack[...] = jnp.zeros_like(pack)
        pack[0:rows, :] = cum
        pack[LANES - 1 : LANES, :] = doc_row_ref[...].astype(F32)
        col_ref[...] = pack[...].T
        pack[LANES - 1 : LANES, :] = jnp.zeros((1, length), F32)
        for j in range(count):
            piece = slice(j * BLOCK, (j + 1) * BLOCK)
            last = cum[:, (j + 1) * BLOCK - 1 : (j + 1) * BLOCK]
            same = doc_row_ref[:, piece] == ends[j]
            pack[0:rows, piece] = jnp.where(
                same, step[:, piece] * jnp.exp2(last - cum[:, piece]), 0.0
            )
        high, low = two_parts(pack[...].T)
        decay_col[:, 0:LANES] = high
        decay_col[:, LANES:] = low
        head_lane = lax.broadcasted_iota(jnp.int32, (1, LANES), 1) < heads
        before = jnp.zeros((1, LANES), F32)
        scal[...] = jnp.zeros_like(scal)
        for j in range(count):
            end = jnp.where(head_lane, col_ref[(j + 1) * BLOCK - 1 : (j + 1) * BLOCK, :], 0.0)
            scal[j : j + 1, :] = jnp.where(head_lane, jnp.exp2(end), 0.0)
            scal[count + j : count + j + 1, :] = jnp.where(head_lane, jnp.exp2(before), 0.0)
            before = before + end
        scal[2 * count : 2 * count + 1, :] = jnp.where(head_lane, jnp.exp2(before), 0.0)
        scal[2 * count + 1 : 2 * count + 2, :] = skip_ref[...]
        high, low = two_parts(scal[...])
        hot = hot_ref[...]
        row_ref[...] = dot(high, hot) + dot(low, hot)
        state[...] = jnp.zeros_like(state)

    start = pl.multiple_of(k * BLOCK, BLOCK)
    end_doc = docs_ref[k * BLOCK + BLOCK - 1]
    prior_doc = docs_ref[jnp.maximum(k * BLOCK - 1, 0)]
    link = jnp.where(end_doc == prior_doc, 1.0, 0.0)
    decay = decay_col[pl.ds(start, BLOCK), :]
    inputs_t = b_ref[...].T
    wide = chunk_of(channels, 512)
    for c in range(0, channels, wide):
        cols = slice(c, c + wide)
        old = state[:, cols]
        enter_ref[0, :, cols] = old
        hot = hot_ref[:, cols]
        grown = dot(decay, jnp.concatenate([hot, hot], axis=0))
        scaled = (x_ref[:, cols].astype(F32) * grown).astype(BF16)
        passage = pick_row(row_ref, 0, count, k, cols) * link
        state[:, cols] = passage * old + dot(inputs_t, scaled)

    @pl.when(k == pl.num_programs(0) - 1)
    def _():
        half = state.shape[0] // 2
        full = jnp.where(ends[count - 1] == docs_ref[0], 1.0, 0.0)
        mine = pl.multiple_of(sub_ref[0] * half, half)
        theirs = pl.multiple_of((1 - sub_ref[0]) * half, half)
        aux_ref[...] = jnp.zeros_like(aux_ref)
        for j in range(tiles):
            cols = slice(j * LANES, (j + 1) * LANES)
            own_ref[j] = state[pl.ds(mine, half), cols]
            sent_ref[j * half : (j + 1) * half, :] = state[pl.ds(theirs, half), cols]
            aux_ref[j : j + 1, :] = row_ref[2 * count : 2 * count + 1, cols] * full
        aux_ref[tiles : tiles + 1, :] = jnp.full((1, LANES), docs_ref[0].astype(F32))
        aux_ref[tiles + 1 : tiles + 2, :] = jnp.full((1, LANES), docs_ref[length - 1].astype(F32))
        sent_ref[tiles * half :, :] = aux_ref[...]


def inner_kernel(
    heads,
    width,
    first_tile,
    count,
    live_ref,
    docs_ref,
    x_ref,
    z_ref,
    b_ref,
    c_ref,
    g_ref,
    col_ref,
    doc_row_ref,
    enter_ref,
    row_ref,
    hot_ref,
    *refs,
):
    y_ref, f_ref, affinity, turned, entry, passed = refs[-6:]
    k = pl.program_id(0)
    half = BLOCK // 2
    per_tile = LANES // width

    @pl.when(k >= live_ref[0])
    def _():
        y_ref[...] = jnp.zeros_like(y_ref)
        f_ref[...] = jnp.zeros_like(f_ref)

    @pl.when(k < live_ref[0])
    def _():
        readout = c_ref[...]
        doc_col = col_ref[:, LANES - 1 : LANES]
        doc_row = doc_row_ref[...].astype(F32)
        t = lax.broadcasted_iota(jnp.int32, (BLOCK, BLOCK), 0)
        s = lax.broadcasted_iota(jnp.int32, (BLOCK, BLOCK), 1)
        affinity[...] = jnp.where(
            (t >= s) & (doc_col == doc_row), dot(readout, b_ref[...], ((1,), (1,))), 0.0
        )
        prior_doc = docs_ref[jnp.maximum(k * BLOCK - 1, 0)]
        lane = lax.broadcasted_iota(jnp.int32, (1, LANES), 1)
        linked = (doc_col == prior_doc.astype(F32)) & (lane < heads)
        high, low = two_parts(jnp.where(linked, jnp.exp2(col_ref[...]), 0.0))
        entry[:, 0:LANES] = high
        entry[:, LANES:] = low
        turned[...] = pltpu.roll(
            col_ref[...], (LANES - first_tile * per_tile) % LANES, 1
        )
        reaches = jnp.where(prior_doc == docs_ref[0], 1.0, 0.0)
        passed[0:1, :] = pick_row(row_ref, count, count, k, slice(None)) * reaches
        twice = jnp.concatenate([readout, readout], axis=1)

        def tile(j, rest):
            cols = pl.ds(pl.multiple_of(j * LANES, LANES), LANES)
            x = x_ref[:, cols]
            columns = turned[...]
            tops, bottoms, masked = [], [], []
            for i in range(per_tile):
                cum = jnp.broadcast_to(columns[:, i : i + 1], (BLOCK, LANES))
                g = g_ref[(first_tile + j) * per_tile + i]
                left, right = g[:, :half], g[:, half:]
                top = jnp.exp2(jnp.minimum(cum[:half] - left, 64.0))
                bottom = jnp.exp2(cum[half:] - left)
                corner = jnp.exp2(jnp.minimum(cum[half:] - right, 64.0))
                tops.append((top * affinity[:half, :half]).astype(BF16))
                bottoms.append((bottom * affinity[half:, :half]).astype(BF16))
                bottoms.append((corner * affinity[half:, half:]).astype(BF16))
                mine = (lane >= i * width) & (lane < (i + 1) * width)
                masked.append(x * jnp.where(mine, 1.0, 0.0).astype(BF16))
            turned[...] = pltpu.roll(columns, LANES - per_tile, 1)
            upper = dot(
                jnp.concatenate(tops, axis=1),
                jnp.concatenate([m[:half] for m in masked], axis=0),
            )
            lower = dot(jnp.concatenate(bottoms, axis=1), jnp.concatenate(masked, axis=0))
            hot = hot_ref[:, cols]
            enter = dot(entry[...], jnp.concatenate([hot, hot], axis=0))
            high, low = two_parts(enter_ref[0, :, cols])
            outer = dot(twice, jnp.concatenate([high, low], axis=0))
            skip = row_ref[2 * count + 1 : 2 * count + 2, cols]
            y = jnp.concatenate([upper, lower], axis=0) + enter * outer + skip * x.astype(F32)
            z = z_ref[:, cols].astype(F32)
            gate = z / (1.0 + jnp.exp2(-LOG2E * z))
            y_ref[:, cols] = y * gate
            f_ref[:, cols] = (enter * gate * passed[0:1, cols]).astype(BF16)
            return rest

        lax.fori_loop(0, x_ref.shape[1] // LANES, tile, 0)


def join_kernel(sub_ref, own_ref, other_ref, c_ref, y_ref, f_ref, gated_ref, square_ref, total):
    k = pl.program_id(0)
    length = c_ref.shape[0]
    wide = y_ref.shape[1]
    start = pl.multiple_of(k * wide, wide)
    second = sub_ref[0] == 1

    @pl.when(k == 0)
    def _():
        total[...] = jnp.zeros_like(total)

    highs, lows = [], []
    for j in range(wide // LANES):
        own, other = own_ref[j], other_ref[j]
        carry = jnp.concatenate(
            [jnp.where(second, other, own), jnp.where(second, own, other)], axis=0
        )
        high, low = two_parts(carry)
        highs.append(high)
        lows.append(low)
    carry = jnp.concatenate(
        [jnp.concatenate(highs, axis=1), jnp.concatenate(lows, axis=1)], axis=0
    )
    for r in range(0, length, BLOCK):
        rows = slice(r, r + BLOCK)
        readout = c_ref[rows, :]
        outer = dot(jnp.concatenate([readout, readout], axis=1), carry)
        gated = y_ref[rows, :] + f_ref[rows, :].astype(F32) * outer
        gated_ref[rows, pl.ds(start, wide)] = gated
        square = total[rows, :]
        for j in range(wide // LANES):
            piece = gated[:, j * LANES : (j + 1) * LANES]
            square = square + piece * piece
        total[rows, :] = square

    @pl.when(k == pl.num_programs(0) - 1)
    def _():
        square_ref[...] = jnp.sum(total[...].T, axis=0, keepdims=True)


def norm_kernel(channels_all, square_ref, gain_ref, gated_ref, out_ref):
    rows = out_ref.shape[0]
    start = pl.multiple_of(pl.program_id(0) * rows, rows)
    scale = lax.rsqrt(square_ref[...] / channels_all + 1e-05)
    scale = jnp.broadcast_to(scale, (LANES, rows)).T
    for j in range(gated_ref.shape[1] // LANES):
        cols = slice(j * LANES, (j + 1) * LANES)
        gated = gated_ref[pl.ds(start, rows), cols]
        out_ref[:, cols] = (gated * gain_ref[:, cols] * scale).astype(BF16)


def chunk_of(total, most):
    wide = most
    while total % wide:
        wide -= LANES
    return wide


def whole(shape):
    return pl.BlockSpec(shape, lambda k, *_: (0,) * len(shape))


SMEM = pl.BlockSpec(memory_space=pltpu.SMEM)
VMEM = pl.BlockSpec(memory_space=pltpu.VMEM)


def plan(chips, tiles):
    chunks = 2 if tiles % 2 == 0 else 1
    hops = chunks + chips - 2
    pieces = 4 if tiles % 4 == 0 else 1
    return chunks, hops, pieces


def on_device(
    token_values,
    gate_values,
    state_input,
    state_readout,
    step_raw,
    step_bias,
    decay_log,
    skip_gain,
    norm_gain,
    document_ids,
    live_blocks,
):
    length, channels = token_values.shape
    heads = step_raw.shape[0]
    width = channels // heads
    states = state_input.shape[1]
    half = states // 2
    count = length // BLOCK
    tiles = channels // LANES
    rows = -(-heads // 8) * 8
    scalars = -(-(2 * count + 2) // 16) * 16
    extra = -(-(tiles + 2) // 8) * 8
    assert lax.axis_size("sub") == 2 and heads < LANES and 2 * half == states

    params = jnp.stack([step_bias, decay_log], axis=1)
    raw = step_raw
    if rows != heads:
        params = jnp.pad(params, ((0, rows - heads), (0, 0)))
        raw = jnp.pad(raw, ((0, rows - heads), (0, 0)))
    skip_row = jnp.pad(skip_gain, (0, LANES - heads)).reshape(1, LANES)
    doc_row = document_ids.reshape(1, length)
    sub = lax.axis_index("sub").astype(jnp.int32).reshape(1)
    hot = jnp.asarray(
        np.arange(LANES)[:, None] == np.arange(channels)[None, :] // width, dtype=BF16
    )

    g, col, enter, own, aux, sent, row = pl.pallas_call(
        functools.partial(state_kernel, heads),
        grid=(count,),
        in_specs=[
            SMEM,
            SMEM,
            SMEM,
            whole((rows, length)),
            whole((rows, 2)),
            whole((1, length)),
            whole((1, LANES)),
            whole((LANES, channels)),
            pl.BlockSpec((BLOCK, channels), lambda k: (k, 0)),
            pl.BlockSpec((BLOCK, states), lambda k: (k, 0)),
        ],
        out_specs=[
            whole((rows, 1, length)),
            whole((length, LANES)),
            pl.BlockSpec((1, states, channels), lambda k: (k, 0, 0)),
            whole((tiles, half, LANES)),
            whole((extra, LANES)),
            whole((tiles * half + extra, LANES)),
            whole((scalars, channels)),
        ],
        out_shape=[
            jax.ShapeDtypeStruct((rows, 1, length), F32),
            jax.ShapeDtypeStruct((length, LANES), F32),
            jax.ShapeDtypeStruct((count, states, channels), F32),
            jax.ShapeDtypeStruct((tiles, half, LANES), F32),
            jax.ShapeDtypeStruct((extra, LANES), F32),
            jax.ShapeDtypeStruct((tiles * half + extra, LANES), F32),
            jax.ShapeDtypeStruct((scalars, channels), F32),
        ],
        scratch_shapes=[
            pltpu.VMEM((LANES, length), F32),
            pltpu.VMEM((length, 2 * LANES), BF16),
            pltpu.VMEM((states, channels), F32),
            pltpu.VMEM((scalars, LANES), F32),
        ],
        name="shard_state",
    )(
        live_blocks,
        document_ids,
        sub,
        raw,
        params,
        doc_row,
        skip_row,
        hot,
        token_values,
        state_input,
    )

    pieces = plan(lax.axis_size("seq"), tiles)[2]
    wide = channels // pieces
    filled = ()
    for q in range(pieces):
        filled = pl.pallas_call(
            functools.partial(inner_kernel, heads, width, q * wide // LANES, count),
            grid=(count,),
            in_specs=[
                SMEM,
                SMEM,
                pl.BlockSpec((BLOCK, wide), lambda k, q=q: (k, q)),
                pl.BlockSpec((BLOCK, wide), lambda k, q=q: (k, q)),
                pl.BlockSpec((BLOCK, states), lambda k: (k, 0)),
                pl.BlockSpec((BLOCK, states), lambda k: (k, 0)),
                pl.BlockSpec((rows, 1, BLOCK), lambda k: (0, 0, k)),
                pl.BlockSpec((BLOCK, LANES), lambda k: (k, 0)),
                pl.BlockSpec((1, BLOCK), lambda k: (0, k)),
                pl.BlockSpec((1, states, wide), lambda k, q=q: (k, 0, q)),
                pl.BlockSpec((scalars, wide), lambda k, q=q: (0, q)),
                pl.BlockSpec((LANES, wide), lambda k, q=q: (0, q)),
            ]
            + [pl.BlockSpec(memory_space=pl.ANY)] * len(filled),
            out_specs=[pl.BlockSpec((BLOCK, wide), lambda k, q=q: (k, q))] * 2,
            out_shape=[
                jax.ShapeDtypeStruct((length, channels), F32),
                jax.ShapeDtypeStruct((length, channels), BF16),
            ],
            scratch_shapes=[
                pltpu.VMEM((BLOCK, BLOCK), F32),
                pltpu.VMEM((BLOCK, LANES), F32),
                pltpu.VMEM((BLOCK, 2 * LANES), BF16),
                pltpu.VMEM((8, wide), F32),
            ],
            input_output_aliases={12: 0, 13: 1} if filled else {},
            cost_estimate=pl.CostEstimate(
                flops=length * wide * 1200,
                bytes_accessed=length * wide * 10,
                transcendentals=0,
            ),
        )(
            live_blocks,
            document_ids,
            token_values,
            gate_values,
            state_input,
            state_readout,
            g,
            col,
            doc_row,
            enter,
            row,
            hot,
            *filled,
        )

    own, other = carry_in(own, aux, sent)

    joined = chunk_of(channels, 512)
    gated, squares = pl.pallas_call(
        join_kernel,
        grid=(channels // joined,),
        in_specs=[
            SMEM,
            pl.BlockSpec((joined // LANES, half, LANES), lambda k: (k, 0, 0)),
            pl.BlockSpec((joined // LANES, half, LANES), lambda k: (k, 0, 0)),
            whole((length, states)),
            pl.BlockSpec((length, joined), lambda k: (0, k)),
            pl.BlockSpec((length, joined), lambda k: (0, k)),
        ],
        out_specs=[VMEM, whole((1, length))],
        out_shape=[
            jax.ShapeDtypeStruct((length, channels), F32),
            jax.ShapeDtypeStruct((1, length), F32),
        ],
        scratch_shapes=[pltpu.VMEM((length, LANES), F32)],
        compiler_params=pltpu.CompilerParams(vmem_limit_bytes=40 << 20),
        name="join",
    )(sub, own, other, state_readout, *filled)

    squares = lax.psum(squares, "head")
    return pl.pallas_call(
        functools.partial(norm_kernel, channels * lax.axis_size("head")),
        grid=(count,),
        in_specs=[pl.BlockSpec((1, BLOCK), lambda k: (0, k)), whole((1, channels)), VMEM],
        out_specs=pl.BlockSpec((BLOCK, channels), lambda k: (k, 0)),
        out_shape=jax.ShapeDtypeStruct((length, channels), BF16),
        compiler_params=pltpu.CompilerParams(vmem_limit_bytes=40 << 20),
        name="norm",
    )(squares, norm_gain.reshape(1, channels), gated)


def carry_in(own, aux, sent):
    tiles, half, _ = own.shape
    body = tiles * half
    second = lax.axis_index("sub") == 1
    place, chips = lax.axis_index("seq"), lax.axis_size("seq")
    got = lax.ppermute(sent, "sub", [(0, 1), (1, 0)])
    got_state, got_aux = got[:body].reshape(tiles, half, LANES), got[body:]
    early = jnp.where(second, got_state, own)
    late = jnp.where(second, own, got_state)
    early_aux = jnp.where(second, got_aux, aux)
    late_aux = jnp.where(second, aux, got_aux)
    first, last = early_aux[tiles : tiles + 1], late_aux[tiles + 1 : tiles + 2]
    link = jnp.where(
        early_aux[tiles + 1 : tiles + 2] == late_aux[tiles : tiles + 1], 1.0, 0.0
    )
    early_decay = early_aux[:tiles].reshape(tiles, 1, LANES)
    late_decay = (late_aux[:tiles] * link).reshape(tiles, 1, LANES)
    chip_state = late_decay * early + late
    chip_decay = late_decay * early_decay

    chunks, hops, _ = plan(chips, tiles)
    size = tiles // chunks
    rows = size * half
    tail = jnp.broadcast_to(last, (8, LANES))

    def at(array, index):
        return lax.dynamic_slice_in_dim(array, index * size, size, 0)

    carry = jnp.zeros((size, half, LANES), F32)
    received = []
    for t in range(hops):
        index = jnp.clip(t - place, 0, chunks - 1)
        send = at(chip_decay, index) * carry + at(chip_state, index)
        send = jnp.concatenate([send.reshape(rows, LANES), tail], axis=0)
        pairs = [(z, z + 1) for z in range(chips - 1) if 0 <= t - z < chunks]
        got = lax.ppermute(send, "seq", pairs)
        joined = jnp.where(got[rows : rows + 1] == first, 1.0, 0.0)
        carry = joined[None] * got[:rows].reshape(size, half, LANES)
        received.append(carry)
    parts = []
    for c in range(chunks):
        part = jnp.zeros((size, half, LANES), F32)
        for z in range(1, chips):
            part = jnp.where(place == z, received[c + z - 1], part)
        parts.append(part)
    entering = jnp.concatenate(parts, axis=0)
    onward = link[None] * (early_decay * entering + early)
    mine = jnp.where(second, onward, entering)
    other = lax.ppermute(jnp.where(second, entering, onward), "sub", [(0, 1), (1, 0)])
    return mine, other


def solution(mesh):
    placed = (
        P(("groups", "seq", "sub"), "head"),
        P(("groups", "seq", "sub"), "head"),
        P(("groups", "seq", "sub"), None),
        P(("groups", "seq", "sub"), None),
        P("head", ("seq", "sub")),
        P("head"),
        P("head"),
        P("head"),
        P("head"),
        P(("groups", "seq", "sub")),
        P(("groups", "seq", "sub")),
    )

    return jax.shard_map(
        on_device,
        mesh=mesh,
        in_specs=placed,
        out_specs=P(("groups", "seq", "sub"), "head"),
        check_vma=False,
    )
```

```python
import functools
import math

import jax
import jax.numpy as jnp
import numpy as np
from jax import lax
from jax.experimental import pallas as pl
from jax.experimental.pallas import tpu as pltpu
from jax.sharding import PartitionSpec as P

BLOCK = 256
LANES = 128
LOG2E = math.log2(math.e)
F32 = jnp.float32
BF16 = jnp.bfloat16


def dot(a, b, contract=((1,), (0,))):
    return lax.dot_general(a, b, (contract, ((), ())), preferred_element_type=F32)


def two_parts(value):
    high = value.astype(BF16)
    low = (value - high.astype(F32)).astype(BF16)
    return high, low


def pick_row(ref, base, count, k, cols):
    row = ref[base : base + 1, cols]
    for j in range(1, count):
        row = jnp.where(k == j, ref[base + j : base + j + 1, cols], row)
    return row


def softplus(v):
    u = jnp.exp(-jnp.abs(v))
    s = u / (2.0 + u)
    q = s * s
    series = jnp.full_like(q, 1.0 / 15.0)
    for odd in (13, 11, 9, 7, 5, 3, 1):
        series = series * q + 1.0 / odd
    return jnp.maximum(v, 0.0) + 2.0 * s * series


def state_kernel(
    heads,
    live_ref,
    docs_ref,
    sub_ref,
    raw_ref,
    bias_ref,
    decay_ref,
    skip_ref,
    doc_row_ref,
    tri_ref,
    hot_ref,
    hot_low_ref,
    x_ref,
    b_ref,
    g_ref,
    col_ref,
    enter_ref,
    own_ref,
    sent_ref,
    row_ref,
    pack,
    col_parts,
    inputs_t,
    state,
    scal,
):
    length = raw_ref.shape[0 + 1]
    rows = raw_ref.shape[0]
    count = length // BLOCK
    wide = x_ref.shape[1]
    ends = [docs_ref[j * BLOCK + BLOCK - 1] for j in range(count)]

    @pl.when(pl.program_id(0) == 0)
    def _():
        inputs_t[...] = b_ref[...].T
        pack[...] = jnp.zeros_like(pack)
        pack[0:1, 0:heads] = bias_ref[...]
        pack[1:2, 0:heads] = decay_ref[...]
        params = pack[0:LANES, 0:LANES].T
        lane = lax.broadcasted_iota(jnp.int32, (1, length), 1)
        step = softplus(raw_ref[...] + params[0:rows, 0:1])
        step = jnp.where(lane < live_ref[0] * BLOCK, step, 0.0)
        rate = (-LOG2E * jnp.exp(params[0:rows, 1:2])) * step
        high, _ = two_parts(rate)
        middle, low = two_parts(rate - high.astype(F32))
        tri = tri_ref[...]
        logs = jnp.where(step > 0.0, LOG2E * jnp.log(step), -1e30)
        for j in range(count):
            piece = slice(j * BLOCK, (j + 1) * BLOCK)
            cum = dot(high[:, piece], tri) + (dot(middle[:, piece], tri) + dot(low[:, piece], tri))
            g_ref[:, piece] = cum - logs[:, piece]
            same = doc_row_ref[:, piece] == ends[j]
            pack[0:rows, piece] = cum
            pack[rows : 2 * rows, piece] = jnp.where(
                same, step[:, piece] * jnp.exp2(cum[:, BLOCK - 1 :] - cum), 0.0
            )
        pack[LANES - 1 : LANES, :] = doc_row_ref[...].astype(F32)
        for j in range(count):
            piece = slice(j * BLOCK, (j + 1) * BLOCK)
            turned = pack[:, piece].T
            col_ref[piece, :] = turned
            high, low = two_parts(turned)
            col_parts[piece, 0:LANES] = high
            col_parts[piece, LANES:] = low
        head_lane = lax.broadcasted_iota(jnp.int32, (1, LANES), 1) < heads
        before = jnp.zeros((1, LANES), F32)
        scal[...] = jnp.zeros_like(scal)
        for j in range(count):
            end = jnp.where(head_lane, col_ref[(j + 1) * BLOCK - 1 : (j + 1) * BLOCK, :], 0.0)
            scal[j : j + 1, :] = jnp.where(head_lane, jnp.exp2(end), 0.0)
            scal[count + j : count + j + 1, :] = jnp.where(head_lane, jnp.exp2(before), 0.0)
            before = before + end
        scal[2 * count : 2 * count + 1, :] = jnp.where(head_lane, jnp.exp2(before), 0.0)
        scal[2 * count + 1 : 2 * count + 2, 0:heads] = skip_ref[...]

    hot = hot_ref[...]
    high, low = two_parts(scal[...])
    row = dot(high, hot) + dot(low, hot)
    row_ref[...] = row
    hot_low = jnp.concatenate([hot_low_ref[...]] * 2, axis=0)
    state[...] = jnp.zeros_like(state)
    for j in range(count):
        piece = slice(j * BLOCK, (j + 1) * BLOCK)
        prior = docs_ref[max(j * BLOCK - 1, 0)]
        passage = row[j : j + 1, :] * jnp.where(ends[j] == prior, 1.0, 0.0)
        grown = dot(col_parts[piece, :], hot_low)
        scaled = (x_ref[piece, :].astype(F32) * grown).astype(BF16)
        old = state[...]
        enter_ref[j] = old
        state[...] = passage * old + dot(inputs_t[:, piece], scaled)

    half = state.shape[0] // 2
    total = row[2 * count : 2 * count + 1, :] * jnp.where(ends[count - 1] == docs_ref[0], 1.0, 0.0)
    mine = pl.multiple_of(sub_ref[0] * half, half)
    theirs = pl.multiple_of((1 - sub_ref[0]) * half, half)
    line = lax.broadcasted_iota(jnp.int32, (8, LANES), 0)
    first, last = docs_ref[0].astype(F32), docs_ref[length - 1].astype(F32)
    for j in range(wide // LANES):
        cols = slice(j * LANES, (j + 1) * LANES)
        foot = jnp.where(line == 0, total[:, cols], jnp.where(line == 1, first, last))
        own_ref[j, 0:half, :] = state[pl.ds(mine, half), cols]
        sent_ref[j, 0:half, :] = state[pl.ds(theirs, half), cols]
        own_ref[j, half:, :] = foot
        sent_ref[j, half:, :] = foot


def prepare_kernel(heads, docs_ref, b_ref, c_ref, col_ref, doc_row_ref, affinity_ref, entry_ref):
    k = pl.program_id(0)
    doc_col = col_ref[:, LANES - 1 : LANES]
    doc_row = doc_row_ref[...].astype(F32)
    t = lax.broadcasted_iota(jnp.int32, (BLOCK, BLOCK), 0)
    s = lax.broadcasted_iota(jnp.int32, (BLOCK, BLOCK), 1)
    affinity_ref[0] = jnp.where(
        (t >= s) & (doc_col == doc_row), dot(c_ref[...], b_ref[...], ((1,), (1,))), 0.0
    )
    prior_doc = docs_ref[jnp.maximum(k * BLOCK - 1, 0)].astype(F32)
    lane = lax.broadcasted_iota(jnp.int32, (1, LANES), 1)
    linked = (doc_col == prior_doc) & (lane < heads)
    high, low = two_parts(jnp.where(linked, jnp.exp2(col_ref[...]), 0.0))
    entry_ref[:, 0:LANES] = high
    entry_ref[:, LANES:] = low


def inner_kernel(
    width,
    first_tile,
    group,
    count,
    live_ref,
    docs_ref,
    x_ref,
    z_ref,
    c_ref,
    g_ref,
    col_ref,
    affinity_ref,
    entry_ref,
    enter_ref,
    row_ref,
    hot_ref,
    *refs,
):
    y_ref, f_ref = refs[-2:]
    k = pl.program_id(0)
    half = BLOCK // 2
    per_tile = LANES // width

    @pl.when(k >= live_ref[0])
    def _():
        y_ref[...] = jnp.zeros_like(y_ref)
        f_ref[...] = jnp.zeros_like(f_ref)

    @pl.when(k < live_ref[0])
    def _():
        readout = c_ref[...]
        twice = jnp.concatenate([readout, readout], axis=1)
        lane = lax.broadcasted_iota(jnp.int32, (1, LANES), 1)
        nothing = jnp.zeros((BLOCK, LANES), BF16)
        reaches = jnp.where(docs_ref[jnp.maximum(k * BLOCK - 1, 0)] == docs_ref[0], 1.0, 0.0)
        passed = pick_row(row_ref, count, count, k, slice(None)) * reaches
        for q in range(x_ref.shape[1] // (group * LANES)):
            cols = slice(q * group * LANES, (q + 1) * group * LANES)
            x = x_ref[:, cols]
            tops, bottoms, masked = [], [], []
            for u in range(group):
                part = x[:, u * LANES : (u + 1) * LANES]
                for i in range(per_tile):
                    h = (first_tile + q * group + u) * per_tile + i
                    cum = jnp.broadcast_to(col_ref[:, h : h + 1], (BLOCK, LANES))
                    left, right = g_ref[h : h + 1, :half], g_ref[h : h + 1, half:]
                    top = jnp.exp2(jnp.minimum(cum[:half] - left, 64.0))
                    bottom = jnp.exp2(cum[half:] - left)
                    corner = jnp.exp2(jnp.minimum(cum[half:] - right, 64.0))
                    tops.append((top * affinity_ref[0, :half, :half]).astype(BF16))
                    bottoms.append((bottom * affinity_ref[0, half:, :half]).astype(BF16))
                    bottoms.append((corner * affinity_ref[0, half:, half:]).astype(BF16))
                    mine = (lane >= i * width) & (lane < (i + 1) * width)
                    kept = part * jnp.where(mine, 1.0, 0.0).astype(BF16)
                    masked.append(
                        jnp.concatenate(
                            [kept if v == u else nothing for v in range(group)], axis=1
                        )
                    )
            upper = dot(
                jnp.concatenate(tops, axis=1),
                jnp.concatenate([m[:half] for m in masked], axis=0),
            )
            lower = dot(jnp.concatenate(bottoms, axis=1), jnp.concatenate(masked, axis=0))
            hot = hot_ref[:, cols]
            enter = dot(entry_ref[...], jnp.concatenate([hot, hot], axis=0))
            high, low = two_parts(enter_ref[0, :, cols])
            outer = dot(twice, jnp.concatenate([high, low], axis=0))
            skip = row_ref[2 * count + 1 : 2 * count + 2, cols]
            y = jnp.concatenate([upper, lower], axis=0) + enter * outer + skip * x.astype(F32)
            z = z_ref[:, cols].astype(F32)
            gate = z / (1.0 + jnp.exp2(-LOG2E * z))
            y_ref[:, cols] = y * gate
            f_ref[:, cols] = (enter * gate * passed[:, cols]).astype(BF16)


def join_kernel(sub_ref, own_ref, other_ref, c_ref, y_ref, f_ref, gated_ref, square_ref, total):
    k = pl.program_id(0)
    length = c_ref.shape[0]
    wide = own_ref.shape[0] * LANES
    here = pl.ds(pl.multiple_of(k * wide, wide), wide)
    second = sub_ref[0] == 1

    @pl.when(k == 0)
    def _():
        total[...] = jnp.zeros_like(total)

    highs, lows = [], []
    for j in range(wide // LANES):
        own, other = own_ref[j], other_ref[j]
        carry = jnp.concatenate(
            [jnp.where(second, other, own), jnp.where(second, own, other)], axis=0
        )
        high, low = two_parts(carry)
        highs.append(high)
        lows.append(low)
    carry = jnp.concatenate(
        [jnp.concatenate(highs, axis=1), jnp.concatenate(lows, axis=1)], axis=0
    )
    for r in range(0, length, BLOCK):
        rows = slice(r, r + BLOCK)
        readout = c_ref[rows, :]
        outer = dot(jnp.concatenate([readout, readout], axis=1), carry)
        gated = y_ref[rows, here] + f_ref[rows, here].astype(F32) * outer
        gated_ref[rows, here] = gated
        square = total[rows, :]
        for j in range(wide // LANES):
            piece = gated[:, j * LANES : (j + 1) * LANES]
            square = square + piece * piece
        total[rows, :] = square

    @pl.when(k == pl.num_programs(0) - 1)
    def _():
        square_ref[...] = jnp.sum(total[...].T, axis=0, keepdims=True)


def norm_kernel(channels_all, square_ref, more_ref, gain_ref, gated_ref, out_ref):
    rows = out_ref.shape[0]
    start = pl.multiple_of(pl.program_id(0) * rows, rows)
    scale = lax.rsqrt((square_ref[...] + more_ref[...]) / channels_all + 1e-05)
    scale = jnp.broadcast_to(scale, (LANES, rows)).T
    for j in range(gated_ref.shape[1] // LANES):
        cols = slice(j * LANES, (j + 1) * LANES)
        gated = gated_ref[pl.ds(start, rows), cols]
        out_ref[:, cols] = (gated * gain_ref[:, cols] * scale).astype(BF16)


def chunk_of(total, most):
    wide = most
    while total % wide:
        wide -= LANES
    return wide


def whole(shape):
    return pl.BlockSpec(shape, lambda k, *_: (0,) * len(shape))


SMEM = pl.BlockSpec(memory_space=pltpu.SMEM)
VMEM = pl.BlockSpec(memory_space=pltpu.VMEM)


def plan(chips, tiles):
    chunks = 2 if tiles % 2 == 0 else 1
    hops = chunks + chips - 2
    group = 2 if tiles % 2 == 0 else 1
    pieces = 5 if tiles % (5 * group) == 0 else 1
    return chunks, hops, group, pieces


def on_device(
    token_values,
    gate_values,
    state_input,
    state_readout,
    step_raw,
    step_bias,
    decay_log,
    skip_gain,
    norm_gain,
    document_ids,
    live_blocks,
):
    length, channels = token_values.shape
    heads = step_raw.shape[0]
    width = channels // heads
    states = state_input.shape[1]
    half = states // 2
    count = length // BLOCK
    tiles = channels // LANES
    rows = -(-heads // 8) * 8
    scalars = -(-(2 * count + 2) // 16) * 16
    assert lax.axis_size("sub") == 2 and 2 * rows < LANES and states == LANES

    raw = step_raw
    if rows != heads:
        raw = jnp.pad(raw, ((0, rows - heads), (0, 0)))
    doc_row = document_ids.reshape(1, length)
    sub = lax.axis_index("sub").astype(jnp.int32).reshape(1)
    head_of = np.arange(channels)[None, :] // width
    lanes = np.arange(LANES)[:, None]
    hot = jnp.asarray(lanes == head_of, dtype=BF16)
    hot_low = jnp.asarray(lanes == head_of + rows, dtype=BF16)
    tri = jnp.asarray(np.triu(np.ones((BLOCK, BLOCK))), dtype=BF16)

    chunk = chunk_of(channels, 512)
    per_chunk = chunk // LANES
    g, col, enter, own, sent, row = pl.pallas_call(
        functools.partial(state_kernel, heads),
        grid=(channels // chunk,),
        in_specs=[
            SMEM,
            SMEM,
            SMEM,
            whole((rows, length)),
            whole((1, heads)),
            whole((1, heads)),
            whole((1, heads)),
            whole((1, length)),
            whole((BLOCK, BLOCK)),
            pl.BlockSpec((LANES, chunk), lambda c: (0, c)),
            pl.BlockSpec((LANES, chunk), lambda c: (0, c)),
            pl.BlockSpec((length, chunk), lambda c: (0, c)),
            whole((length, states)),
        ],
        out_specs=[
            whole((rows, length)),
            whole((length, LANES)),
            pl.BlockSpec((count, states, chunk), lambda c: (0, 0, c)),
            pl.BlockSpec((per_chunk, half + 8, LANES), lambda c: (c, 0, 0)),
            pl.BlockSpec((per_chunk, half + 8, LANES), lambda c: (c, 0, 0)),
            pl.BlockSpec((scalars, chunk), lambda c: (0, c)),
        ],
        out_shape=[
            jax.ShapeDtypeStruct((rows, length), F32),
            jax.ShapeDtypeStruct((length, LANES), F32),
            jax.ShapeDtypeStruct((count, states, channels), F32),
            jax.ShapeDtypeStruct((tiles, half + 8, LANES), F32),
            jax.ShapeDtypeStruct((tiles, half + 8, LANES), F32),
            jax.ShapeDtypeStruct((scalars, channels), F32),
        ],
        scratch_shapes=[
            pltpu.VMEM((LANES, length), F32),
            pltpu.VMEM((length, 2 * LANES), BF16),
            pltpu.VMEM((states, length), BF16),
            pltpu.VMEM((states, chunk), F32),
            pltpu.VMEM((scalars, LANES), F32),
        ],
        compiler_params=pltpu.CompilerParams(vmem_limit_bytes=24 << 20),
        name="shard_state",
    )(
        live_blocks,
        document_ids,
        sub,
        raw,
        step_bias.reshape(1, heads),
        decay_log.reshape(1, heads),
        skip_gain.reshape(1, heads),
        doc_row,
        tri,
        hot,
        hot_low,
        token_values,
        state_input,
    )

    affinity, entry = pl.pallas_call(
        functools.partial(prepare_kernel, heads),
        grid=(count,),
        in_specs=[
            SMEM,
            pl.BlockSpec((BLOCK, states), lambda k: (k, 0)),
            pl.BlockSpec((BLOCK, states), lambda k: (k, 0)),
            pl.BlockSpec((BLOCK, LANES), lambda k: (k, 0)),
            pl.BlockSpec((1, BLOCK), lambda k: (0, k)),
        ],
        out_specs=[
            pl.BlockSpec((1, BLOCK, BLOCK), lambda k: (k, 0, 0)),
            pl.BlockSpec((BLOCK, 2 * LANES), lambda k: (k, 0)),
        ],
        out_shape=[
            jax.ShapeDtypeStruct((count, BLOCK, BLOCK), F32),
            jax.ShapeDtypeStruct((length, 2 * LANES), BF16),
        ],
        compiler_params=pltpu.CompilerParams(vmem_limit_bytes=16 << 20),
        name="prepare",
    )(document_ids, state_input, state_readout, col, doc_row)

    group, pieces = plan(lax.axis_size("seq"), tiles)[2:]
    wide = channels // pieces
    filled = ()
    for q in range(pieces):
        filled = pl.pallas_call(
            functools.partial(inner_kernel, width, q * wide // LANES, group, count),
            grid=(count,),
            in_specs=[
                SMEM,
                SMEM,
                pl.BlockSpec((BLOCK, wide), lambda k, q=q: (k, q)),
                pl.BlockSpec((BLOCK, wide), lambda k, q=q: (k, q)),
                pl.BlockSpec((BLOCK, states), lambda k: (k, 0)),
                pl.BlockSpec((rows, BLOCK), lambda k: (0, k)),
                pl.BlockSpec((BLOCK, LANES), lambda k: (k, 0)),
                pl.BlockSpec((1, BLOCK, BLOCK), lambda k: (k, 0, 0)),
                pl.BlockSpec((BLOCK, 2 * LANES), lambda k: (k, 0)),
                pl.BlockSpec((1, states, wide), lambda k, q=q: (k, 0, q)),
                pl.BlockSpec((scalars, wide), lambda k, q=q: (0, q)),
                pl.BlockSpec((LANES, wide), lambda k, q=q: (0, q)),
            ]
            + [pl.BlockSpec(memory_space=pl.ANY)] * len(filled),
            out_specs=[pl.BlockSpec((BLOCK, wide), lambda k, q=q: (k, q))] * 2,
            out_shape=[
                jax.ShapeDtypeStruct((length, channels), F32),
                jax.ShapeDtypeStruct((length, channels), BF16),
            ],
            input_output_aliases={12: 0, 13: 1} if filled else {},
            cost_estimate=pl.CostEstimate(
                flops=length * wide * 1200,
                bytes_accessed=length * wide * 10,
                transcendentals=0,
            ),
            compiler_params=pltpu.CompilerParams(vmem_limit_bytes=16 << 20),
        )(
            live_blocks,
            document_ids,
            token_values,
            gate_values,
            state_readout,
            g,
            col,
            affinity,
            entry,
            enter,
            row,
            hot,
            *filled,
        )

    own, other = carry_in(own, sent, half)

    gated, squares = pl.pallas_call(
        join_kernel,
        grid=(channels // chunk,),
        in_specs=[
            SMEM,
            pl.BlockSpec((per_chunk, half, LANES), lambda k: (k, 0, 0)),
            pl.BlockSpec((per_chunk, half, LANES), lambda k: (k, 0, 0)),
            whole((length, states)),
            VMEM,
            VMEM,
        ],
        out_specs=[VMEM, whole((1, length))],
        out_shape=[
            jax.ShapeDtypeStruct((length, channels), F32),
            jax.ShapeDtypeStruct((1, length), F32),
        ],
        scratch_shapes=[pltpu.VMEM((length, LANES), F32)],
        compiler_params=pltpu.CompilerParams(vmem_limit_bytes=16 << 20),
        input_output_aliases={4: 0},
        name="join",
    )(sub, own, other, state_readout, *filled)

    squares, more = summed(squares, "head")
    return pl.pallas_call(
        functools.partial(norm_kernel, channels * lax.axis_size("head")),
        grid=(count,),
        in_specs=[
            pl.BlockSpec((1, BLOCK), lambda k: (0, k)),
            pl.BlockSpec((1, BLOCK), lambda k: (0, k)),
            whole((1, channels)),
            VMEM,
        ],
        out_specs=pl.BlockSpec((BLOCK, channels), lambda k: (k, 0)),
        out_shape=jax.ShapeDtypeStruct((length, channels), BF16),
        compiler_params=pltpu.CompilerParams(vmem_limit_bytes=16 << 20),
        name="norm",
    )(squares, more, norm_gain.reshape(1, channels), gated)


def summed(value, axis):
    size = lax.axis_size(axis)
    if size & (size - 1):
        total = value
        for shift in range(1, size):
            total = total + lax.ppermute(value, axis, [(i, (i + shift) % size) for i in range(size)])
        return total, jnp.zeros_like(value)
    more, shift = jnp.zeros_like(value), 1
    while shift < size:
        value = value + more if shift > 1 else value
        more = lax.ppermute(value, axis, [(i, i ^ shift) for i in range(size)])
        shift *= 2
    return value, more


def carry_in(own, sent, half):
    tiles = own.shape[0]
    second = lax.axis_index("sub") == 1
    place, chips = lax.axis_index("seq"), lax.axis_size("seq")
    got = lax.ppermute(sent, "sub", [(0, 1), (1, 0)])
    early = jnp.where(second, got, own)
    late = jnp.where(second, own, got)
    first, last = early[0, half + 1], late[0, half + 2]
    link = jnp.where(early[0, half + 2] == late[0, half + 1], 1.0, 0.0)
    early_decay, late_decay = early[:, half : half + 1], late[:, half : half + 1] * link
    early, late = early[:, :half], late[:, :half]
    chip_state = late_decay * early + late
    chip_decay = late_decay * early_decay

    chunks, hops = plan(chips, tiles)[:2]
    size = tiles // chunks
    rows = size * half
    tail = jnp.broadcast_to(last, (8, LANES))

    def at(array, index):
        return lax.dynamic_slice_in_dim(array, index * size, size, 0)

    carry = jnp.zeros((size, half, LANES), F32)
    received = []
    for t in range(hops):
        index = jnp.clip(t - place, 0, chunks - 1)
        send = at(chip_decay, index) * carry + at(chip_state, index)
        send = jnp.concatenate([send.reshape(rows, LANES), tail], axis=0)
        pairs = [(z, z + 1) for z in range(chips - 1) if 0 <= t - z < chunks]
        got = lax.ppermute(send, "seq", pairs)
        joined = jnp.where(got[rows : rows + 1] == first, 1.0, 0.0)
        carry = joined[None] * got[:rows].reshape(size, half, LANES)
        received.append(carry)
    parts = []
    for c in range(chunks):
        part = jnp.zeros((size, half, LANES), F32)
        for z in range(1, chips):
            part = jnp.where(place == z, received[c + z - 1], part)
        parts.append(part)
    entering = jnp.concatenate(parts, axis=0)
    onward = link * (early_decay * entering + early)
    mine = jnp.where(second, onward, entering)
    other = lax.ppermute(jnp.where(second, entering, onward), "sub", [(0, 1), (1, 0)])
    return mine, other


def solution(mesh):
    placed = (
        P(("groups", "seq", "sub"), "head"),
        P(("groups", "seq", "sub"), "head"),
        P(("groups", "seq", "sub"), None),
        P(("groups", "seq", "sub"), None),
        P("head", ("seq", "sub")),
        P("head"),
        P("head"),
        P("head"),
        P("head"),
        P(("groups", "seq", "sub")),
        P(("groups", "seq", "sub")),
    )

    return jax.shard_map(
        on_device,
        mesh=mesh,
        in_specs=placed,
        out_specs=P(("groups", "seq", "sub"), "head"),
        check_vma=False,
    )
```

```python
import functools
import math

import jax
import jax.numpy as jnp
import numpy as np
from jax import lax
from jax.experimental import pallas as pl
from jax.experimental.pallas import tpu as pltpu
from jax.sharding import PartitionSpec as P

BLOCK = 256
LANES = 128
LOG2E = math.log2(math.e)
F32 = jnp.float32
BF16 = jnp.bfloat16


def dot(a, b, contract=((1,), (0,))):
    return lax.dot_general(a, b, (contract, ((), ())), preferred_element_type=F32)


def two_parts(value):
    high = value.astype(BF16)
    low = (value - high.astype(F32)).astype(BF16)
    return high, low


def pick_row(ref, base, count, k, cols):
    row = ref[base : base + 1, cols]
    for j in range(1, count):
        row = jnp.where(k == j, ref[base + j : base + j + 1, cols], row)
    return row


def softplus(v):
    u = jnp.exp(-jnp.abs(v))
    s = u / (2.0 + u)
    q = s * s
    series = jnp.full_like(q, 1.0 / 15.0)
    for odd in (13, 11, 9, 7, 5, 3, 1):
        series = series * q + 1.0 / odd
    return jnp.maximum(v, 0.0) + 2.0 * s * series


def state_kernel(
    heads,
    live_ref,
    docs_ref,
    sub_ref,
    raw_ref,
    bias_ref,
    decay_ref,
    skip_ref,
    doc_row_ref,
    tri_ref,
    hot_ref,
    hot_low_ref,
    x_ref,
    b_ref,
    g_ref,
    col_ref,
    enter_ref,
    own_ref,
    sent_ref,
    row_ref,
    pack,
    col_parts,
    inputs_t,
    state,
    scal,
):
    length = raw_ref.shape[0 + 1]
    rows = raw_ref.shape[0]
    count = length // BLOCK
    wide = x_ref.shape[1]
    ends = [docs_ref[j * BLOCK + BLOCK - 1] for j in range(count)]

    @pl.when(pl.program_id(0) == 0)
    def _():
        inputs_t[...] = b_ref[...].T
        pack[...] = jnp.zeros_like(pack)
        pack[0:1, 0:heads] = bias_ref[...]
        pack[1:2, 0:heads] = decay_ref[...]
        params = pack[0:LANES, 0:LANES].T
        lane = lax.broadcasted_iota(jnp.int32, (1, length), 1)
        step = softplus(raw_ref[...] + params[0:rows, 0:1])
        step = jnp.where(lane < live_ref[0] * BLOCK, step, 0.0)
        rate = (-LOG2E * jnp.exp(params[0:rows, 1:2])) * step
        high, _ = two_parts(rate)
        middle, low = two_parts(rate - high.astype(F32))
        tri = tri_ref[...]
        logs = jnp.where(step > 0.0, LOG2E * jnp.log(step), -1e30)
        for j in range(count):
            piece = slice(j * BLOCK, (j + 1) * BLOCK)
            cum = dot(high[:, piece], tri) + (dot(middle[:, piece], tri) + dot(low[:, piece], tri))
            g_ref[:, piece] = cum - logs[:, piece]
            same = doc_row_ref[:, piece] == ends[j]
            pack[0:rows, piece] = cum
            pack[rows : 2 * rows, piece] = jnp.where(
                same, step[:, piece] * jnp.exp2(cum[:, BLOCK - 1 :] - cum), 0.0
            )
        pack[LANES - 1 : LANES, :] = doc_row_ref[...].astype(F32)
        for j in range(count):
            piece = slice(j * BLOCK, (j + 1) * BLOCK)
            turned = pack[:, piece].T
            col_ref[piece, :] = turned
            high, low = two_parts(turned)
            col_parts[piece, 0:LANES] = high
            col_parts[piece, LANES:] = low
        head_lane = lax.broadcasted_iota(jnp.int32, (1, LANES), 1) < heads
        before = jnp.zeros((1, LANES), F32)
        scal[...] = jnp.zeros_like(scal)
        for j in range(count):
            end = jnp.where(head_lane, col_ref[(j + 1) * BLOCK - 1 : (j + 1) * BLOCK, :], 0.0)
            scal[j : j + 1, :] = jnp.where(head_lane, jnp.exp2(end), 0.0)
            scal[count + j : count + j + 1, :] = jnp.where(head_lane, jnp.exp2(before), 0.0)
            before = before + end
        scal[2 * count : 2 * count + 1, :] = jnp.where(head_lane, jnp.exp2(before), 0.0)
        scal[2 * count + 1 : 2 * count + 2, 0:heads] = skip_ref[...]

    hot = hot_ref[...]
    high, low = two_parts(scal[...])
    row = dot(high, hot) + dot(low, hot)
    row_ref[...] = row
    hot_low = jnp.concatenate([hot_low_ref[...]] * 2, axis=0)
    state[...] = jnp.zeros_like(state)
    for j in range(count):
        piece = slice(j * BLOCK, (j + 1) * BLOCK)
        prior = docs_ref[max(j * BLOCK - 1, 0)]
        passage = row[j : j + 1, :] * jnp.where(ends[j] == prior, 1.0, 0.0)
        grown = dot(col_parts[piece, :], hot_low)
        scaled = (x_ref[piece, :].astype(F32) * grown).astype(BF16)
        old = state[...]
        enter_ref[j] = old
        state[...] = passage * old + dot(inputs_t[:, piece], scaled)

    half = state.shape[0] // 2
    total = row[2 * count : 2 * count + 1, :] * jnp.where(ends[count - 1] == docs_ref[0], 1.0, 0.0)
    mine = pl.multiple_of(sub_ref[0] * half, half)
    theirs = pl.multiple_of((1 - sub_ref[0]) * half, half)
    line = lax.broadcasted_iota(jnp.int32, (8, LANES), 0)
    first, last = docs_ref[0].astype(F32), docs_ref[length - 1].astype(F32)
    for j in range(wide // LANES):
        cols = slice(j * LANES, (j + 1) * LANES)
        foot = jnp.where(line == 0, total[:, cols], jnp.where(line == 1, first, last))
        own_ref[j, 0:half, :] = state[pl.ds(mine, half), cols]
        sent_ref[j, 0:half, :] = state[pl.ds(theirs, half), cols]
        own_ref[j, half:, :] = foot
        sent_ref[j, half:, :] = foot


def prepare_kernel(heads, docs_ref, b_ref, c_ref, col_ref, doc_row_ref, affinity_ref, entry_ref):
    k = pl.program_id(0)
    doc_col = col_ref[:, LANES - 1 : LANES]
    doc_row = doc_row_ref[...].astype(F32)
    t = lax.broadcasted_iota(jnp.int32, (BLOCK, BLOCK), 0)
    s = lax.broadcasted_iota(jnp.int32, (BLOCK, BLOCK), 1)
    affinity_ref[0] = jnp.where(
        (t >= s) & (doc_col == doc_row), dot(c_ref[...], b_ref[...], ((1,), (1,))), 0.0
    )
    prior_doc = docs_ref[jnp.maximum(k * BLOCK - 1, 0)].astype(F32)
    lane = lax.broadcasted_iota(jnp.int32, (1, LANES), 1)
    linked = (doc_col == prior_doc) & (lane < heads)
    high, low = two_parts(jnp.where(linked, jnp.exp2(col_ref[...]), 0.0))
    entry_ref[:, 0:LANES] = high
    entry_ref[:, LANES:] = low


def inner_kernel(
    width,
    first_tile,
    group,
    count,
    live_ref,
    docs_ref,
    x_ref,
    z_ref,
    c_ref,
    g_ref,
    col_ref,
    affinity_ref,
    entry_ref,
    enter_ref,
    row_ref,
    hot_ref,
    *refs,
):
    y_ref, f_ref = refs[-2:]
    k = pl.program_id(0)
    half = BLOCK // 2
    per_tile = LANES // width

    @pl.when(k >= live_ref[0])
    def _():
        y_ref[...] = jnp.zeros_like(y_ref)
        f_ref[...] = jnp.zeros_like(f_ref)

    @pl.when(k < live_ref[0])
    def _():
        readout = c_ref[...]
        twice = jnp.concatenate([readout, readout], axis=1)
        lane = lax.broadcasted_iota(jnp.int32, (1, LANES), 1)
        nothing = jnp.zeros((BLOCK, LANES), BF16)
        reaches = jnp.where(docs_ref[jnp.maximum(k * BLOCK - 1, 0)] == docs_ref[0], 1.0, 0.0)
        passed = pick_row(row_ref, count, count, k, slice(None)) * reaches
        for q in range(x_ref.shape[1] // (group * LANES)):
            cols = slice(q * group * LANES, (q + 1) * group * LANES)
            x = x_ref[:, cols]
            tops, bottoms, masked = [], [], []
            for u in range(group):
                part = x[:, u * LANES : (u + 1) * LANES]
                for i in range(per_tile):
                    h = (first_tile + q * group + u) * per_tile + i
                    cum = jnp.broadcast_to(col_ref[:, h : h + 1], (BLOCK, LANES))
                    left, right = g_ref[h : h + 1, :half], g_ref[h : h + 1, half:]
                    top = jnp.exp2(jnp.minimum(cum[:half] - left, 64.0))
                    bottom = jnp.exp2(cum[half:] - left)
                    corner = jnp.exp2(jnp.minimum(cum[half:] - right, 64.0))
                    tops.append((top * affinity_ref[0, :half, :half]).astype(BF16))
                    bottoms.append((bottom * affinity_ref[0, half:, :half]).astype(BF16))
                    bottoms.append((corner * affinity_ref[0, half:, half:]).astype(BF16))
                    mine = (lane >= i * width) & (lane < (i + 1) * width)
                    kept = part * jnp.where(mine, 1.0, 0.0).astype(BF16)
                    masked.append(
                        jnp.concatenate(
                            [kept if v == u else nothing for v in range(group)], axis=1
                        )
                    )
            upper = dot(
                jnp.concatenate(tops, axis=1),
                jnp.concatenate([m[:half] for m in masked], axis=0),
            )
            lower = dot(jnp.concatenate(bottoms, axis=1), jnp.concatenate(masked, axis=0))
            hot = hot_ref[:, cols]
            enter = dot(entry_ref[...], jnp.concatenate([hot, hot], axis=0))
            high, low = two_parts(enter_ref[0, :, cols])
            outer = dot(twice, jnp.concatenate([high, low], axis=0))
            skip = row_ref[2 * count + 1 : 2 * count + 2, cols]
            y = jnp.concatenate([upper, lower], axis=0) + enter * outer + skip * x.astype(F32)
            z = z_ref[:, cols].astype(F32)
            gate = z / (1.0 + jnp.exp2(-LOG2E * z))
            y_ref[:, cols] = y * gate
            f_ref[:, cols] = (enter * gate * passed[:, cols]).astype(BF16)


def join_kernel(sub_ref, own_ref, other_ref, c_ref, y_ref, f_ref, gated_ref, square_ref, total):
    k = pl.program_id(0)
    length = c_ref.shape[0]
    wide = own_ref.shape[0] * LANES
    here = pl.ds(pl.multiple_of(k * wide, wide), wide)
    second = sub_ref[0] == 1

    @pl.when(k == 0)
    def _():
        total[...] = jnp.zeros_like(total)

    highs, lows = [], []
    for j in range(wide // LANES):
        own, other = own_ref[j], other_ref[j]
        carry = jnp.concatenate(
            [jnp.where(second, other, own), jnp.where(second, own, other)], axis=0
        )
        high, low = two_parts(carry)
        highs.append(high)
        lows.append(low)
    carry = jnp.concatenate(
        [jnp.concatenate(highs, axis=1), jnp.concatenate(lows, axis=1)], axis=0
    )
    for r in range(0, length, BLOCK):
        rows = slice(r, r + BLOCK)
        readout = c_ref[rows, :]
        outer = dot(jnp.concatenate([readout, readout], axis=1), carry)
        gated = y_ref[rows, :] + f_ref[rows, :].astype(F32) * outer
        gated_ref[rows, here] = gated
        square = total[rows, :]
        for j in range(wide // LANES):
            piece = gated[:, j * LANES : (j + 1) * LANES]
            square = square + piece * piece
        total[rows, :] = square

    @pl.when(k == pl.num_programs(0) - 1)
    def _():
        square_ref[...] = jnp.sum(total[...].T, axis=0, keepdims=True)


def norm_kernel(channels_all, square_ref, more_ref, gain_ref, gated_ref, out_ref):
    rows = out_ref.shape[0]
    start = pl.multiple_of(pl.program_id(0) * rows, rows)
    scale = lax.rsqrt((square_ref[...] + more_ref[...]) / channels_all + 1e-05)
    scale = jnp.broadcast_to(scale, (LANES, rows)).T
    for j in range(gated_ref.shape[1] // LANES):
        cols = slice(j * LANES, (j + 1) * LANES)
        gated = gated_ref[pl.ds(start, rows), cols]
        out_ref[:, cols] = (gated * gain_ref[:, cols] * scale).astype(BF16)


def chunk_of(total, most):
    wide = most
    while total % wide:
        wide -= LANES
    return wide


def whole(shape):
    return pl.BlockSpec(shape, lambda k, *_: (0,) * len(shape))


SMEM = pl.BlockSpec(memory_space=pltpu.SMEM)
VMEM = pl.BlockSpec(memory_space=pltpu.VMEM)


def plan(chips, tiles):
    chunks = 2 if tiles % 2 == 0 else 1
    hops = chunks + chips - 2
    group = 2 if tiles % 2 == 0 else 1
    pieces = 5 if tiles % (5 * group) == 0 else 1
    return chunks, hops, group, pieces


def on_device(
    token_values,
    gate_values,
    state_input,
    state_readout,
    step_raw,
    step_bias,
    decay_log,
    skip_gain,
    norm_gain,
    document_ids,
    live_blocks,
):
    length, channels = token_values.shape
    heads = step_raw.shape[0]
    width = channels // heads
    states = state_input.shape[1]
    half = states // 2
    count = length // BLOCK
    tiles = channels // LANES
    rows = -(-heads // 8) * 8
    scalars = -(-(2 * count + 2) // 16) * 16
    assert lax.axis_size("sub") == 2 and 2 * rows < LANES and states == LANES

    raw = step_raw
    if rows != heads:
        raw = jnp.pad(raw, ((0, rows - heads), (0, 0)))
    doc_row = document_ids.reshape(1, length)
    sub = lax.axis_index("sub").astype(jnp.int32).reshape(1)
    head_of = np.arange(channels)[None, :] // width
    lanes = np.arange(LANES)[:, None]
    hot = jnp.asarray(lanes == head_of, dtype=BF16)
    hot_low = jnp.asarray(lanes == head_of + rows, dtype=BF16)
    tri = jnp.asarray(np.triu(np.ones((BLOCK, BLOCK))), dtype=BF16)

    chunk = chunk_of(channels, 512)
    per_chunk = chunk // LANES
    g, col, enter, own, sent, row = pl.pallas_call(
        functools.partial(state_kernel, heads),
        grid=(channels // chunk,),
        in_specs=[
            SMEM,
            SMEM,
            SMEM,
            whole((rows, length)),
            whole((1, heads)),
            whole((1, heads)),
            whole((1, heads)),
            whole((1, length)),
            whole((BLOCK, BLOCK)),
            pl.BlockSpec((LANES, chunk), lambda c: (0, c)),
            pl.BlockSpec((LANES, chunk), lambda c: (0, c)),
            pl.BlockSpec((length, chunk), lambda c: (0, c)),
            whole((length, states)),
        ],
        out_specs=[
            whole((rows, length)),
            whole((length, LANES)),
            pl.BlockSpec((count, states, chunk), lambda c: (0, 0, c)),
            pl.BlockSpec((per_chunk, half + 8, LANES), lambda c: (c, 0, 0)),
            pl.BlockSpec((per_chunk, half + 8, LANES), lambda c: (c, 0, 0)),
            pl.BlockSpec((scalars, chunk), lambda c: (0, c)),
        ],
        out_shape=[
            jax.ShapeDtypeStruct((rows, length), F32),
            jax.ShapeDtypeStruct((length, LANES), F32),
            jax.ShapeDtypeStruct((count, states, channels), F32),
            jax.ShapeDtypeStruct((tiles, half + 8, LANES), F32),
            jax.ShapeDtypeStruct((tiles, half + 8, LANES), F32),
            jax.ShapeDtypeStruct((scalars, channels), F32),
        ],
        scratch_shapes=[
            pltpu.VMEM((LANES, length), F32),
            pltpu.VMEM((length, 2 * LANES), BF16),
            pltpu.VMEM((states, length), BF16),
            pltpu.VMEM((states, chunk), F32),
            pltpu.VMEM((scalars, LANES), F32),
        ],
        name="shard_state",
    )(
        live_blocks,
        document_ids,
        sub,
        raw,
        step_bias.reshape(1, heads),
        decay_log.reshape(1, heads),
        skip_gain.reshape(1, heads),
        doc_row,
        tri,
        hot,
        hot_low,
        token_values,
        state_input,
    )

    affinity, entry = pl.pallas_call(
        functools.partial(prepare_kernel, heads),
        grid=(count,),
        in_specs=[
            SMEM,
            pl.BlockSpec((BLOCK, states), lambda k: (k, 0)),
            pl.BlockSpec((BLOCK, states), lambda k: (k, 0)),
            pl.BlockSpec((BLOCK, LANES), lambda k: (k, 0)),
            pl.BlockSpec((1, BLOCK), lambda k: (0, k)),
        ],
        out_specs=[
            pl.BlockSpec((1, BLOCK, BLOCK), lambda k: (k, 0, 0)),
            pl.BlockSpec((BLOCK, 2 * LANES), lambda k: (k, 0)),
        ],
        out_shape=[
            jax.ShapeDtypeStruct((count, BLOCK, BLOCK), F32),
            jax.ShapeDtypeStruct((length, 2 * LANES), BF16),
        ],
        name="prepare",
    )(document_ids, state_input, state_readout, col, doc_row)

    group, pieces = plan(lax.axis_size("seq"), tiles)[2:]
    wide = channels // pieces
    filled = ()
    for q in range(pieces):
        filled = pl.pallas_call(
            functools.partial(inner_kernel, width, q * wide // LANES, group, count),
            grid=(count,),
            in_specs=[
                SMEM,
                SMEM,
                pl.BlockSpec((BLOCK, wide), lambda k, q=q: (k, q)),
                pl.BlockSpec((BLOCK, wide), lambda k, q=q: (k, q)),
                pl.BlockSpec((BLOCK, states), lambda k: (k, 0)),
                pl.BlockSpec((rows, BLOCK), lambda k: (0, k)),
                pl.BlockSpec((BLOCK, LANES), lambda k: (k, 0)),
                pl.BlockSpec((1, BLOCK, BLOCK), lambda k: (k, 0, 0)),
                pl.BlockSpec((BLOCK, 2 * LANES), lambda k: (k, 0)),
                pl.BlockSpec((1, states, wide), lambda k, q=q: (k, 0, q)),
                pl.BlockSpec((scalars, wide), lambda k, q=q: (0, q)),
                pl.BlockSpec((LANES, wide), lambda k, q=q: (0, q)),
            ]
            + [pl.BlockSpec(memory_space=pl.ANY)] * len(filled),
            out_specs=[pl.BlockSpec((BLOCK, wide), lambda k, q=q: (k, q))] * 2,
            out_shape=[
                jax.ShapeDtypeStruct((length, channels), F32),
                jax.ShapeDtypeStruct((length, channels), BF16),
            ],
            input_output_aliases={12: 0, 13: 1} if filled else {},
            cost_estimate=pl.CostEstimate(
                flops=length * wide * 1200,
                bytes_accessed=length * wide * 10,
                transcendentals=0,
            ),
        )(
            live_blocks,
            document_ids,
            token_values,
            gate_values,
            state_readout,
            g,
            col,
            affinity,
            entry,
            enter,
            row,
            hot,
            *filled,
        )

    own, other = carry_in(own, sent, half)

    gated, squares = pl.pallas_call(
        join_kernel,
        grid=(channels // chunk,),
        in_specs=[
            SMEM,
            pl.BlockSpec((per_chunk, half, LANES), lambda k: (k, 0, 0)),
            pl.BlockSpec((per_chunk, half, LANES), lambda k: (k, 0, 0)),
            whole((length, states)),
            pl.BlockSpec((length, chunk), lambda k: (0, k)),
            pl.BlockSpec((length, chunk), lambda k: (0, k)),
        ],
        out_specs=[VMEM, whole((1, length))],
        out_shape=[
            jax.ShapeDtypeStruct((length, channels), F32),
            jax.ShapeDtypeStruct((1, length), F32),
        ],
        scratch_shapes=[pltpu.VMEM((length, LANES), F32)],
        compiler_params=pltpu.CompilerParams(vmem_limit_bytes=24 << 20),
        name="join",
    )(sub, own, other, state_readout, *filled)

    squares, more = summed(squares, "head")
    return pl.pallas_call(
        functools.partial(norm_kernel, channels * lax.axis_size("head")),
        grid=(count,),
        in_specs=[
            pl.BlockSpec((1, BLOCK), lambda k: (0, k)),
            pl.BlockSpec((1, BLOCK), lambda k: (0, k)),
            whole((1, channels)),
            VMEM,
        ],
        out_specs=pl.BlockSpec((BLOCK, channels), lambda k: (k, 0)),
        out_shape=jax.ShapeDtypeStruct((length, channels), BF16),
        compiler_params=pltpu.CompilerParams(vmem_limit_bytes=16 << 20),
        name="norm",
    )(squares, more, norm_gain.reshape(1, channels), gated)


def summed(value, axis):
    size = lax.axis_size(axis)
    if size & (size - 1):
        total = value
        for shift in range(1, size):
            total = total + lax.ppermute(value, axis, [(i, (i + shift) % size) for i in range(size)])
        return total, jnp.zeros_like(value)
    more, shift = jnp.zeros_like(value), 1
    while shift < size:
        value = value + more if shift > 1 else value
        more = lax.ppermute(value, axis, [(i, i ^ shift) for i in range(size)])
        shift *= 2
    return value, more


def carry_in(own, sent, half):
    tiles = own.shape[0]
    second = lax.axis_index("sub") == 1
    place, chips = lax.axis_index("seq"), lax.axis_size("seq")
    got = lax.ppermute(sent, "sub", [(0, 1), (1, 0)])
    early = jnp.where(second, got, own)
    late = jnp.where(second, own, got)
    first, last = early[0, half + 1], late[0, half + 2]
    link = jnp.where(early[0, half + 2] == late[0, half + 1], 1.0, 0.0)
    early_decay, late_decay = early[:, half : half + 1], late[:, half : half + 1] * link
    early, late = early[:, :half], late[:, :half]
    chip_state = late_decay * early + late
    chip_decay = late_decay * early_decay

    chunks, hops = plan(chips, tiles)[:2]
    size = tiles // chunks
    rows = size * half
    tail = jnp.broadcast_to(last, (8, LANES))

    def at(array, index):
        return lax.dynamic_slice_in_dim(array, index * size, size, 0)

    carry = jnp.zeros((size, half, LANES), F32)
    received = []
    for t in range(hops):
        index = jnp.clip(t - place, 0, chunks - 1)
        send = at(chip_decay, index) * carry + at(chip_state, index)
        send = jnp.concatenate([send.reshape(rows, LANES), tail], axis=0)
        pairs = [(z, z + 1) for z in range(chips - 1) if 0 <= t - z < chunks]
        got = lax.ppermute(send, "seq", pairs)
        joined = jnp.where(got[rows : rows + 1] == first, 1.0, 0.0)
        carry = joined[None] * got[:rows].reshape(size, half, LANES)
        received.append(carry)
    parts = []
    for c in range(chunks):
        part = jnp.zeros((size, half, LANES), F32)
        for z in range(1, chips):
            part = jnp.where(place == z, received[c + z - 1], part)
        parts.append(part)
    entering = jnp.concatenate(parts, axis=0)
    onward = link * (early_decay * entering + early)
    mine = jnp.where(second, onward, entering)
    other = lax.ppermute(jnp.where(second, entering, onward), "sub", [(0, 1), (1, 0)])
    return mine, other


def solution(mesh):
    placed = (
        P(("groups", "seq", "sub"), "head"),
        P(("groups", "seq", "sub"), "head"),
        P(("groups", "seq", "sub"), None),
        P(("groups", "seq", "sub"), None),
        P("head", ("seq", "sub")),
        P("head"),
        P("head"),
        P("head"),
        P("head"),
        P(("groups", "seq", "sub")),
        P(("groups", "seq", "sub")),
    )

    return jax.shard_map(
        on_device,
        mesh=mesh,
        in_specs=placed,
        out_specs=P(("groups", "seq", "sub"), "head"),
        check_vma=False,
    )
```

```python
import functools
import math

import jax
import jax.numpy as jnp
import numpy as np
from jax import lax
from jax.experimental import pallas as pl
from jax.experimental.pallas import tpu as pltpu
from jax.sharding import PartitionSpec as P

BLOCK = 256
LANES = 128
LOG2E = math.log2(math.e)
F32 = jnp.float32
BF16 = jnp.bfloat16


def dot(a, b, contract=((1,), (0,))):
    return lax.dot_general(a, b, (contract, ((), ())), preferred_element_type=F32)


def two_parts(value):
    high = value.astype(BF16)
    low = (value - high.astype(F32)).astype(BF16)
    return high, low


def pick_row(ref, base, count, k, cols):
    row = ref[base : base + 1, cols]
    for j in range(1, count):
        row = jnp.where(k == j, ref[base + j : base + j + 1, cols], row)
    return row


def softplus(v):
    u = jnp.exp(-jnp.abs(v))
    s = u / (2.0 + u)
    q = s * s
    series = jnp.full_like(q, 1.0 / 15.0)
    for odd in (13, 11, 9, 7, 5, 3, 1):
        series = series * q + 1.0 / odd
    return jnp.maximum(v, 0.0) + 2.0 * s * series


def state_kernel(
    heads,
    live_ref,
    docs_ref,
    sub_ref,
    raw_ref,
    bias_ref,
    decay_ref,
    skip_ref,
    doc_row_ref,
    tri_ref,
    hot_ref,
    hot_low_ref,
    x_ref,
    b_ref,
    g_ref,
    col_ref,
    enter_ref,
    own_ref,
    sent_ref,
    row_ref,
    pack,
    col_parts,
    inputs_t,
    state,
    scal,
):
    length = raw_ref.shape[0 + 1]
    rows = raw_ref.shape[0]
    count = length // BLOCK
    wide = x_ref.shape[1]
    ends = [docs_ref[j * BLOCK + BLOCK - 1] for j in range(count)]

    @pl.when(pl.program_id(0) == 0)
    def _():
        inputs_t[...] = b_ref[...].T
        pack[...] = jnp.zeros_like(pack)
        pack[0:1, 0:heads] = bias_ref[...]
        pack[1:2, 0:heads] = decay_ref[...]
        params = pack[0:LANES, 0:LANES].T
        lane = lax.broadcasted_iota(jnp.int32, (1, length), 1)
        step = softplus(raw_ref[...] + params[0:rows, 0:1])
        step = jnp.where(lane < live_ref[0] * BLOCK, step, 0.0)
        rate = (-LOG2E * jnp.exp(params[0:rows, 1:2])) * step
        high, _ = two_parts(rate)
        middle, low = two_parts(rate - high.astype(F32))
        tri = tri_ref[...]
        logs = jnp.where(step > 0.0, LOG2E * jnp.log(step), -1e30)
        for j in range(count):
            piece = slice(j * BLOCK, (j + 1) * BLOCK)
            cum = dot(high[:, piece], tri) + (dot(middle[:, piece], tri) + dot(low[:, piece], tri))
            g_ref[:, piece] = cum - logs[:, piece]
            same = doc_row_ref[:, piece] == ends[j]
            pack[0:rows, piece] = cum
            pack[rows : 2 * rows, piece] = jnp.where(
                same, step[:, piece] * jnp.exp2(cum[:, BLOCK - 1 :] - cum), 0.0
            )
        pack[LANES - 1 : LANES, :] = doc_row_ref[...].astype(F32)
        for j in range(count):
            piece = slice(j * BLOCK, (j + 1) * BLOCK)
            turned = pack[:, piece].T
            col_ref[piece, :] = turned
            high, low = two_parts(turned)
            col_parts[piece, 0:LANES] = high
            col_parts[piece, LANES:] = low
        head_lane = lax.broadcasted_iota(jnp.int32, (1, LANES), 1) < heads
        before = jnp.zeros((1, LANES), F32)
        scal[...] = jnp.zeros_like(scal)
        for j in range(count):
            end = jnp.where(head_lane, col_ref[(j + 1) * BLOCK - 1 : (j + 1) * BLOCK, :], 0.0)
            scal[j : j + 1, :] = jnp.where(head_lane, jnp.exp2(end), 0.0)
            scal[count + j : count + j + 1, :] = jnp.where(head_lane, jnp.exp2(before), 0.0)
            before = before + end
        scal[2 * count : 2 * count + 1, :] = jnp.where(head_lane, jnp.exp2(before), 0.0)
        scal[2 * count + 1 : 2 * count + 2, 0:heads] = skip_ref[...]

    hot = hot_ref[...]
    high, low = two_parts(scal[...])
    row = dot(high, hot) + dot(low, hot)
    row_ref[...] = row
    hot_low = jnp.concatenate([hot_low_ref[...]] * 2, axis=0)
    state[...] = jnp.zeros_like(state)
    scaled = (x_ref[...].astype(F32) * dot(col_parts[...], hot_low)).astype(BF16)
    for j in range(count):
        piece = slice(j * BLOCK, (j + 1) * BLOCK)
        prior = docs_ref[max(j * BLOCK - 1, 0)]
        passage = row[j : j + 1, :] * jnp.where(ends[j] == prior, 1.0, 0.0)
        old = state[...]
        enter_ref[j] = old.astype(BF16)
        state[...] = passage * old + dot(inputs_t[:, piece], scaled[piece])

    half = state.shape[0] // 2
    total = row[2 * count : 2 * count + 1, :] * jnp.where(ends[count - 1] == docs_ref[0], 1.0, 0.0)
    mine = pl.multiple_of(sub_ref[0] * half, half)
    theirs = pl.multiple_of((1 - sub_ref[0]) * half, half)
    line = lax.broadcasted_iota(jnp.int32, (8, LANES), 0)
    first, last = docs_ref[0].astype(F32), docs_ref[length - 1].astype(F32)
    for j in range(wide // LANES):
        cols = slice(j * LANES, (j + 1) * LANES)
        foot = jnp.where(line == 0, total[:, cols], jnp.where(line == 1, first, last))
        own_ref[j, 0:half, :] = state[pl.ds(mine, half), cols]
        sent_ref[j, 0:half, :] = state[pl.ds(theirs, half), cols]
        own_ref[j, half:, :] = foot
        sent_ref[j, half:, :] = foot


def prepare_kernel(heads, docs_ref, b_ref, c_ref, col_ref, doc_row_ref, affinity_ref, entry_ref):
    t = lax.broadcasted_iota(jnp.int32, (BLOCK, BLOCK), 0)
    s = lax.broadcasted_iota(jnp.int32, (BLOCK, BLOCK), 1)
    lane = lax.broadcasted_iota(jnp.int32, (1, LANES), 1)
    for j in range(affinity_ref.shape[0]):
        piece = slice(j * BLOCK, (j + 1) * BLOCK)
        block = pl.program_id(0) * affinity_ref.shape[0] + j
        columns = col_ref[piece, :]
        doc_col = columns[:, LANES - 1 :]
        doc_row = doc_row_ref[:, piece].astype(F32)
        affinity_ref[j] = jnp.where(
            (t >= s) & (doc_col == doc_row),
            dot(c_ref[piece, :], b_ref[piece, :], ((1,), (1,))),
            0.0,
        )
        prior_doc = docs_ref[jnp.maximum(block * BLOCK - 1, 0)].astype(F32)
        linked = (doc_col == prior_doc) & (lane < heads)
        high, low = two_parts(jnp.where(linked, jnp.exp2(columns), 0.0))
        entry_ref[piece, 0:LANES] = high
        entry_ref[piece, LANES:] = low


def inner_kernel(
    width,
    first_tile,
    group,
    count,
    live_ref,
    docs_ref,
    x_ref,
    z_ref,
    c_ref,
    g_ref,
    col_ref,
    affinity_ref,
    entry_ref,
    enter_ref,
    row_ref,
    hot_ref,
    *refs,
):
    y_ref, f_ref = refs[-2:]
    k = pl.program_id(0)
    half = BLOCK // 2
    per_tile = LANES // width

    @pl.when(k >= live_ref[0])
    def _():
        y_ref[...] = jnp.zeros_like(y_ref)
        f_ref[...] = jnp.zeros_like(f_ref)

    @pl.when(k < live_ref[0])
    def _():
        readout = c_ref[...]
        lane = lax.broadcasted_iota(jnp.int32, (1, LANES), 1)
        nothing = jnp.zeros((BLOCK, LANES), BF16)
        reaches = jnp.where(docs_ref[jnp.maximum(k * BLOCK - 1, 0)] == docs_ref[0], 1.0, 0.0)
        passed = pick_row(row_ref, count, count, k, slice(None)) * reaches
        for q in range(x_ref.shape[1] // (group * LANES)):
            cols = slice(q * group * LANES, (q + 1) * group * LANES)
            x = x_ref[:, cols]
            tops, bottoms, masked = [], [], []
            for u in range(group):
                part = x[:, u * LANES : (u + 1) * LANES]
                for i in range(per_tile):
                    h = (first_tile + q * group + u) * per_tile + i
                    cum = jnp.broadcast_to(col_ref[:, h : h + 1], (BLOCK, LANES))
                    left, right = g_ref[h : h + 1, :half], g_ref[h : h + 1, half:]
                    top = jnp.exp2(jnp.minimum(cum[:half] - left, 64.0))
                    bottom = jnp.exp2(cum[half:] - left)
                    corner = jnp.exp2(jnp.minimum(cum[half:] - right, 64.0))
                    tops.append((top * affinity_ref[0, :half, :half]).astype(BF16))
                    bottoms.append((bottom * affinity_ref[0, half:, :half]).astype(BF16))
                    bottoms.append((corner * affinity_ref[0, half:, half:]).astype(BF16))
                    mine = (lane >= i * width) & (lane < (i + 1) * width)
                    kept = part * jnp.where(mine, 1.0, 0.0).astype(BF16)
                    masked.append(
                        jnp.concatenate(
                            [kept if v == u else nothing for v in range(group)], axis=1
                        )
                    )
            upper = dot(
                jnp.concatenate(tops, axis=1),
                jnp.concatenate([m[:half] for m in masked], axis=0),
            )
            lower = dot(jnp.concatenate(bottoms, axis=1), jnp.concatenate(masked, axis=0))
            hot = jnp.concatenate([hot_ref[:, cols]] * 2, axis=0)
            enter = dot(entry_ref[...], hot)
            outer = dot(readout, enter_ref[0, :, cols])
            skip = row_ref[2 * count + 1 : 2 * count + 2, cols]
            y = jnp.concatenate([upper, lower], axis=0) + enter * outer + skip * x.astype(F32)
            z = z_ref[:, cols].astype(F32)
            gate = z / (1.0 + jnp.exp2(-LOG2E * z))
            y_ref[:, cols] = y * gate
            f_ref[:, cols] = (enter * gate * passed[:, cols]).astype(BF16)


def join_kernel(sub_ref, own_ref, other_ref, c_ref, y_ref, f_ref, gated_ref, square_ref, total):
    k = pl.program_id(0)
    length = c_ref.shape[0]
    wide = own_ref.shape[0] * LANES
    here = pl.ds(pl.multiple_of(k * wide, wide), wide)
    second = sub_ref[0] == 1

    @pl.when(k == 0)
    def _():
        total[...] = jnp.zeros_like(total)

    parts = []
    for j in range(wide // LANES):
        own, other = own_ref[j].astype(BF16), other_ref[j].astype(BF16)
        parts.append(
            jnp.concatenate(
                [jnp.where(second, other, own), jnp.where(second, own, other)], axis=0
            )
        )
    carry = jnp.concatenate(parts, axis=1)
    for r in range(0, length, BLOCK):
        rows = slice(r, r + BLOCK)
        outer = dot(c_ref[rows, :], carry)
        gated = y_ref[rows, :] + f_ref[rows, :].astype(F32) * outer
        gated_ref[rows, here] = gated
        square = total[rows, :]
        for j in range(wide // LANES):
            piece = gated[:, j * LANES : (j + 1) * LANES]
            square = square + piece * piece
        total[rows, :] = square

    @pl.when(k == pl.num_programs(0) - 1)
    def _():
        square_ref[...] = jnp.sum(total[...].T, axis=0, keepdims=True)


def norm_kernel(channels_all, square_ref, more_ref, gain_ref, gated_ref, out_ref):
    rows = out_ref.shape[0]
    start = pl.multiple_of(pl.program_id(0) * rows, rows)
    scale = lax.rsqrt((square_ref[...] + more_ref[...]) / channels_all + 1e-05)
    scale = jnp.broadcast_to(scale, (LANES, rows)).T
    for j in range(gated_ref.shape[1] // LANES):
        cols = slice(j * LANES, (j + 1) * LANES)
        gated = gated_ref[pl.ds(start, rows), cols]
        out_ref[:, cols] = (gated * gain_ref[:, cols] * scale).astype(BF16)


def chunk_of(total, most):
    wide = most
    while total % wide:
        wide -= LANES
    return wide


def whole(shape):
    return pl.BlockSpec(shape, lambda k, *_: (0,) * len(shape))


SMEM = pl.BlockSpec(memory_space=pltpu.SMEM)
VMEM = pl.BlockSpec(memory_space=pltpu.VMEM)


def plan(chips, tiles):
    chunks = 2 if tiles % 2 == 0 else 1
    pieces = (tiles,)
    if tiles % 10 == 0:
        pieces = (3 * tiles // 10,) * 2 + (tiles // 5,) * 2
    return chunks, chunks + chips - 2, pieces


def on_device(
    token_values,
    gate_values,
    state_input,
    state_readout,
    step_raw,
    step_bias,
    decay_log,
    skip_gain,
    norm_gain,
    document_ids,
    live_blocks,
):
    length, channels = token_values.shape
    heads = step_raw.shape[0]
    width = channels // heads
    states = state_input.shape[1]
    half = states // 2
    count = length // BLOCK
    tiles = channels // LANES
    rows = -(-heads // 8) * 8
    scalars = -(-(2 * count + 2) // 16) * 16
    assert lax.axis_size("sub") == 2 and 2 * rows < LANES and states == LANES

    raw = step_raw
    if rows != heads:
        raw = jnp.pad(raw, ((0, rows - heads), (0, 0)))
    doc_row = document_ids.reshape(1, length)
    sub = lax.axis_index("sub").astype(jnp.int32).reshape(1)
    head_of = np.arange(channels)[None, :] // width
    lanes = np.arange(LANES)[:, None]
    hot = jnp.asarray(lanes == head_of, dtype=BF16)
    hot_low = jnp.asarray(lanes == head_of + rows, dtype=BF16)
    tri = jnp.asarray(np.triu(np.ones((BLOCK, BLOCK))), dtype=BF16)

    chunk = chunk_of(channels, 512)
    per_chunk = chunk // LANES
    g, col, enter, own, sent, row = pl.pallas_call(
        functools.partial(state_kernel, heads),
        grid=(channels // chunk,),
        in_specs=[
            SMEM,
            SMEM,
            SMEM,
            whole((rows, length)),
            whole((1, heads)),
            whole((1, heads)),
            whole((1, heads)),
            whole((1, length)),
            whole((BLOCK, BLOCK)),
            pl.BlockSpec((LANES, chunk), lambda c: (0, c)),
            pl.BlockSpec((LANES, chunk), lambda c: (0, c)),
            pl.BlockSpec((length, chunk), lambda c: (0, c)),
            whole((length, states)),
        ],
        out_specs=[
            whole((rows, length)),
            whole((length, LANES)),
            pl.BlockSpec((count, states, chunk), lambda c: (0, 0, c)),
            pl.BlockSpec((per_chunk, half + 8, LANES), lambda c: (c, 0, 0)),
            pl.BlockSpec((per_chunk, half + 8, LANES), lambda c: (c, 0, 0)),
            pl.BlockSpec((scalars, chunk), lambda c: (0, c)),
        ],
        out_shape=[
            jax.ShapeDtypeStruct((rows, length), F32),
            jax.ShapeDtypeStruct((length, LANES), F32),
            jax.ShapeDtypeStruct((count, states, channels), BF16),
            jax.ShapeDtypeStruct((tiles, half + 8, LANES), F32),
            jax.ShapeDtypeStruct((tiles, half + 8, LANES), F32),
            jax.ShapeDtypeStruct((scalars, channels), F32),
        ],
        scratch_shapes=[
            pltpu.VMEM((LANES, length), F32),
            pltpu.VMEM((length, 2 * LANES), BF16),
            pltpu.VMEM((states, length), BF16),
            pltpu.VMEM((states, chunk), F32),
            pltpu.VMEM((scalars, LANES), F32),
        ],
        name="shard_state",
    )(
        live_blocks,
        document_ids,
        sub,
        raw,
        step_bias.reshape(1, heads),
        decay_log.reshape(1, heads),
        skip_gain.reshape(1, heads),
        doc_row,
        tri,
        hot,
        hot_low,
        token_values,
        state_input,
    )

    span = 2 if count % 2 == 0 else 1
    affinity, entry = pl.pallas_call(
        functools.partial(prepare_kernel, heads),
        grid=(count // span,),
        in_specs=[
            SMEM,
            pl.BlockSpec((span * BLOCK, states), lambda k: (k, 0)),
            pl.BlockSpec((span * BLOCK, states), lambda k: (k, 0)),
            pl.BlockSpec((span * BLOCK, LANES), lambda k: (k, 0)),
            pl.BlockSpec((1, span * BLOCK), lambda k: (0, k)),
        ],
        out_specs=[
            pl.BlockSpec((span, BLOCK, BLOCK), lambda k: (k, 0, 0)),
            pl.BlockSpec((span * BLOCK, 2 * LANES), lambda k: (k, 0)),
        ],
        out_shape=[
            jax.ShapeDtypeStruct((count, BLOCK, BLOCK), F32),
            jax.ShapeDtypeStruct((length, 2 * LANES), BF16),
        ],
        name="prepare",
    )(document_ids, state_input, state_readout, col, doc_row)

    pieces = plan(lax.axis_size("seq"), tiles)[2]
    group = 2 if tiles % 2 == 0 else 1
    filled, at = (), 0
    for size in pieces:
        wide, first = size * LANES, at // size
        filled = pl.pallas_call(
            functools.partial(inner_kernel, width, at, group, count),
            grid=(count,),
            in_specs=[
                SMEM,
                SMEM,
                pl.BlockSpec((BLOCK, wide), lambda k, q=first: (k, q)),
                pl.BlockSpec((BLOCK, wide), lambda k, q=first: (k, q)),
                pl.BlockSpec((BLOCK, states), lambda k: (k, 0)),
                pl.BlockSpec((rows, BLOCK), lambda k: (0, k)),
                pl.BlockSpec((BLOCK, LANES), lambda k: (k, 0)),
                pl.BlockSpec((1, BLOCK, BLOCK), lambda k: (k, 0, 0)),
                pl.BlockSpec((BLOCK, 2 * LANES), lambda k: (k, 0)),
                pl.BlockSpec((1, states, wide), lambda k, q=first: (k, 0, q)),
                pl.BlockSpec((scalars, wide), lambda k, q=first: (0, q)),
                pl.BlockSpec((LANES, wide), lambda k, q=first: (0, q)),
            ]
            + [pl.BlockSpec(memory_space=pl.ANY)] * len(filled),
            out_specs=[pl.BlockSpec((BLOCK, wide), lambda k, q=first: (k, q))] * 2,
            out_shape=[
                jax.ShapeDtypeStruct((length, channels), F32),
                jax.ShapeDtypeStruct((length, channels), BF16),
            ],
            input_output_aliases={12: 0, 13: 1} if filled else {},
            cost_estimate=pl.CostEstimate(
                flops=length * wide * 1200,
                bytes_accessed=length * wide * 10,
                transcendentals=0,
            ),
        )(
            live_blocks,
            document_ids,
            token_values,
            gate_values,
            state_readout,
            g,
            col,
            affinity,
            entry,
            enter,
            row,
            hot,
            *filled,
        )
        at += size

    own, other = carry_in(own, sent, half)

    gated, squares = pl.pallas_call(
        join_kernel,
        grid=(channels // chunk,),
        in_specs=[
            SMEM,
            pl.BlockSpec((per_chunk, half, LANES), lambda k: (k, 0, 0)),
            pl.BlockSpec((per_chunk, half, LANES), lambda k: (k, 0, 0)),
            whole((length, states)),
            pl.BlockSpec((length, chunk), lambda k: (0, k)),
            pl.BlockSpec((length, chunk), lambda k: (0, k)),
        ],
        out_specs=[VMEM, whole((1, length))],
        out_shape=[
            jax.ShapeDtypeStruct((length, channels), F32),
            jax.ShapeDtypeStruct((1, length), F32),
        ],
        scratch_shapes=[pltpu.VMEM((length, LANES), F32)],
        compiler_params=pltpu.CompilerParams(vmem_limit_bytes=24 << 20),
        name="join",
    )(
        sub,
        own,
        other,
        state_readout,
        *[pltpu.with_memory_space_constraint(part, pltpu.HBM) for part in filled],
    )

    squares, more = summed(squares, "head")
    return pl.pallas_call(
        functools.partial(norm_kernel, channels * lax.axis_size("head")),
        grid=(count,),
        in_specs=[
            pl.BlockSpec((1, BLOCK), lambda k: (0, k)),
            pl.BlockSpec((1, BLOCK), lambda k: (0, k)),
            whole((1, channels)),
            VMEM,
        ],
        out_specs=pl.BlockSpec((BLOCK, channels), lambda k: (k, 0)),
        out_shape=jax.ShapeDtypeStruct((length, channels), BF16),
        compiler_params=pltpu.CompilerParams(vmem_limit_bytes=16 << 20),
        name="norm",
    )(squares, more, norm_gain.reshape(1, channels), gated)


def summed(value, axis):
    size = lax.axis_size(axis)
    if size & (size - 1):
        total = value
        for shift in range(1, size):
            total = total + lax.ppermute(value, axis, [(i, (i + shift) % size) for i in range(size)])
        return total, jnp.zeros_like(value)
    more, shift = jnp.zeros_like(value), 1
    while shift < size:
        value = value + more if shift > 1 else value
        more = lax.ppermute(value, axis, [(i, i ^ shift) for i in range(size)])
        shift *= 2
    return value, more


def carry_in(own, sent, half):
    tiles = own.shape[0]
    second = lax.axis_index("sub") == 1
    place, chips = lax.axis_index("seq"), lax.axis_size("seq")
    got = lax.ppermute(sent, "sub", [(0, 1), (1, 0)])
    early = jnp.where(second, got, own)
    late = jnp.where(second, own, got)
    first, last = early[0, half + 1], late[0, half + 2]
    link = jnp.where(early[0, half + 2] == late[0, half + 1], 1.0, 0.0)
    early_decay, late_decay = early[:, half : half + 1], late[:, half : half + 1] * link
    early, late = early[:, :half], late[:, :half]
    chip_state = late_decay * early + late
    chip_decay = late_decay * early_decay

    chunks, hops = plan(chips, tiles)[:2]
    size = tiles // chunks
    rows = size * half
    tail = jnp.broadcast_to(last, (8, LANES))

    def at(array, index):
        return lax.dynamic_slice_in_dim(array, index * size, size, 0)

    carry = jnp.zeros((size, half, LANES), F32)
    received = []
    for t in range(hops):
        index = jnp.clip(t - place, 0, chunks - 1)
        send = at(chip_decay, index) * carry + at(chip_state, index)
        send = jnp.concatenate([send.reshape(rows, LANES), tail], axis=0)
        pairs = [(z, z + 1) for z in range(chips - 1) if 0 <= t - z < chunks]
        got = lax.ppermute(send, "seq", pairs)
        joined = jnp.where(got[rows : rows + 1] == first, 1.0, 0.0)
        carry = joined[None] * got[:rows].reshape(size, half, LANES)
        received.append(carry)
    parts = []
    for c in range(chunks):
        part = jnp.zeros((size, half, LANES), F32)
        for z in range(1, chips):
            part = jnp.where(place == z, received[c + z - 1], part)
        parts.append(part)
    entering = jnp.concatenate(parts, axis=0)
    onward = link * (early_decay * entering + early)
    mine = jnp.where(second, onward, entering)
    other = lax.ppermute(jnp.where(second, entering, onward), "sub", [(0, 1), (1, 0)])
    return mine, other


def solution(mesh):
    placed = (
        P(("groups", "seq", "sub"), "head"),
        P(("groups", "seq", "sub"), "head"),
        P(("groups", "seq", "sub"), None),
        P(("groups", "seq", "sub"), None),
        P("head", ("seq", "sub")),
        P("head"),
        P("head"),
        P("head"),
        P("head"),
        P(("groups", "seq", "sub")),
        P(("groups", "seq", "sub")),
    )

    return jax.shard_map(
        on_device,
        mesh=mesh,
        in_specs=placed,
        out_specs=P(("groups", "seq", "sub"), "head"),
        check_vma=False,
    )
```

```python
import functools
import math

import jax
import jax.numpy as jnp
import numpy as np
from jax import lax
from jax.experimental import pallas as pl
from jax.experimental.pallas import tpu as pltpu
from jax.sharding import PartitionSpec as P

BLOCK = 256
LANES = 128
LOG2E = math.log2(math.e)
INNER_VMEM = 40 << 20
F32 = jnp.float32
BF16 = jnp.bfloat16


def dot(a, b, contract=((1,), (0,))):
    return lax.dot_general(a, b, (contract, ((), ())), preferred_element_type=F32)


def two_parts(value):
    high = value.astype(BF16)
    low = (value - high.astype(F32)).astype(BF16)
    return high, low


def pick_row(ref, base, count, k, cols):
    row = ref[base : base + 1, cols]
    for j in range(1, count):
        row = jnp.where(k == j, ref[base + j : base + j + 1, cols], row)
    return row


def softplus(v):
    u = jnp.exp(-jnp.abs(v))
    s = u / (2.0 + u)
    q = s * s
    series = jnp.full_like(q, 1.0 / 15.0)
    for odd in (13, 11, 9, 7, 5, 3, 1):
        series = series * q + 1.0 / odd
    return jnp.maximum(v, 0.0) + 2.0 * s * series


def state_kernel(
    heads,
    live_ref,
    docs_ref,
    sub_ref,
    raw_ref,
    bias_ref,
    decay_ref,
    skip_ref,
    doc_row_ref,
    tri_ref,
    hot_ref,
    hot_low_ref,
    x_ref,
    b_ref,
    g_ref,
    col_ref,
    enter_ref,
    own_ref,
    sent_ref,
    row_ref,
    pack,
    col_parts,
    inputs_t,
    state,
    scal,
):
    length = raw_ref.shape[0 + 1]
    rows = raw_ref.shape[0]
    count = length // BLOCK
    wide = x_ref.shape[1]
    ends = [docs_ref[j * BLOCK + BLOCK - 1] for j in range(count)]

    @pl.when(pl.program_id(0) == 0)
    def _():
        inputs_t[...] = b_ref[...].T
        pack[...] = jnp.zeros_like(pack)
        pack[0:1, 0:heads] = bias_ref[...]
        pack[1:2, 0:heads] = decay_ref[...]
        params = pack[0:LANES, 0:LANES].T
        lane = lax.broadcasted_iota(jnp.int32, (1, length), 1)
        step = softplus(raw_ref[...] + params[0:rows, 0:1])
        step = jnp.where(lane < live_ref[0] * BLOCK, step, 0.0)
        rate = (-LOG2E * jnp.exp(params[0:rows, 1:2])) * step
        high, _ = two_parts(rate)
        middle, low = two_parts(rate - high.astype(F32))
        tri = tri_ref[...]
        logs = jnp.where(step > 0.0, LOG2E * jnp.log(step), -1e30)
        for j in range(count):
            piece = slice(j * BLOCK, (j + 1) * BLOCK)
            cum = dot(high[:, piece], tri) + (dot(middle[:, piece], tri) + dot(low[:, piece], tri))
            g_ref[:, piece] = cum - logs[:, piece]
            same = doc_row_ref[:, piece] == ends[j]
            pack[0:rows, piece] = cum
            pack[rows : 2 * rows, piece] = jnp.where(
                same, step[:, piece] * jnp.exp2(cum[:, BLOCK - 1 :] - cum), 0.0
            )
        pack[LANES - 1 : LANES, :] = doc_row_ref[...].astype(F32)
        for j in range(count):
            piece = slice(j * BLOCK, (j + 1) * BLOCK)
            turned = pack[:, piece].T
            col_ref[piece, :] = turned
            high, low = two_parts(turned)
            col_parts[piece, 0:LANES] = high
            col_parts[piece, LANES:] = low
        head_lane = lax.broadcasted_iota(jnp.int32, (1, LANES), 1) < heads
        before = jnp.zeros((1, LANES), F32)
        scal[...] = jnp.zeros_like(scal)
        for j in range(count):
            end = jnp.where(head_lane, col_ref[(j + 1) * BLOCK - 1 : (j + 1) * BLOCK, :], 0.0)
            scal[j : j + 1, :] = jnp.where(head_lane, jnp.exp2(end), 0.0)
            scal[count + j : count + j + 1, :] = jnp.where(head_lane, jnp.exp2(before), 0.0)
            before = before + end
        scal[2 * count : 2 * count + 1, :] = jnp.where(head_lane, jnp.exp2(before), 0.0)
        scal[2 * count + 1 : 2 * count + 2, 0:heads] = skip_ref[...]

    hot = hot_ref[...]
    high, low = two_parts(scal[...])
    row = dot(high, hot) + dot(low, hot)
    row_ref[...] = row
    hot_low = jnp.concatenate([hot_low_ref[...]] * 2, axis=0)
    state[...] = jnp.zeros_like(state)
    scaled = (x_ref[...].astype(F32) * dot(col_parts[...], hot_low)).astype(BF16)
    for j in range(count):
        piece = slice(j * BLOCK, (j + 1) * BLOCK)
        prior = docs_ref[max(j * BLOCK - 1, 0)]
        passage = row[j : j + 1, :] * jnp.where(ends[j] == prior, 1.0, 0.0)
        old = state[...]
        enter_ref[j] = old.astype(BF16)
        state[...] = passage * old + dot(inputs_t[:, piece], scaled[piece])

    half = state.shape[0] // 2
    total = row[2 * count : 2 * count + 1, :] * jnp.where(ends[count - 1] == docs_ref[0], 1.0, 0.0)
    mine = pl.multiple_of(sub_ref[0] * half, half)
    theirs = pl.multiple_of((1 - sub_ref[0]) * half, half)
    line = lax.broadcasted_iota(jnp.int32, (8, LANES), 0)
    first, last = docs_ref[0].astype(F32), docs_ref[length - 1].astype(F32)
    for j in range(wide // LANES):
        cols = slice(j * LANES, (j + 1) * LANES)
        foot = jnp.where(line == 0, total[:, cols], jnp.where(line == 1, first, last))
        own_ref[j, 0:half, :] = state[pl.ds(mine, half), cols]
        sent_ref[j, 0:half, :] = state[pl.ds(theirs, half), cols]
        own_ref[j, half:, :] = foot
        sent_ref[j, half:, :] = foot


def prepare_kernel(heads, docs_ref, b_ref, c_ref, col_ref, doc_row_ref, affinity_ref, entry_ref):
    t = lax.broadcasted_iota(jnp.int32, (BLOCK, BLOCK), 0)
    s = lax.broadcasted_iota(jnp.int32, (BLOCK, BLOCK), 1)
    lane = lax.broadcasted_iota(jnp.int32, (1, LANES), 1)
    for j in range(affinity_ref.shape[0]):
        piece = slice(j * BLOCK, (j + 1) * BLOCK)
        block = pl.program_id(0) * affinity_ref.shape[0] + j
        columns = col_ref[piece, :]
        doc_col = columns[:, LANES - 1 :]
        doc_row = doc_row_ref[:, piece].astype(F32)
        affinity_ref[j] = jnp.where(
            (t >= s) & (doc_col == doc_row),
            dot(c_ref[piece, :], b_ref[piece, :], ((1,), (1,))),
            0.0,
        )
        prior_doc = docs_ref[jnp.maximum(block * BLOCK - 1, 0)].astype(F32)
        linked = (doc_col == prior_doc) & (lane < heads)
        high, low = two_parts(jnp.where(linked, jnp.exp2(columns), 0.0))
        entry_ref[piece, 0:LANES] = high
        entry_ref[piece, LANES:] = low


def inner_kernel(
    width,
    first_tile,
    group,
    count,
    live_ref,
    docs_ref,
    x_ref,
    z_ref,
    c_ref,
    g_ref,
    col_ref,
    affinity_ref,
    entry_ref,
    enter_ref,
    row_ref,
    hot_ref,
    *refs,
):
    y_ref, f_ref = refs[-2:]
    k = pl.program_id(0)
    half = BLOCK // 2
    per_tile = LANES // width

    @pl.when(k >= live_ref[0])
    def _():
        y_ref[...] = jnp.zeros_like(y_ref)
        f_ref[...] = jnp.zeros_like(f_ref)

    @pl.when(k < live_ref[0])
    def _():
        readout = c_ref[...]
        lane = lax.broadcasted_iota(jnp.int32, (1, LANES), 1)
        nothing = jnp.zeros((BLOCK, LANES), BF16)
        reaches = jnp.where(docs_ref[jnp.maximum(k * BLOCK - 1, 0)] == docs_ref[0], 1.0, 0.0)
        passed = pick_row(row_ref, count, count, k, slice(None)) * reaches
        for q in range(x_ref.shape[1] // (group * LANES)):
            cols = slice(q * group * LANES, (q + 1) * group * LANES)
            x = x_ref[:, cols]
            tops, bottoms, masked = [], [], []
            for u in range(group):
                part = x[:, u * LANES : (u + 1) * LANES]
                for i in range(per_tile):
                    h = (first_tile + q * group + u) * per_tile + i
                    cum = jnp.broadcast_to(col_ref[:, h : h + 1], (BLOCK, LANES))
                    left, right = g_ref[h : h + 1, :half], g_ref[h : h + 1, half:]
                    top = jnp.exp2(jnp.minimum(cum[:half] - left, 64.0))
                    bottom = jnp.exp2(cum[half:] - left)
                    corner = jnp.exp2(jnp.minimum(cum[half:] - right, 64.0))
                    tops.append((top * affinity_ref[0, :half, :half]).astype(BF16))
                    bottoms.append((bottom * affinity_ref[0, half:, :half]).astype(BF16))
                    bottoms.append((corner * affinity_ref[0, half:, half:]).astype(BF16))
                    mine = (lane >= i * width) & (lane < (i + 1) * width)
                    kept = part * jnp.where(mine, 1.0, 0.0).astype(BF16)
                    masked.append(
                        jnp.concatenate(
                            [kept if v == u else nothing for v in range(group)], axis=1
                        )
                    )
            upper = dot(
                jnp.concatenate(tops, axis=1),
                jnp.concatenate([m[:half] for m in masked], axis=0),
            )
            lower = dot(jnp.concatenate(bottoms, axis=1), jnp.concatenate(masked, axis=0))
            hot = jnp.concatenate([hot_ref[:, cols]] * 2, axis=0)
            enter = dot(entry_ref[...], hot)
            outer = dot(readout, enter_ref[0, :, cols])
            skip = row_ref[2 * count + 1 : 2 * count + 2, cols]
            y = jnp.concatenate([upper, lower], axis=0) + enter * outer + skip * x.astype(F32)
            z = z_ref[:, cols].astype(F32)
            gate = z / (1.0 + jnp.exp2(-LOG2E * z))
            y_ref[:, cols] = y * gate
            f_ref[:, cols] = (enter * gate * passed[:, cols]).astype(BF16)


def join_kernel(sub_ref, own_ref, other_ref, c_ref, *refs):
    pieces = (len(refs) - 3) // 2
    gated_ref, square_ref, total = refs[2 * pieces :]
    length = c_ref.shape[0]
    second = sub_ref[0] == 1
    total[...] = jnp.zeros_like(total)
    tile = 0
    for y_ref, f_ref in zip(refs[:pieces], refs[pieces : 2 * pieces]):
        wide = chunk_of(y_ref.shape[1], 4 * LANES)
        for c in range(0, y_ref.shape[1], wide):
            parts = []
            for j in range(tile, tile + wide // LANES):
                own, other = own_ref[j].astype(BF16), other_ref[j].astype(BF16)
                parts.append(
                    jnp.concatenate(
                        [jnp.where(second, other, own), jnp.where(second, own, other)], axis=0
                    )
                )
            carry = jnp.concatenate(parts, axis=1)
            for r in range(0, length, BLOCK):
                rows = slice(r, r + BLOCK)
                outer = dot(c_ref[rows, :], carry)
                gated = y_ref[rows, c : c + wide] + f_ref[rows, c : c + wide].astype(F32) * outer
                gated_ref[rows, tile * LANES : tile * LANES + wide] = gated
                square = total[rows, :]
                for j in range(0, wide, LANES):
                    square = square + gated[:, j : j + LANES] * gated[:, j : j + LANES]
                total[rows, :] = square
            tile += wide // LANES
    square_ref[...] = jnp.sum(total[...].T, axis=0, keepdims=True)


def norm_kernel(channels_all, square_ref, more_ref, gain_ref, gated_ref, out_ref):
    rows = out_ref.shape[0]
    start = pl.multiple_of(pl.program_id(0) * rows, rows)
    scale = lax.rsqrt((square_ref[...] + more_ref[...]) / channels_all + 1e-05)
    scale = jnp.broadcast_to(scale, (LANES, rows)).T
    for j in range(gated_ref.shape[1] // LANES):
        cols = slice(j * LANES, (j + 1) * LANES)
        gated = gated_ref[pl.ds(start, rows), cols]
        out_ref[:, cols] = (gated * gain_ref[:, cols] * scale).astype(BF16)


def chunk_of(total, most):
    wide = most
    while total % wide:
        wide -= LANES
    return wide


def whole(shape):
    return pl.BlockSpec(shape, lambda k, *_: (0,) * len(shape))


SMEM = pl.BlockSpec(memory_space=pltpu.SMEM)
VMEM = pl.BlockSpec(memory_space=pltpu.VMEM)


def plan(chips, tiles):
    chunks = 2 if tiles % 2 == 0 else 1
    pieces = (tiles,)
    if tiles % 10 == 0:
        pieces = (3 * tiles // 10,) * 2 + (tiles // 5,) * 2
    return chunks, chunks + chips - 2, pieces


def on_device(
    token_values,
    gate_values,
    state_input,
    state_readout,
    step_raw,
    step_bias,
    decay_log,
    skip_gain,
    norm_gain,
    document_ids,
    live_blocks,
):
    length, channels = token_values.shape
    heads = step_raw.shape[0]
    width = channels // heads
    states = state_input.shape[1]
    half = states // 2
    count = length // BLOCK
    tiles = channels // LANES
    rows = -(-heads // 8) * 8
    scalars = -(-(2 * count + 2) // 16) * 16
    assert lax.axis_size("sub") == 2 and 2 * rows < LANES and states == LANES

    raw = step_raw
    if rows != heads:
        raw = jnp.pad(raw, ((0, rows - heads), (0, 0)))
    doc_row = document_ids.reshape(1, length)
    sub = lax.axis_index("sub").astype(jnp.int32).reshape(1)
    head_of = np.arange(channels)[None, :] // width
    lanes = np.arange(LANES)[:, None]
    hot = jnp.asarray(lanes == head_of, dtype=BF16)
    hot_low = jnp.asarray(lanes == head_of + rows, dtype=BF16)
    tri = jnp.asarray(np.triu(np.ones((BLOCK, BLOCK))), dtype=BF16)

    chunk = chunk_of(channels, 512)
    per_chunk = chunk // LANES
    g, col, enter, own, sent, row = pl.pallas_call(
        functools.partial(state_kernel, heads),
        grid=(channels // chunk,),
        in_specs=[
            SMEM,
            SMEM,
            SMEM,
            whole((rows, length)),
            whole((1, heads)),
            whole((1, heads)),
            whole((1, heads)),
            whole((1, length)),
            whole((BLOCK, BLOCK)),
            pl.BlockSpec((LANES, chunk), lambda c: (0, c)),
            pl.BlockSpec((LANES, chunk), lambda c: (0, c)),
            pl.BlockSpec((length, chunk), lambda c: (0, c)),
            whole((length, states)),
        ],
        out_specs=[
            whole((rows, length)),
            whole((length, LANES)),
            pl.BlockSpec((count, states, chunk), lambda c: (0, 0, c)),
            pl.BlockSpec((per_chunk, half + 8, LANES), lambda c: (c, 0, 0)),
            pl.BlockSpec((per_chunk, half + 8, LANES), lambda c: (c, 0, 0)),
            pl.BlockSpec((scalars, chunk), lambda c: (0, c)),
        ],
        out_shape=[
            jax.ShapeDtypeStruct((rows, length), F32),
            jax.ShapeDtypeStruct((length, LANES), F32),
            jax.ShapeDtypeStruct((count, states, channels), BF16),
            jax.ShapeDtypeStruct((tiles, half + 8, LANES), F32),
            jax.ShapeDtypeStruct((tiles, half + 8, LANES), F32),
            jax.ShapeDtypeStruct((scalars, channels), F32),
        ],
        scratch_shapes=[
            pltpu.VMEM((LANES, length), F32),
            pltpu.VMEM((length, 2 * LANES), BF16),
            pltpu.VMEM((states, length), BF16),
            pltpu.VMEM((states, chunk), F32),
            pltpu.VMEM((scalars, LANES), F32),
        ],
        name="shard_state",
    )(
        live_blocks,
        document_ids,
        sub,
        raw,
        step_bias.reshape(1, heads),
        decay_log.reshape(1, heads),
        skip_gain.reshape(1, heads),
        doc_row,
        tri,
        hot,
        hot_low,
        token_values,
        state_input,
    )

    span = 2 if count % 2 == 0 else 1
    affinity, entry = pl.pallas_call(
        functools.partial(prepare_kernel, heads),
        grid=(count // span,),
        in_specs=[
            SMEM,
            pl.BlockSpec((span * BLOCK, states), lambda k: (k, 0)),
            pl.BlockSpec((span * BLOCK, states), lambda k: (k, 0)),
            pl.BlockSpec((span * BLOCK, LANES), lambda k: (k, 0)),
            pl.BlockSpec((1, span * BLOCK), lambda k: (0, k)),
        ],
        out_specs=[
            pl.BlockSpec((span, BLOCK, BLOCK), lambda k: (k, 0, 0)),
            pl.BlockSpec((span * BLOCK, 2 * LANES), lambda k: (k, 0)),
        ],
        out_shape=[
            jax.ShapeDtypeStruct((count, BLOCK, BLOCK), F32),
            jax.ShapeDtypeStruct((length, 2 * LANES), BF16),
        ],
        name="prepare",
    )(document_ids, state_input, state_readout, col, doc_row)

    pieces = plan(lax.axis_size("seq"), tiles)[2]
    group = 2 if tiles % 2 == 0 else 1
    ys, fs, at = [], [], 0
    inputs = [
        pltpu.with_memory_space_constraint(value, pltpu.HBM)
        for value in (
            token_values,
            gate_values,
            state_readout,
            g,
            col,
            affinity,
            entry,
            enter,
            row,
            hot,
        )
    ]
    for size in pieces:
        wide, first = size * LANES, at // size
        y, f = pl.pallas_call(
            functools.partial(inner_kernel, width, at, group, count),
            grid=(count,),
            in_specs=[
                SMEM,
                SMEM,
                pl.BlockSpec((BLOCK, wide), lambda k, q=first: (k, q)),
                pl.BlockSpec((BLOCK, wide), lambda k, q=first: (k, q)),
                pl.BlockSpec((BLOCK, states), lambda k: (k, 0)),
                pl.BlockSpec((rows, BLOCK), lambda k: (0, k)),
                pl.BlockSpec((BLOCK, LANES), lambda k: (k, 0)),
                pl.BlockSpec((1, BLOCK, BLOCK), lambda k: (k, 0, 0)),
                pl.BlockSpec((BLOCK, 2 * LANES), lambda k: (k, 0)),
                pl.BlockSpec((1, states, wide), lambda k, q=first: (k, 0, q)),
                pl.BlockSpec((scalars, wide), lambda k, q=first: (0, q)),
                pl.BlockSpec((LANES, wide), lambda k, q=first: (0, q)),
            ],
            out_specs=[pl.BlockSpec((BLOCK, wide), lambda k: (k, 0))] * 2,
            out_shape=[
                jax.ShapeDtypeStruct((length, wide), F32),
                jax.ShapeDtypeStruct((length, wide), BF16),
            ],
            cost_estimate=pl.CostEstimate(
                flops=length * wide * 1200,
                bytes_accessed=length * wide * 10,
                transcendentals=0,
            ),
            compiler_params=pltpu.CompilerParams(vmem_limit_bytes=INNER_VMEM),
        )(live_blocks, document_ids, *inputs)
        ys.append(y)
        fs.append(f)
        at += size

    own, other = carry_in(own, sent, half)

    gated, squares = pl.pallas_call(
        join_kernel,
        in_specs=[SMEM] + [VMEM] * (3 + 2 * len(pieces)),
        out_specs=[VMEM, VMEM],
        out_shape=[
            jax.ShapeDtypeStruct((length, channels), F32),
            jax.ShapeDtypeStruct((1, length), F32),
        ],
        scratch_shapes=[pltpu.VMEM((length, LANES), F32)],
        compiler_params=pltpu.CompilerParams(vmem_limit_bytes=16 << 20),
        name="join",
    )(sub, own, other, state_readout, *ys, *fs)

    squares, more = summed(squares, "head")
    return pl.pallas_call(
        functools.partial(norm_kernel, channels * lax.axis_size("head")),
        grid=(count,),
        in_specs=[
            pl.BlockSpec((1, BLOCK), lambda k: (0, k)),
            pl.BlockSpec((1, BLOCK), lambda k: (0, k)),
            whole((1, channels)),
            VMEM,
        ],
        out_specs=pl.BlockSpec((BLOCK, channels), lambda k: (k, 0)),
        out_shape=jax.ShapeDtypeStruct((length, channels), BF16),
        compiler_params=pltpu.CompilerParams(vmem_limit_bytes=16 << 20),
        name="norm",
    )(squares, more, norm_gain.reshape(1, channels), gated)


def summed(value, axis):
    size = lax.axis_size(axis)
    if size & (size - 1):
        total = value
        for shift in range(1, size):
            total = total + lax.ppermute(value, axis, [(i, (i + shift) % size) for i in range(size)])
        return total, jnp.zeros_like(value)
    more, shift = jnp.zeros_like(value), 1
    while shift < size:
        value = value + more if shift > 1 else value
        more = lax.ppermute(value, axis, [(i, i ^ shift) for i in range(size)])
        shift *= 2
    return value, more


def carry_in(own, sent, half):
    tiles = own.shape[0]
    second = lax.axis_index("sub") == 1
    place, chips = lax.axis_index("seq"), lax.axis_size("seq")
    got = lax.ppermute(sent, "sub", [(0, 1), (1, 0)])
    early = jnp.where(second, got, own)
    late = jnp.where(second, own, got)
    first, last = early[0, half + 1], late[0, half + 2]
    link = jnp.where(early[0, half + 2] == late[0, half + 1], 1.0, 0.0)
    early_decay, late_decay = early[:, half : half + 1], late[:, half : half + 1] * link
    early, late = early[:, :half], late[:, :half]
    chip_state = late_decay * early + late
    chip_decay = late_decay * early_decay

    chunks, hops = plan(chips, tiles)[:2]
    size = tiles // chunks
    rows = size * half
    tail = jnp.broadcast_to(last, (8, LANES))

    def at(array, index):
        return lax.dynamic_slice_in_dim(array, index * size, size, 0)

    carry = jnp.zeros((size, half, LANES), F32)
    received = []
    for t in range(hops):
        index = jnp.clip(t - place, 0, chunks - 1)
        send = at(chip_decay, index) * carry + at(chip_state, index)
        send = jnp.concatenate([send.reshape(rows, LANES), tail], axis=0)
        pairs = [(z, z + 1) for z in range(chips - 1) if 0 <= t - z < chunks]
        got = lax.ppermute(send, "seq", pairs)
        joined = jnp.where(got[rows : rows + 1] == first, 1.0, 0.0)
        carry = joined[None] * got[:rows].reshape(size, half, LANES)
        received.append(carry)
    parts = []
    for c in range(chunks):
        part = jnp.zeros((size, half, LANES), F32)
        for z in range(1, chips):
            part = jnp.where(place == z, received[c + z - 1], part)
        parts.append(part)
    entering = jnp.concatenate(parts, axis=0)
    onward = link * (early_decay * entering + early)
    mine = jnp.where(second, onward, entering)
    other = lax.ppermute(jnp.where(second, entering, onward), "sub", [(0, 1), (1, 0)])
    return mine, other


def solution(mesh):
    placed = (
        P(("groups", "seq", "sub"), "head"),
        P(("groups", "seq", "sub"), "head"),
        P(("groups", "seq", "sub"), None),
        P(("groups", "seq", "sub"), None),
        P("head", ("seq", "sub")),
        P("head"),
        P("head"),
        P("head"),
        P("head"),
        P(("groups", "seq", "sub")),
        P(("groups", "seq", "sub")),
    )

    return jax.shard_map(
        on_device,
        mesh=mesh,
        in_specs=placed,
        out_specs=P(("groups", "seq", "sub"), "head"),
        check_vma=False,
    )
```

```python
import functools
import math

import jax
import jax.numpy as jnp
import numpy as np
from jax import lax
from jax.experimental import pallas as pl
from jax.experimental.pallas import tpu as pltpu
from jax.sharding import PartitionSpec as P

BLOCK = 256
LANES = 128
LOG2E = math.log2(math.e)
INNER_VMEM = 24 << 20
EARLY_VMEM = 32 << 20
F32 = jnp.float32
BF16 = jnp.bfloat16


def dot(a, b, contract=((1,), (0,))):
    return lax.dot_general(a, b, (contract, ((), ())), preferred_element_type=F32)


def two_parts(value):
    high = value.astype(BF16)
    low = (value - high.astype(F32)).astype(BF16)
    return high, low


def pick_row(ref, base, count, k, cols):
    row = ref[base : base + 1, cols]
    for j in range(1, count):
        row = jnp.where(k == j, ref[base + j : base + j + 1, cols], row)
    return row


def softplus(v):
    u = jnp.exp(-jnp.abs(v))
    s = u / (2.0 + u)
    q = s * s
    series = jnp.full_like(q, 1.0 / 15.0)
    for odd in (13, 11, 9, 7, 5, 3, 1):
        series = series * q + 1.0 / odd
    return jnp.maximum(v, 0.0) + 2.0 * s * series


def state_kernel(
    heads,
    live_ref,
    docs_ref,
    spot_ref,
    raw_ref,
    bias_ref,
    decay_ref,
    skip_ref,
    doc_row_ref,
    tri_ref,
    hot_ref,
    hot_low_ref,
    x_ref,
    b_ref,
    g_ref,
    col_ref,
    enter_ref,
    own_ref,
    sent_ref,
    row_ref,
    pack,
    col_parts,
    inputs_t,
    state,
    scal,
):
    length = raw_ref.shape[0 + 1]
    rows = raw_ref.shape[0]
    count = length // BLOCK
    wide = x_ref.shape[1]
    ends = [docs_ref[j * BLOCK + BLOCK - 1] for j in range(count)]

    @pl.when(pl.program_id(0) == 0)
    def _():
        inputs_t[...] = b_ref[...].T
        pack[...] = jnp.zeros_like(pack)
        pack[0:1, 0:heads] = bias_ref[...]
        pack[1:2, 0:heads] = decay_ref[...]
        params = pack[0:LANES, 0:LANES].T
        lane = lax.broadcasted_iota(jnp.int32, (1, length), 1)
        step = softplus(raw_ref[...] + params[0:rows, 0:1])
        step = jnp.where(lane < live_ref[0] * BLOCK, step, 0.0)
        rate = (-LOG2E * jnp.exp(params[0:rows, 1:2])) * step
        high, _ = two_parts(rate)
        middle, low = two_parts(rate - high.astype(F32))
        tri = tri_ref[...]
        logs = jnp.where(step > 0.0, LOG2E * jnp.log(step), -1e30)
        for j in range(count):
            piece = slice(j * BLOCK, (j + 1) * BLOCK)
            cum = dot(high[:, piece], tri) + (dot(middle[:, piece], tri) + dot(low[:, piece], tri))
            g_ref[:, piece] = cum - logs[:, piece]
            same = doc_row_ref[:, piece] == ends[j]
            pack[0:rows, piece] = cum
            pack[rows : 2 * rows, piece] = jnp.where(
                same, step[:, piece] * jnp.exp2(cum[:, BLOCK - 1 :] - cum), 0.0
            )
        pack[LANES - 1 : LANES, :] = doc_row_ref[...].astype(F32)
        for j in range(count):
            piece = slice(j * BLOCK, (j + 1) * BLOCK)
            turned = pack[:, piece].T
            col_ref[piece, :] = turned
            high, low = two_parts(turned)
            col_parts[piece, 0:LANES] = high
            col_parts[piece, LANES:] = low
        head_lane = lax.broadcasted_iota(jnp.int32, (1, LANES), 1) < heads
        before = jnp.zeros((1, LANES), F32)
        scal[...] = jnp.zeros_like(scal)
        for j in range(count):
            end = jnp.where(head_lane, col_ref[(j + 1) * BLOCK - 1 : (j + 1) * BLOCK, :], 0.0)
            scal[j : j + 1, :] = jnp.where(head_lane, jnp.exp2(end), 0.0)
            scal[count + j : count + j + 1, :] = jnp.where(head_lane, jnp.exp2(before), 0.0)
            before = before + end
        scal[2 * count : 2 * count + 1, :] = jnp.where(head_lane, jnp.exp2(before), 0.0)
        scal[2 * count + 1 : 2 * count + 2, 0:heads] = skip_ref[...]

    hot = hot_ref[...]
    high, low = two_parts(scal[...])
    row = dot(high, hot) + dot(low, hot)
    row_ref[...] = row
    hot_low = jnp.concatenate([hot_low_ref[...]] * 2, axis=0)
    state[...] = jnp.zeros_like(state)
    scaled = (x_ref[...].astype(F32) * dot(col_parts[...], hot_low)).astype(BF16)
    for j in range(count):
        piece = slice(j * BLOCK, (j + 1) * BLOCK)
        prior = docs_ref[max(j * BLOCK - 1, 0)]
        passage = row[j : j + 1, :] * jnp.where(ends[j] == prior, 1.0, 0.0)
        old = state[...]
        enter_ref[j] = old.astype(BF16)
        state[...] = passage * old + dot(inputs_t[:, piece], scaled[piece])

    half = state.shape[0] // 2
    total = row[2 * count : 2 * count + 1, :] * jnp.where(ends[count - 1] == docs_ref[0], 1.0, 0.0)
    mine = pl.multiple_of(spot_ref[0] * half, half)
    theirs = pl.multiple_of((1 - spot_ref[0]) * half, half)
    line = lax.broadcasted_iota(jnp.int32, (8, LANES), 0)
    marks = jnp.zeros((8, LANES), F32)
    for at, mark in enumerate((docs_ref[0], docs_ref[length - 1], spot_ref[0], spot_ref[1])):
        marks = jnp.where(line == at + 1, mark.astype(F32), marks)
    for j in range(wide // LANES):
        cols = slice(j * LANES, (j + 1) * LANES)
        foot = jnp.where(line == 0, total[:, cols], marks)
        own_ref[j, 0:half, :] = state[pl.ds(mine, half), cols]
        sent_ref[j, 0:half, :] = state[pl.ds(theirs, half), cols]
        own_ref[j, half:, :] = foot
        sent_ref[j, half:, :] = foot


def prepare_kernel(heads, docs_ref, b_ref, c_ref, col_ref, doc_row_ref, affinity_ref, entry_ref):
    t = lax.broadcasted_iota(jnp.int32, (BLOCK, BLOCK), 0)
    s = lax.broadcasted_iota(jnp.int32, (BLOCK, BLOCK), 1)
    lane = lax.broadcasted_iota(jnp.int32, (1, LANES), 1)
    for j in range(affinity_ref.shape[0]):
        piece = slice(j * BLOCK, (j + 1) * BLOCK)
        block = pl.program_id(0) * affinity_ref.shape[0] + j
        columns = col_ref[piece, :]
        doc_col = columns[:, LANES - 1 :]
        doc_row = doc_row_ref[:, piece].astype(F32)
        affinity_ref[j] = jnp.where(
            (t >= s) & (doc_col == doc_row),
            dot(c_ref[piece, :], b_ref[piece, :], ((1,), (1,))),
            0.0,
        )
        prior_doc = docs_ref[jnp.maximum(block * BLOCK - 1, 0)].astype(F32)
        linked = (doc_col == prior_doc) & (lane < heads)
        high, low = two_parts(jnp.where(linked, jnp.exp2(columns), 0.0))
        entry_ref[piece, 0:LANES] = high
        entry_ref[piece, LANES:] = low


def inner_kernel(
    width,
    first_tile,
    group,
    count,
    live_ref,
    docs_ref,
    x_ref,
    z_ref,
    c_ref,
    g_ref,
    col_ref,
    affinity_ref,
    entry_ref,
    enter_ref,
    row_ref,
    hot_ref,
    *refs,
):
    y_ref, f_ref = refs[-2:]
    k = pl.program_id(0)
    half = BLOCK // 2
    per_tile = LANES // width

    @pl.when(k >= live_ref[0])
    def _():
        y_ref[...] = jnp.zeros_like(y_ref)
        f_ref[...] = jnp.zeros_like(f_ref)

    @pl.when(k < live_ref[0])
    def _():
        readout = c_ref[...]
        lane = lax.broadcasted_iota(jnp.int32, (1, LANES), 1)
        nothing = jnp.zeros((BLOCK, LANES), BF16)
        reaches = jnp.where(docs_ref[jnp.maximum(k * BLOCK - 1, 0)] == docs_ref[0], 1.0, 0.0)
        passed = pick_row(row_ref, count, count, k, slice(None)) * reaches
        for q in range(x_ref.shape[1] // (group * LANES)):
            cols = slice(q * group * LANES, (q + 1) * group * LANES)
            x = x_ref[:, cols]
            tops, bottoms, masked = [], [], []
            for u in range(group):
                part = x[:, u * LANES : (u + 1) * LANES]
                for i in range(per_tile):
                    h = (first_tile + q * group + u) * per_tile + i
                    cum = jnp.broadcast_to(col_ref[:, h : h + 1], (BLOCK, LANES))
                    left, right = g_ref[h : h + 1, :half], g_ref[h : h + 1, half:]
                    top = jnp.exp2(jnp.minimum(cum[:half] - left, 64.0))
                    bottom = jnp.exp2(cum[half:] - left)
                    corner = jnp.exp2(jnp.minimum(cum[half:] - right, 64.0))
                    tops.append((top * affinity_ref[0, :half, :half]).astype(BF16))
                    bottoms.append((bottom * affinity_ref[0, half:, :half]).astype(BF16))
                    bottoms.append((corner * affinity_ref[0, half:, half:]).astype(BF16))
                    mine = (lane >= i * width) & (lane < (i + 1) * width)
                    kept = part * jnp.where(mine, 1.0, 0.0).astype(BF16)
                    masked.append(
                        jnp.concatenate(
                            [kept if v == u else nothing for v in range(group)], axis=1
                        )
                    )
            upper = dot(
                jnp.concatenate(tops, axis=1),
                jnp.concatenate([m[:half] for m in masked], axis=0),
            )
            lower = dot(jnp.concatenate(bottoms, axis=1), jnp.concatenate(masked, axis=0))
            hot = jnp.concatenate([hot_ref[:, cols]] * 2, axis=0)
            enter = dot(entry_ref[...], hot)
            outer = dot(readout, enter_ref[0, :, cols])
            skip = row_ref[2 * count + 1 : 2 * count + 2, cols]
            y = jnp.concatenate([upper, lower], axis=0) + enter * outer + skip * x.astype(F32)
            z = z_ref[:, cols].astype(F32)
            gate = z / (1.0 + jnp.exp2(-LOG2E * z))
            y_ref[:, cols] = y * gate
            f_ref[:, cols] = (enter * gate * passed[:, cols]).astype(BF16)


def join_kernel(spot_ref, own_ref, other_ref, c_ref, *refs):
    pieces = (len(refs) - 3) // 2
    gated_ref, square_ref, total = refs[2 * pieces :]
    length = c_ref.shape[0]
    second = spot_ref[0] == 1
    total[...] = jnp.zeros_like(total)
    tile = 0
    for y_ref, f_ref in zip(refs[:pieces], refs[pieces : 2 * pieces]):
        wide = chunk_of(y_ref.shape[1], 4 * LANES)
        for c in range(0, y_ref.shape[1], wide):
            parts = []
            for j in range(tile, tile + wide // LANES):
                own, other = own_ref[j].astype(BF16), other_ref[j].astype(BF16)
                parts.append(
                    jnp.concatenate(
                        [jnp.where(second, other, own), jnp.where(second, own, other)], axis=0
                    )
                )
            carry = jnp.concatenate(parts, axis=1)
            for r in range(0, length, BLOCK):
                rows = slice(r, r + BLOCK)
                outer = dot(c_ref[rows, :], carry)
                gated = y_ref[rows, c : c + wide] + f_ref[rows, c : c + wide].astype(F32) * outer
                gated_ref[rows, tile * LANES : tile * LANES + wide] = gated
                square = total[rows, :]
                for j in range(0, wide, LANES):
                    square = square + gated[:, j : j + LANES] * gated[:, j : j + LANES]
                total[rows, :] = square
            tile += wide // LANES
    square_ref[...] = jnp.sum(total[...].T, axis=0, keepdims=True)


def norm_kernel(channels_all, square_ref, more_ref, gain_ref, gated_ref, out_ref, scale):
    rows = out_ref.shape[0]
    start = pl.multiple_of(pl.program_id(0) * rows, rows)
    row = lax.rsqrt((square_ref[...] + more_ref[...]) / channels_all + 1e-05)
    scale[...] = jnp.broadcast_to(row, (LANES, rows)).T

    def strip(i, rest):
        at = pl.multiple_of(i * 32, 32)
        part = scale[pl.ds(at, 32), :]
        for j in range(gated_ref.shape[1] // LANES):
            cols = slice(j * LANES, (j + 1) * LANES)
            gated = gated_ref[pl.ds(start + at, 32), cols]
            out_ref[pl.ds(at, 32), cols] = (gated * gain_ref[:, cols] * part).astype(BF16)
        return rest

    lax.fori_loop(0, rows // 32, strip, 0)


def chunk_of(total, most):
    wide = most
    while total % wide:
        wide -= LANES
    return wide


def whole(shape):
    return pl.BlockSpec(shape, lambda k, *_: (0,) * len(shape))


def in_hbm(*values):
    return [pltpu.with_memory_space_constraint(value, pltpu.HBM) for value in values]


SMEM = pl.BlockSpec(memory_space=pltpu.SMEM)
VMEM = pl.BlockSpec(memory_space=pltpu.VMEM)


def plan(chips, tiles):
    chunks = 2 if tiles % 2 == 0 else 1
    pieces = (tiles,)
    if tiles % 10 == 0:
        pieces = (3 * tiles // 10,) * 2 + (tiles // 5,) * 2
    return chunks, chunks + chips - 2, pieces


def on_device(
    token_values,
    gate_values,
    state_input,
    state_readout,
    step_raw,
    step_bias,
    decay_log,
    skip_gain,
    norm_gain,
    document_ids,
    live_blocks,
):
    length, channels = token_values.shape
    heads = step_raw.shape[0]
    width = channels // heads
    states = state_input.shape[1]
    half = states // 2
    count = length // BLOCK
    tiles = channels // LANES
    rows = -(-heads // 8) * 8
    scalars = -(-(2 * count + 2) // 16) * 16
    assert lax.axis_size("sub") == 2 and 2 * rows < LANES and states == LANES

    raw = step_raw
    if rows != heads:
        raw = jnp.pad(raw, ((0, rows - heads), (0, 0)))
    doc_row = document_ids.reshape(1, length)
    spot = jnp.stack([lax.axis_index("sub"), lax.axis_index("seq")]).astype(jnp.int32)
    head_of = np.arange(channels)[None, :] // width
    lanes = np.arange(LANES)[:, None]
    hot = jnp.asarray(lanes == head_of, dtype=BF16)
    hot_low = jnp.asarray(lanes == head_of + rows, dtype=BF16)
    tri = jnp.asarray(np.triu(np.ones((BLOCK, BLOCK))), dtype=BF16)

    chunk = chunk_of(channels, 512)
    per_chunk = chunk // LANES
    g, col, enter, own, sent, row = pl.pallas_call(
        functools.partial(state_kernel, heads),
        grid=(channels // chunk,),
        in_specs=[
            SMEM,
            SMEM,
            SMEM,
            whole((rows, length)),
            whole((1, heads)),
            whole((1, heads)),
            whole((1, heads)),
            whole((1, length)),
            whole((BLOCK, BLOCK)),
            pl.BlockSpec((LANES, chunk), lambda c: (0, c)),
            pl.BlockSpec((LANES, chunk), lambda c: (0, c)),
            pl.BlockSpec((length, chunk), lambda c: (0, c)),
            whole((length, states)),
        ],
        out_specs=[
            whole((rows, length)),
            whole((length, LANES)),
            pl.BlockSpec((count, states, chunk), lambda c: (0, 0, c)),
            pl.BlockSpec((per_chunk, half + 8, LANES), lambda c: (c, 0, 0)),
            pl.BlockSpec((per_chunk, half + 8, LANES), lambda c: (c, 0, 0)),
            pl.BlockSpec((scalars, chunk), lambda c: (0, c)),
        ],
        out_shape=[
            jax.ShapeDtypeStruct((rows, length), F32),
            jax.ShapeDtypeStruct((length, LANES), F32),
            jax.ShapeDtypeStruct((count, states, channels), BF16),
            jax.ShapeDtypeStruct((tiles, half + 8, LANES), F32),
            jax.ShapeDtypeStruct((tiles, half + 8, LANES), F32),
            jax.ShapeDtypeStruct((scalars, channels), F32),
        ],
        scratch_shapes=[
            pltpu.VMEM((LANES, length), F32),
            pltpu.VMEM((length, 2 * LANES), BF16),
            pltpu.VMEM((states, length), BF16),
            pltpu.VMEM((states, chunk), F32),
            pltpu.VMEM((scalars, LANES), F32),
        ],
        compiler_params=pltpu.CompilerParams(vmem_limit_bytes=EARLY_VMEM),
        name="shard_state",
    )(
        live_blocks,
        document_ids,
        spot,
        *in_hbm(
            raw,
            step_bias.reshape(1, heads),
            decay_log.reshape(1, heads),
            skip_gain.reshape(1, heads),
            doc_row,
            tri,
            hot,
            hot_low,
            token_values,
            state_input,
        ),
    )

    span = 2 if count % 2 == 0 else 1
    affinity, entry = pl.pallas_call(
        functools.partial(prepare_kernel, heads),
        grid=(count // span,),
        in_specs=[
            SMEM,
            pl.BlockSpec((span * BLOCK, states), lambda k: (k, 0)),
            pl.BlockSpec((span * BLOCK, states), lambda k: (k, 0)),
            pl.BlockSpec((span * BLOCK, LANES), lambda k: (k, 0)),
            pl.BlockSpec((1, span * BLOCK), lambda k: (0, k)),
        ],
        out_specs=[
            pl.BlockSpec((span, BLOCK, BLOCK), lambda k: (k, 0, 0)),
            pl.BlockSpec((span * BLOCK, 2 * LANES), lambda k: (k, 0)),
        ],
        out_shape=[
            jax.ShapeDtypeStruct((count, BLOCK, BLOCK), F32),
            jax.ShapeDtypeStruct((length, 2 * LANES), BF16),
        ],
        compiler_params=pltpu.CompilerParams(vmem_limit_bytes=EARLY_VMEM),
        name="prepare",
    )(document_ids, *in_hbm(state_input, state_readout), col, doc_row)

    pieces = plan(lax.axis_size("seq"), tiles)[2]
    group = 2 if tiles % 2 == 0 else 1
    ys, fs, at = [], [], 0
    x, z, readout, heads_hot = in_hbm(token_values, gate_values, state_readout, hot)
    inputs = (x, z, readout, g, col, affinity, entry, enter, row, heads_hot)
    for size in pieces:
        wide, first = size * LANES, at // size
        y, f = pl.pallas_call(
            functools.partial(inner_kernel, width, at, group, count),
            grid=(count,),
            in_specs=[
                SMEM,
                SMEM,
                pl.BlockSpec((BLOCK, wide), lambda k, q=first: (k, q)),
                pl.BlockSpec((BLOCK, wide), lambda k, q=first: (k, q)),
                pl.BlockSpec((BLOCK, states), lambda k: (k, 0)),
                pl.BlockSpec((rows, BLOCK), lambda k: (0, k)),
                pl.BlockSpec((BLOCK, LANES), lambda k: (k, 0)),
                pl.BlockSpec((1, BLOCK, BLOCK), lambda k: (k, 0, 0)),
                pl.BlockSpec((BLOCK, 2 * LANES), lambda k: (k, 0)),
                pl.BlockSpec((1, states, wide), lambda k, q=first: (k, 0, q)),
                pl.BlockSpec((scalars, wide), lambda k, q=first: (0, q)),
                pl.BlockSpec((LANES, wide), lambda k, q=first: (0, q)),
            ],
            out_specs=[pl.BlockSpec((BLOCK, wide), lambda k: (k, 0))] * 2,
            out_shape=[
                jax.ShapeDtypeStruct((length, wide), F32),
                jax.ShapeDtypeStruct((length, wide), BF16),
            ],
            cost_estimate=pl.CostEstimate(
                flops=length * wide * 1200,
                bytes_accessed=length * wide * 10,
                transcendentals=0,
            ),
            compiler_params=pltpu.CompilerParams(vmem_limit_bytes=INNER_VMEM),
        )(live_blocks, document_ids, *inputs)
        ys.append(y)
        fs.append(f)
        at += size

    own, other = carry_in(own, sent, half)

    gated, squares = pl.pallas_call(
        join_kernel,
        in_specs=[SMEM] + [VMEM] * (3 + 2 * len(pieces)),
        out_specs=[VMEM, VMEM],
        out_shape=[
            jax.ShapeDtypeStruct((length, channels), F32),
            jax.ShapeDtypeStruct((1, length), F32),
        ],
        scratch_shapes=[pltpu.VMEM((length, LANES), F32)],
        compiler_params=pltpu.CompilerParams(vmem_limit_bytes=16 << 20),
        name="join",
    )(spot, own, other, state_readout, *ys, *fs)

    squares, more = summed(squares, "head")
    return pl.pallas_call(
        functools.partial(norm_kernel, channels * lax.axis_size("head")),
        grid=(count,),
        in_specs=[
            pl.BlockSpec((1, BLOCK), lambda k: (0, k)),
            pl.BlockSpec((1, BLOCK), lambda k: (0, k)),
            whole((1, channels)),
            VMEM,
        ],
        out_specs=pl.BlockSpec((BLOCK, channels), lambda k: (k, 0)),
        out_shape=jax.ShapeDtypeStruct((length, channels), BF16),
        scratch_shapes=[pltpu.VMEM((BLOCK, LANES), F32)],
        compiler_params=pltpu.CompilerParams(vmem_limit_bytes=16 << 20),
        name="norm",
    )(squares, more, norm_gain.reshape(1, channels), gated)


def summed(value, axis):
    size = lax.axis_size(axis)
    if size & (size - 1):
        total = value
        for shift in range(1, size):
            total = total + lax.ppermute(value, axis, [(i, (i + shift) % size) for i in range(size)])
        return total, jnp.zeros_like(value)
    more, shift = jnp.zeros_like(value), 1
    while shift < size:
        value = value + more if shift > 1 else value
        more = lax.ppermute(value, axis, [(i, i ^ shift) for i in range(size)])
        shift *= 2
    return value, more


def carry_in(own, sent, half):
    tiles = own.shape[0]
    chips = lax.axis_size("seq")
    second, place = own[0, half + 3] == 1.0, own[0, half + 4]
    got = lax.ppermute(sent, "sub", [(0, 1), (1, 0)])
    early = jnp.where(second, got, own)
    late = jnp.where(second, own, got)
    first, last = early[0, half + 1], late[0, half + 2]
    link = jnp.where(early[0, half + 2] == late[0, half + 1], 1.0, 0.0)
    early_decay, late_decay = early[:, half : half + 1], late[:, half : half + 1] * link
    early, late = early[:, :half], late[:, :half]
    chip_state = late_decay * early + late
    chip_decay = late_decay * early_decay

    chunks, hops = plan(chips, tiles)[:2]
    size = tiles // chunks
    rows = size * half
    tail = jnp.broadcast_to(last, (8, LANES))

    def at(array, t):
        part = array[:size]
        for c in range(1, chunks):
            part = jnp.where(place <= t - c, array[c * size : (c + 1) * size], part)
        return part

    carry = jnp.zeros((size, half, LANES), F32)
    received = []
    for t in range(hops):
        send = at(chip_decay, t) * carry + at(chip_state, t)
        send = jnp.concatenate([send.reshape(rows, LANES), tail], axis=0)
        pairs = [(z, z + 1) for z in range(chips - 1) if 0 <= t - z < chunks]
        got = lax.ppermute(send, "seq", pairs)
        joined = jnp.where(got[rows] == first, 1.0, 0.0)
        carry = joined * got[:rows].reshape(size, half, LANES)
        received.append(carry)
    parts = []
    for c in range(chunks):
        part = jnp.zeros((size, half, LANES), F32)
        for z in range(1, chips):
            part = jnp.where(place == z, received[c + z - 1], part)
        parts.append(part)
    entering = jnp.concatenate(parts, axis=0)
    onward = link * (early_decay * entering + early)
    mine = jnp.where(second, onward, entering)
    other = lax.ppermute(jnp.where(second, entering, onward), "sub", [(0, 1), (1, 0)])
    return mine, other


def solution(mesh):
    placed = (
        P(("groups", "seq", "sub"), "head"),
        P(("groups", "seq", "sub"), "head"),
        P(("groups", "seq", "sub"), None),
        P(("groups", "seq", "sub"), None),
        P("head", ("seq", "sub")),
        P("head"),
        P("head"),
        P("head"),
        P("head"),
        P(("groups", "seq", "sub")),
        P(("groups", "seq", "sub")),
    )

    return jax.shard_map(
        on_device,
        mesh=mesh,
        in_specs=placed,
        out_specs=P(("groups", "seq", "sub"), "head"),
        check_vma=False,
    )
```

```python
import functools
import math

import jax
import jax.numpy as jnp
import numpy as np
from jax import lax
from jax.experimental import pallas as pl
from jax.experimental.pallas import tpu as pltpu
from jax.sharding import PartitionSpec as P

BLOCK = 256
LANES = 128
LOG2E = math.log2(math.e)
INNER_VMEM = 24 << 20
EARLY_VMEM = 32 << 20
F32 = jnp.float32
BF16 = jnp.bfloat16


def dot(a, b, contract=((1,), (0,))):
    return lax.dot_general(a, b, (contract, ((), ())), preferred_element_type=F32)


def two_parts(value):
    high = value.astype(BF16)
    low = (value - high.astype(F32)).astype(BF16)
    return high, low


def pick_row(ref, base, count, k, cols):
    row = ref[base : base + 1, cols]
    for j in range(1, count):
        row = jnp.where(k == j, ref[base + j : base + j + 1, cols], row)
    return row


def softplus(v):
    u = jnp.exp(-jnp.abs(v))
    s = u / (2.0 + u)
    q = s * s
    series = jnp.full_like(q, 1.0 / 15.0)
    for odd in (13, 11, 9, 7, 5, 3, 1):
        series = series * q + 1.0 / odd
    return jnp.maximum(v, 0.0) + 2.0 * s * series


def state_kernel(
    heads,
    live_ref,
    docs_ref,
    spot_ref,
    raw_ref,
    bias_ref,
    decay_ref,
    skip_ref,
    doc_row_ref,
    tri_ref,
    hot_ref,
    hot_low_ref,
    x_ref,
    b_ref,
    g_ref,
    col_ref,
    enter_ref,
    own_ref,
    sent_ref,
    row_ref,
    pack,
    col_parts,
    inputs_t,
    state,
    scal,
):
    length = raw_ref.shape[0 + 1]
    rows = raw_ref.shape[0]
    count = length // BLOCK
    wide = x_ref.shape[1]
    ends = [docs_ref[j * BLOCK + BLOCK - 1] for j in range(count)]

    @pl.when(pl.program_id(0) == 0)
    def _():
        inputs_t[...] = b_ref[...].T
        pack[...] = jnp.zeros_like(pack)
        pack[0:1, 0:heads] = bias_ref[...]
        pack[1:2, 0:heads] = decay_ref[...]
        params = pack[0:LANES, 0:LANES].T
        lane = lax.broadcasted_iota(jnp.int32, (1, length), 1)
        step = softplus(raw_ref[...] + params[0:rows, 0:1])
        step = jnp.where(lane < live_ref[0] * BLOCK, step, 0.0)
        rate = (-LOG2E * jnp.exp(params[0:rows, 1:2])) * step
        high, _ = two_parts(rate)
        middle, low = two_parts(rate - high.astype(F32))
        tri = tri_ref[...]
        logs = jnp.where(step > 0.0, LOG2E * jnp.log(step), -1e30)
        for j in range(count):
            piece = slice(j * BLOCK, (j + 1) * BLOCK)
            cum = dot(high[:, piece], tri) + (dot(middle[:, piece], tri) + dot(low[:, piece], tri))
            g_ref[:, piece] = cum - logs[:, piece]
            same = doc_row_ref[:, piece] == ends[j]
            pack[0:rows, piece] = cum
            pack[rows : 2 * rows, piece] = jnp.where(
                same, step[:, piece] * jnp.exp2(cum[:, BLOCK - 1 :] - cum), 0.0
            )
        pack[LANES - 1 : LANES, :] = doc_row_ref[...].astype(F32)
        for j in range(count):
            piece = slice(j * BLOCK, (j + 1) * BLOCK)
            turned = pack[:, piece].T
            col_ref[piece, :] = turned
            high, low = two_parts(turned)
            col_parts[piece, 0:LANES] = high
            col_parts[piece, LANES:] = low
        head_lane = lax.broadcasted_iota(jnp.int32, (1, LANES), 1) < heads
        before = jnp.zeros((1, LANES), F32)
        scal[...] = jnp.zeros_like(scal)
        for j in range(count):
            end = jnp.where(head_lane, col_ref[(j + 1) * BLOCK - 1 : (j + 1) * BLOCK, :], 0.0)
            scal[j : j + 1, :] = jnp.where(head_lane, jnp.exp2(end), 0.0)
            scal[count + j : count + j + 1, :] = jnp.where(head_lane, jnp.exp2(before), 0.0)
            before = before + end
        scal[2 * count : 2 * count + 1, :] = jnp.where(head_lane, jnp.exp2(before), 0.0)
        scal[2 * count + 1 : 2 * count + 2, 0:heads] = skip_ref[...]

    hot = hot_ref[...]
    high, low = two_parts(scal[...])
    row = dot(high, hot) + dot(low, hot)
    row_ref[...] = row
    hot_low = jnp.concatenate([hot_low_ref[...]] * 2, axis=0)
    state[...] = jnp.zeros_like(state)
    scaled = (x_ref[...].astype(F32) * dot(col_parts[...], hot_low)).astype(BF16)
    for j in range(count):
        piece = slice(j * BLOCK, (j + 1) * BLOCK)
        prior = docs_ref[max(j * BLOCK - 1, 0)]
        passage = row[j : j + 1, :] * jnp.where(ends[j] == prior, 1.0, 0.0)
        old = state[...]
        enter_ref[j] = old.astype(BF16)
        state[...] = passage * old + dot(inputs_t[:, piece], scaled[piece])

    half = state.shape[0] // 2
    total = row[2 * count : 2 * count + 1, :] * jnp.where(ends[count - 1] == docs_ref[0], 1.0, 0.0)
    mine = pl.multiple_of(spot_ref[0] * half, half)
    theirs = pl.multiple_of((1 - spot_ref[0]) * half, half)
    line = lax.broadcasted_iota(jnp.int32, (8, LANES), 0)
    marks = jnp.zeros((8, LANES), F32)
    for at, mark in enumerate((docs_ref[0], docs_ref[length - 1], spot_ref[0], spot_ref[1])):
        marks = jnp.where(line == at + 1, mark.astype(F32), marks)
    for j in range(wide // LANES):
        cols = slice(j * LANES, (j + 1) * LANES)
        foot = jnp.where(line == 0, total[:, cols], marks)
        own_ref[j, 0:half, :] = state[pl.ds(mine, half), cols]
        sent_ref[j, 0:half, :] = state[pl.ds(theirs, half), cols]
        own_ref[j, half:, :] = foot
        sent_ref[j, half:, :] = foot


def prepare_kernel(heads, docs_ref, b_ref, c_ref, col_ref, doc_row_ref, affinity_ref, entry_ref):
    t = lax.broadcasted_iota(jnp.int32, (BLOCK, BLOCK), 0)
    s = lax.broadcasted_iota(jnp.int32, (BLOCK, BLOCK), 1)
    lane = lax.broadcasted_iota(jnp.int32, (1, LANES), 1)
    for j in range(affinity_ref.shape[0]):
        piece = slice(j * BLOCK, (j + 1) * BLOCK)
        block = pl.program_id(0) * affinity_ref.shape[0] + j
        columns = col_ref[piece, :]
        doc_col = columns[:, LANES - 1 :]
        doc_row = doc_row_ref[:, piece].astype(F32)
        affinity_ref[j] = jnp.where(
            (t >= s) & (doc_col == doc_row),
            dot(c_ref[piece, :], b_ref[piece, :], ((1,), (1,))),
            0.0,
        )
        prior_doc = docs_ref[jnp.maximum(block * BLOCK - 1, 0)].astype(F32)
        linked = (doc_col == prior_doc) & (lane < heads)
        high, low = two_parts(jnp.where(linked, jnp.exp2(columns), 0.0))
        entry_ref[piece, 0:LANES] = high
        entry_ref[piece, LANES:] = low


def inner_kernel(
    width,
    first_tile,
    group,
    count,
    live_ref,
    docs_ref,
    x_ref,
    z_ref,
    c_ref,
    g_ref,
    col_ref,
    affinity_ref,
    entry_ref,
    enter_ref,
    row_ref,
    hot_ref,
    *refs,
):
    y_ref, f_ref = refs[-2:]
    k = pl.program_id(0)
    half = BLOCK // 2
    per_tile = LANES // width

    @pl.when(k >= live_ref[0])
    def _():
        y_ref[...] = jnp.zeros_like(y_ref)
        f_ref[...] = jnp.zeros_like(f_ref)

    @pl.when(k < live_ref[0])
    def _():
        readout = c_ref[...]
        lane = lax.broadcasted_iota(jnp.int32, (1, LANES), 1)
        nothing = jnp.zeros((BLOCK, LANES), BF16)
        reaches = jnp.where(docs_ref[jnp.maximum(k * BLOCK - 1, 0)] == docs_ref[0], 1.0, 0.0)
        passed = pick_row(row_ref, count, count, k, slice(None)) * reaches
        for q in range(x_ref.shape[1] // (group * LANES)):
            cols = slice(q * group * LANES, (q + 1) * group * LANES)
            x = x_ref[:, cols]
            tops, bottoms, masked = [], [], []
            for u in range(group):
                part = x[:, u * LANES : (u + 1) * LANES]
                for i in range(per_tile):
                    h = (first_tile + q * group + u) * per_tile + i
                    cum = jnp.broadcast_to(col_ref[:, h : h + 1], (BLOCK, LANES))
                    left, right = g_ref[h : h + 1, :half], g_ref[h : h + 1, half:]
                    top = jnp.exp2(jnp.minimum(cum[:half] - left, 64.0))
                    bottom = jnp.exp2(cum[half:] - left)
                    corner = jnp.exp2(jnp.minimum(cum[half:] - right, 64.0))
                    tops.append((top * affinity_ref[0, :half, :half]).astype(BF16))
                    bottoms.append((bottom * affinity_ref[0, half:, :half]).astype(BF16))
                    bottoms.append((corner * affinity_ref[0, half:, half:]).astype(BF16))
                    mine = (lane >= i * width) & (lane < (i + 1) * width)
                    kept = part * jnp.where(mine, 1.0, 0.0).astype(BF16)
                    masked.append(
                        jnp.concatenate(
                            [kept if v == u else nothing for v in range(group)], axis=1
                        )
                    )
            upper = dot(
                jnp.concatenate(tops, axis=1),
                jnp.concatenate([m[:half] for m in masked], axis=0),
            )
            lower = dot(jnp.concatenate(bottoms, axis=1), jnp.concatenate(masked, axis=0))
            hot = jnp.concatenate([hot_ref[:, cols]] * 2, axis=0)
            enter = dot(entry_ref[...], hot)
            outer = dot(readout, enter_ref[0, :, cols])
            skip = row_ref[2 * count + 1 : 2 * count + 2, cols]
            y = jnp.concatenate([upper, lower], axis=0) + enter * outer + skip * x.astype(F32)
            z = z_ref[:, cols].astype(F32)
            gate = z / (1.0 + jnp.exp2(-LOG2E * z))
            y_ref[:, cols] = y * gate
            f_ref[:, cols] = enter * gate * passed[:, cols]


def join_kernel(spot_ref, own_ref, other_ref, c_ref, *refs):
    pieces = (len(refs) - 3) // 2
    gated_ref, square_ref, total = refs[2 * pieces :]
    length = c_ref.shape[0]
    second = spot_ref[0] == 1
    total[...] = jnp.zeros_like(total)
    tile = 0
    for y_ref, f_ref in zip(refs[:pieces], refs[pieces : 2 * pieces]):
        wide = chunk_of(y_ref.shape[1], 4 * LANES)
        for c in range(0, y_ref.shape[1], wide):
            parts = []
            for j in range(tile, tile + wide // LANES):
                own, other = own_ref[j].astype(BF16), other_ref[j].astype(BF16)
                parts.append(
                    jnp.concatenate(
                        [jnp.where(second, other, own), jnp.where(second, own, other)], axis=0
                    )
                )
            carry = jnp.concatenate(parts, axis=1)
            for r in range(0, length, BLOCK):
                rows = slice(r, r + BLOCK)
                outer = dot(c_ref[rows, :], carry)
                gated = y_ref[rows, c : c + wide] + f_ref[rows, c : c + wide] * outer
                gated_ref[rows, tile * LANES : tile * LANES + wide] = gated
                square = total[rows, :]
                for j in range(0, wide, LANES):
                    square = square + gated[:, j : j + LANES] * gated[:, j : j + LANES]
                total[rows, :] = square
            tile += wide // LANES
    square_ref[...] = jnp.sum(total[...].T, axis=0, keepdims=True)


def norm_kernel(channels_all, square_ref, more_ref, gain_ref, gated_ref, out_ref, scale):
    rows = out_ref.shape[0]
    start = pl.multiple_of(pl.program_id(0) * rows, rows)
    row = lax.rsqrt((square_ref[...] + more_ref[...]) / channels_all + 1e-05)
    scale[...] = jnp.broadcast_to(row, (LANES, rows)).T
    for r in range(0, rows, 16):
        part = scale[r : r + 16, :]
        for j in range(gated_ref.shape[1] // LANES):
            cols = slice(j * LANES, (j + 1) * LANES)
            gated = gated_ref[pl.ds(start + r, 16), cols]
            out_ref[r : r + 16, cols] = (gated * part * gain_ref[:, cols]).astype(BF16)


def chunk_of(total, most):
    wide = most
    while total % wide:
        wide -= LANES
    return wide


def whole(shape):
    return pl.BlockSpec(shape, lambda k, *_: (0,) * len(shape))


def in_hbm(*values):
    return [pltpu.with_memory_space_constraint(value, pltpu.HBM) for value in values]


SMEM = pl.BlockSpec(memory_space=pltpu.SMEM)
VMEM = pl.BlockSpec(memory_space=pltpu.VMEM)


def plan(chips, tiles):
    chunks = 2 if tiles % 2 == 0 else 1
    pieces = (tiles,)
    if tiles % 10 == 0:
        pieces = (3 * tiles // 10,) * 2 + (tiles // 5,) * 2
    return chunks, chunks + chips - 2, pieces


def on_device(
    token_values,
    gate_values,
    state_input,
    state_readout,
    step_raw,
    step_bias,
    decay_log,
    skip_gain,
    norm_gain,
    document_ids,
    live_blocks,
):
    length, channels = token_values.shape
    heads = step_raw.shape[0]
    width = channels // heads
    states = state_input.shape[1]
    half = states // 2
    count = length // BLOCK
    tiles = channels // LANES
    rows = -(-heads // 8) * 8
    scalars = -(-(2 * count + 2) // 16) * 16
    assert lax.axis_size("sub") == 2 and 2 * rows < LANES and states == LANES

    raw = step_raw
    if rows != heads:
        raw = jnp.pad(raw, ((0, rows - heads), (0, 0)))
    doc_row = document_ids.reshape(1, length)
    spot = jnp.stack([lax.axis_index("sub"), lax.axis_index("seq")]).astype(jnp.int32)
    head_of = np.arange(channels)[None, :] // width
    lanes = np.arange(LANES)[:, None]
    hot = jnp.asarray(lanes == head_of, dtype=BF16)
    hot_low = jnp.asarray(lanes == head_of + rows, dtype=BF16)
    tri = jnp.asarray(np.triu(np.ones((BLOCK, BLOCK))), dtype=BF16)

    chunk = chunk_of(channels, 512)
    per_chunk = chunk // LANES
    g, col, enter, own, sent, row = pl.pallas_call(
        functools.partial(state_kernel, heads),
        grid=(channels // chunk,),
        in_specs=[
            SMEM,
            SMEM,
            SMEM,
            whole((rows, length)),
            whole((1, heads)),
            whole((1, heads)),
            whole((1, heads)),
            whole((1, length)),
            whole((BLOCK, BLOCK)),
            pl.BlockSpec((LANES, chunk), lambda c: (0, c)),
            pl.BlockSpec((LANES, chunk), lambda c: (0, c)),
            pl.BlockSpec((length, chunk), lambda c: (0, c)),
            whole((length, states)),
        ],
        out_specs=[
            whole((rows, length)),
            whole((length, LANES)),
            pl.BlockSpec((count, states, chunk), lambda c: (0, 0, c)),
            pl.BlockSpec((per_chunk, half + 8, LANES), lambda c: (c, 0, 0)),
            pl.BlockSpec((per_chunk, half + 8, LANES), lambda c: (c, 0, 0)),
            pl.BlockSpec((scalars, chunk), lambda c: (0, c)),
        ],
        out_shape=[
            jax.ShapeDtypeStruct((rows, length), F32),
            jax.ShapeDtypeStruct((length, LANES), F32),
            jax.ShapeDtypeStruct((count, states, channels), BF16),
            jax.ShapeDtypeStruct((tiles, half + 8, LANES), F32),
            jax.ShapeDtypeStruct((tiles, half + 8, LANES), F32),
            jax.ShapeDtypeStruct((scalars, channels), F32),
        ],
        scratch_shapes=[
            pltpu.VMEM((LANES, length), F32),
            pltpu.VMEM((length, 2 * LANES), BF16),
            pltpu.VMEM((states, length), BF16),
            pltpu.VMEM((states, chunk), F32),
            pltpu.VMEM((scalars, LANES), F32),
        ],
        compiler_params=pltpu.CompilerParams(vmem_limit_bytes=EARLY_VMEM),
        name="shard_state",
    )(
        live_blocks,
        document_ids,
        spot,
        *in_hbm(
            raw,
            step_bias.reshape(1, heads),
            decay_log.reshape(1, heads),
            skip_gain.reshape(1, heads),
            doc_row,
            tri,
            hot,
            hot_low,
            token_values,
            state_input,
        ),
    )

    span = 2 if count % 2 == 0 else 1
    affinity, entry = pl.pallas_call(
        functools.partial(prepare_kernel, heads),
        grid=(count // span,),
        in_specs=[
            SMEM,
            pl.BlockSpec((span * BLOCK, states), lambda k: (k, 0)),
            pl.BlockSpec((span * BLOCK, states), lambda k: (k, 0)),
            pl.BlockSpec((span * BLOCK, LANES), lambda k: (k, 0)),
            pl.BlockSpec((1, span * BLOCK), lambda k: (0, k)),
        ],
        out_specs=[
            pl.BlockSpec((span, BLOCK, BLOCK), lambda k: (k, 0, 0)),
            pl.BlockSpec((span * BLOCK, 2 * LANES), lambda k: (k, 0)),
        ],
        out_shape=[
            jax.ShapeDtypeStruct((count, BLOCK, BLOCK), F32),
            jax.ShapeDtypeStruct((length, 2 * LANES), BF16),
        ],
        compiler_params=pltpu.CompilerParams(vmem_limit_bytes=EARLY_VMEM),
        name="prepare",
    )(document_ids, *in_hbm(state_input, state_readout), col, doc_row)

    pieces = plan(lax.axis_size("seq"), tiles)[2]
    group = 2 if tiles % 2 == 0 else 1
    ys, fs, at = [], [], 0
    x, z, readout, heads_hot = in_hbm(token_values, gate_values, state_readout, hot)
    inputs = (x, z, readout, g, col, affinity, entry, enter, row, heads_hot)
    for size in pieces:
        wide, first = size * LANES, at // size
        y, f = pl.pallas_call(
            functools.partial(inner_kernel, width, at, group, count),
            grid=(count,),
            in_specs=[
                SMEM,
                SMEM,
                pl.BlockSpec((BLOCK, wide), lambda k, q=first: (k, q)),
                pl.BlockSpec((BLOCK, wide), lambda k, q=first: (k, q)),
                pl.BlockSpec((BLOCK, states), lambda k: (k, 0)),
                pl.BlockSpec((rows, BLOCK), lambda k: (0, k)),
                pl.BlockSpec((BLOCK, LANES), lambda k: (k, 0)),
                pl.BlockSpec((1, BLOCK, BLOCK), lambda k: (k, 0, 0)),
                pl.BlockSpec((BLOCK, 2 * LANES), lambda k: (k, 0)),
                pl.BlockSpec((1, states, wide), lambda k, q=first: (k, 0, q)),
                pl.BlockSpec((scalars, wide), lambda k, q=first: (0, q)),
                pl.BlockSpec((LANES, wide), lambda k, q=first: (0, q)),
            ],
            out_specs=[pl.BlockSpec((BLOCK, wide), lambda k: (k, 0))] * 2,
            out_shape=[
                jax.ShapeDtypeStruct((length, wide), F32),
                jax.ShapeDtypeStruct((length, wide), F32),
            ],
            cost_estimate=pl.CostEstimate(
                flops=length * wide * 1200,
                bytes_accessed=length * wide * 10,
                transcendentals=0,
            ),
            compiler_params=pltpu.CompilerParams(vmem_limit_bytes=INNER_VMEM),
        )(live_blocks, document_ids, *inputs)
        ys.append(y)
        fs.append(f)
        at += size

    own, other = carry_in(own, sent, half)

    gated, squares = pl.pallas_call(
        join_kernel,
        in_specs=[SMEM] + [VMEM] * (3 + 2 * len(pieces)),
        out_specs=[VMEM, VMEM],
        out_shape=[
            jax.ShapeDtypeStruct((length, channels), F32),
            jax.ShapeDtypeStruct((1, length), F32),
        ],
        scratch_shapes=[pltpu.VMEM((length, LANES), F32)],
        compiler_params=pltpu.CompilerParams(vmem_limit_bytes=16 << 20),
        name="join",
    )(spot, own, other, state_readout, *ys, *fs)

    squares, more = summed(squares, "head")
    return pl.pallas_call(
        functools.partial(norm_kernel, channels * lax.axis_size("head")),
        grid=(length // LANES,),
        in_specs=[
            pl.BlockSpec((1, LANES), lambda k: (0, k)),
            pl.BlockSpec((1, LANES), lambda k: (0, k)),
            whole((1, channels)),
            VMEM,
        ],
        out_specs=pl.BlockSpec((LANES, channels), lambda k: (k, 0)),
        out_shape=jax.ShapeDtypeStruct((length, channels), BF16),
        scratch_shapes=[pltpu.VMEM((LANES, LANES), F32)],
        compiler_params=pltpu.CompilerParams(vmem_limit_bytes=16 << 20),
        name="norm",
    )(squares, more, norm_gain.reshape(1, channels), gated)


def summed(value, axis):
    size = lax.axis_size(axis)
    if size & (size - 1):
        total = value
        for shift in range(1, size):
            total = total + lax.ppermute(value, axis, [(i, (i + shift) % size) for i in range(size)])
        return total, jnp.zeros_like(value)
    more, shift = jnp.zeros_like(value), 1
    while shift < size:
        value = value + more if shift > 1 else value
        more = lax.ppermute(value, axis, [(i, i ^ shift) for i in range(size)])
        shift *= 2
    return value, more


def carry_in(own, sent, half):
    tiles = own.shape[0]
    chips = lax.axis_size("seq")
    second, place = own[0, half + 3] == 1.0, own[0, half + 4]
    got = lax.ppermute(sent, "sub", [(0, 1), (1, 0)])
    early = jnp.where(second, got, own)
    late = jnp.where(second, own, got)
    first, last = early[0, half + 1], late[0, half + 2]
    link = jnp.where(early[0, half + 2] == late[0, half + 1], 1.0, 0.0)
    early_decay, late_decay = early[:, half : half + 1], late[:, half : half + 1] * link
    early, late = early[:, :half], late[:, :half]
    chip_state = late_decay * early + late
    chip_decay = late_decay * early_decay

    chunks, hops = plan(chips, tiles)[:2]
    size = tiles // chunks
    rows = size * half
    tail = jnp.broadcast_to(last, (8, LANES))

    def at(array, t):
        part = array[:size]
        for c in range(1, chunks):
            part = jnp.where(place <= t - c, array[c * size : (c + 1) * size], part)
        return part

    carry = jnp.zeros((size, half, LANES), F32)
    received = []
    for t in range(hops):
        send = at(chip_decay, t) * carry + at(chip_state, t)
        send = jnp.concatenate([send.reshape(rows, LANES), tail], axis=0)
        pairs = [(z, z + 1) for z in range(chips - 1) if 0 <= t - z < chunks]
        got = lax.ppermute(send, "seq", pairs)
        joined = jnp.where(got[rows] == first, 1.0, 0.0)
        carry = joined * got[:rows].reshape(size, half, LANES)
        received.append(carry)
    parts = []
    for c in range(chunks):
        part = jnp.zeros((size, half, LANES), F32)
        for z in range(1, chips):
            part = jnp.where(place == z, received[c + z - 1], part)
        parts.append(part)
    entering = jnp.concatenate(parts, axis=0)
    onward = link * (early_decay * entering + early)
    mine = jnp.where(second, onward, entering)
    other = lax.ppermute(jnp.where(second, entering, onward), "sub", [(0, 1), (1, 0)])
    return mine, other


def solution(mesh):
    placed = (
        P(("groups", "seq", "sub"), "head"),
        P(("groups", "seq", "sub"), "head"),
        P(("groups", "seq", "sub"), None),
        P(("groups", "seq", "sub"), None),
        P("head", ("seq", "sub")),
        P("head"),
        P("head"),
        P("head"),
        P("head"),
        P(("groups", "seq", "sub")),
        P(("groups", "seq", "sub")),
    )

    return jax.shard_map(
        on_device,
        mesh=mesh,
        in_specs=placed,
        out_specs=P(("groups", "seq", "sub"), "head"),
        check_vma=False,
    )
```

```python
import functools
import math

import jax
import jax.numpy as jnp
import numpy as np
from jax import lax
from jax.experimental import pallas as pl
from jax.experimental.pallas import tpu as pltpu
from jax.sharding import PartitionSpec as P

BLOCK = 256
LANES = 128
LOG2E = math.log2(math.e)
CHUNKS = 3
INNER_VMEM = 16 << 20
EARLY_VMEM = 32 << 20
F32 = jnp.float32
BF16 = jnp.bfloat16


def dot(a, b, contract=((1,), (0,))):
    return lax.dot_general(a, b, (contract, ((), ())), preferred_element_type=F32)


def two_parts(value):
    high = value.astype(BF16)
    low = (value - high.astype(F32)).astype(BF16)
    return high, low


def pick_row(ref, base, count, k, cols):
    row = ref[base : base + 1, cols]
    for j in range(1, count):
        row = jnp.where(k == j, ref[base + j : base + j + 1, cols], row)
    return row


def softplus(v):
    u = jnp.exp(-jnp.abs(v))
    s = u / (2.0 + u)
    q = s * s
    series = jnp.full_like(q, 1.0 / 15.0)
    for odd in (13, 11, 9, 7, 5, 3, 1):
        series = series * q + 1.0 / odd
    return jnp.maximum(v, 0.0) + 2.0 * s * series


def state_kernel(
    heads,
    live_ref,
    docs_ref,
    spot_ref,
    raw_ref,
    bias_ref,
    decay_ref,
    skip_ref,
    doc_row_ref,
    tri_ref,
    hot_ref,
    hot_low_ref,
    x_ref,
    b_ref,
    g_ref,
    col_ref,
    enter_ref,
    own_ref,
    sent_ref,
    row_ref,
    pack,
    col_parts,
    inputs_t,
    state,
    scal,
):
    length = raw_ref.shape[0 + 1]
    rows = raw_ref.shape[0]
    count = length // BLOCK
    wide = x_ref.shape[1]
    ends = [docs_ref[j * BLOCK + BLOCK - 1] for j in range(count)]

    @pl.when(pl.program_id(0) == 0)
    def _():
        inputs_t[...] = b_ref[...].T
        pack[...] = jnp.zeros_like(pack)
        pack[0:1, 0:heads] = bias_ref[...]
        pack[1:2, 0:heads] = decay_ref[...]
        params = pack[0:LANES, 0:LANES].T
        lane = lax.broadcasted_iota(jnp.int32, (1, length), 1)
        step = softplus(raw_ref[...] + params[0:rows, 0:1])
        step = jnp.where(lane < live_ref[0] * BLOCK, step, 0.0)
        rate = (-LOG2E * jnp.exp(params[0:rows, 1:2])) * step
        high, _ = two_parts(rate)
        middle, low = two_parts(rate - high.astype(F32))
        tri = tri_ref[...]
        logs = jnp.where(step > 0.0, LOG2E * jnp.log(step), -1e30)
        for j in range(count):
            piece = slice(j * BLOCK, (j + 1) * BLOCK)
            cum = dot(high[:, piece], tri) + (dot(middle[:, piece], tri) + dot(low[:, piece], tri))
            g_ref[:, piece] = cum - logs[:, piece]
            same = doc_row_ref[:, piece] == ends[j]
            pack[0:rows, piece] = cum
            pack[rows : 2 * rows, piece] = jnp.where(
                same, step[:, piece] * jnp.exp2(cum[:, BLOCK - 1 :] - cum), 0.0
            )
        pack[LANES - 1 : LANES, :] = doc_row_ref[...].astype(F32)
        for j in range(count):
            piece = slice(j * BLOCK, (j + 1) * BLOCK)
            turned = pack[:, piece].T
            col_ref[piece, :] = turned
            high, low = two_parts(turned)
            col_parts[piece, 0:LANES] = high
            col_parts[piece, LANES:] = low
        head_lane = lax.broadcasted_iota(jnp.int32, (1, LANES), 1) < heads
        before = jnp.zeros((1, LANES), F32)
        scal[...] = jnp.zeros_like(scal)
        for j in range(count):
            end = jnp.where(head_lane, col_ref[(j + 1) * BLOCK - 1 : (j + 1) * BLOCK, :], 0.0)
            scal[j : j + 1, :] = jnp.where(head_lane, jnp.exp2(end), 0.0)
            scal[count + j : count + j + 1, :] = jnp.where(head_lane, jnp.exp2(before), 0.0)
            before = before + end
        scal[2 * count : 2 * count + 1, :] = jnp.where(head_lane, jnp.exp2(before), 0.0)
        scal[2 * count + 1 : 2 * count + 2, 0:heads] = skip_ref[...]

    hot = hot_ref[...]
    high, low = two_parts(scal[...])
    row = dot(high, hot) + dot(low, hot)
    row_ref[...] = row
    hot_low = jnp.concatenate([hot_low_ref[...]] * 2, axis=0)
    state[...] = jnp.zeros_like(state)
    scaled = (x_ref[...].astype(F32) * dot(col_parts[...], hot_low)).astype(BF16)
    for j in range(count):
        piece = slice(j * BLOCK, (j + 1) * BLOCK)
        prior = docs_ref[max(j * BLOCK - 1, 0)]
        passage = row[j : j + 1, :] * jnp.where(ends[j] == prior, 1.0, 0.0)
        old = state[...]
        enter_ref[j] = old.astype(BF16)
        state[...] = passage * old + dot(inputs_t[:, piece], scaled[piece])

    half = state.shape[0] // 2
    total = row[2 * count : 2 * count + 1, :] * jnp.where(ends[count - 1] == docs_ref[0], 1.0, 0.0)
    mine = pl.multiple_of(spot_ref[0] * half, half)
    theirs = pl.multiple_of((1 - spot_ref[0]) * half, half)
    line = lax.broadcasted_iota(jnp.int32, (8, LANES), 0)
    marks = jnp.zeros((8, LANES), F32)
    for at, mark in enumerate((docs_ref[0], docs_ref[length - 1], spot_ref[0], spot_ref[1])):
        marks = jnp.where(line == at + 1, mark.astype(F32), marks)
    for j in range(wide // LANES):
        cols = slice(j * LANES, (j + 1) * LANES)
        foot = jnp.where(line == 0, total[:, cols], marks)
        own_ref[j, 0:half, :] = state[pl.ds(mine, half), cols]
        sent_ref[j, 0:half, :] = state[pl.ds(theirs, half), cols]
        own_ref[j, half:, :] = foot
        sent_ref[j, half:, :] = foot


def prepare_kernel(heads, docs_ref, b_ref, c_ref, col_ref, doc_row_ref, affinity_ref, entry_ref):
    t = lax.broadcasted_iota(jnp.int32, (BLOCK, BLOCK), 0)
    s = lax.broadcasted_iota(jnp.int32, (BLOCK, BLOCK), 1)
    lane = lax.broadcasted_iota(jnp.int32, (1, LANES), 1)
    for j in range(affinity_ref.shape[0]):
        piece = slice(j * BLOCK, (j + 1) * BLOCK)
        block = pl.program_id(0) * affinity_ref.shape[0] + j
        columns = col_ref[piece, :]
        doc_col = columns[:, LANES - 1 :]
        doc_row = doc_row_ref[:, piece].astype(F32)
        affinity_ref[j] = jnp.where(
            (t >= s) & (doc_col == doc_row),
            dot(c_ref[piece, :], b_ref[piece, :], ((1,), (1,))),
            0.0,
        )
        prior_doc = docs_ref[jnp.maximum(block * BLOCK - 1, 0)].astype(F32)
        linked = (doc_col == prior_doc) & (lane < heads)
        high, low = two_parts(jnp.where(linked, jnp.exp2(columns), 0.0))
        entry_ref[piece, 0:LANES] = high
        entry_ref[piece, LANES:] = low


def inner_kernel(
    width,
    first_tile,
    group,
    count,
    live_ref,
    docs_ref,
    x_ref,
    z_ref,
    c_ref,
    g_ref,
    col_ref,
    affinity_ref,
    entry_ref,
    enter_ref,
    row_ref,
    hot_ref,
    *refs,
):
    y_ref, f_ref = refs[-2:]
    k = pl.program_id(0)
    half = BLOCK // 2
    per_tile = LANES // width

    @pl.when(k >= live_ref[0])
    def _():
        y_ref[...] = jnp.zeros_like(y_ref)
        f_ref[...] = jnp.zeros_like(f_ref)

    @pl.when(k < live_ref[0])
    def _():
        readout = c_ref[...]
        lane = lax.broadcasted_iota(jnp.int32, (1, LANES), 1)
        nothing = jnp.zeros((BLOCK, LANES), BF16)
        reaches = jnp.where(docs_ref[jnp.maximum(k * BLOCK - 1, 0)] == docs_ref[0], 1.0, 0.0)
        passed = pick_row(row_ref, count, count, k, slice(None)) * reaches
        for q in range(x_ref.shape[1] // (group * LANES)):
            cols = slice(q * group * LANES, (q + 1) * group * LANES)
            x = x_ref[:, cols]
            tops, bottoms, masked = [], [], []
            for u in range(group):
                part = x[:, u * LANES : (u + 1) * LANES]
                for i in range(per_tile):
                    h = (first_tile + q * group + u) * per_tile + i
                    cum = jnp.broadcast_to(col_ref[:, h : h + 1], (BLOCK, LANES))
                    left, right = g_ref[h : h + 1, :half], g_ref[h : h + 1, half:]
                    top = jnp.exp2(jnp.minimum(cum[:half] - left, 64.0))
                    bottom = jnp.exp2(cum[half:] - left)
                    corner = jnp.exp2(jnp.minimum(cum[half:] - right, 64.0))
                    tops.append((top * affinity_ref[0, :half, :half]).astype(BF16))
                    bottoms.append((bottom * affinity_ref[0, half:, :half]).astype(BF16))
                    bottoms.append((corner * affinity_ref[0, half:, half:]).astype(BF16))
                    mine = (lane >= i * width) & (lane < (i + 1) * width)
                    kept = part * jnp.where(mine, 1.0, 0.0).astype(BF16)
                    masked.append(
                        jnp.concatenate(
                            [kept if v == u else nothing for v in range(group)], axis=1
                        )
                    )
            upper = dot(
                jnp.concatenate(tops, axis=1),
                jnp.concatenate([m[:half] for m in masked], axis=0),
            )
            lower = dot(jnp.concatenate(bottoms, axis=1), jnp.concatenate(masked, axis=0))
            hot = jnp.concatenate([hot_ref[:, cols]] * 2, axis=0)
            enter = dot(entry_ref[...], hot)
            outer = dot(readout, enter_ref[0, :, cols])
            skip = row_ref[2 * count + 1 : 2 * count + 2, cols]
            y = jnp.concatenate([upper, lower], axis=0) + enter * outer + skip * x.astype(F32)
            z = z_ref[:, cols].astype(F32)
            gate = z / (1.0 + jnp.exp2(-LOG2E * z))
            y_ref[:, cols] = y * gate
            f_ref[:, cols] = enter * gate * passed[:, cols]


def join_kernel(spot_ref, own_ref, other_ref, c_ref, *refs):
    pieces = (len(refs) - 3) // 2
    gated_ref, square_ref, total = refs[2 * pieces :]
    length = c_ref.shape[0]
    second = spot_ref[0] == 1
    total[...] = jnp.zeros_like(total)
    tile = 0
    for y_ref, f_ref in zip(refs[:pieces], refs[pieces : 2 * pieces]):
        wide = chunk_of(y_ref.shape[1], 4 * LANES)
        for c in range(0, y_ref.shape[1], wide):
            parts = []
            for j in range(tile, tile + wide // LANES):
                own, other = own_ref[j].astype(BF16), other_ref[j].astype(BF16)
                parts.append(
                    jnp.concatenate(
                        [jnp.where(second, other, own), jnp.where(second, own, other)], axis=0
                    )
                )
            carry = jnp.concatenate(parts, axis=1)
            for r in range(0, length, BLOCK):
                rows = slice(r, r + BLOCK)
                outer = dot(c_ref[rows, :], carry)
                gated = y_ref[rows, c : c + wide] + f_ref[rows, c : c + wide] * outer
                gated_ref[rows, tile * LANES : tile * LANES + wide] = gated
                square = total[rows, :]
                for j in range(0, wide, LANES):
                    square = square + gated[:, j : j + LANES] * gated[:, j : j + LANES]
                total[rows, :] = square
            tile += wide // LANES
    square_ref[...] = jnp.sum(total[...].T, axis=0, keepdims=True)


def gain_kernel(gain_ref, gated_ref, out_ref):
    for r in range(0, gated_ref.shape[0], BLOCK):
        for j in range(0, gated_ref.shape[1], LANES):
            piece = (slice(r, r + BLOCK), slice(j, j + LANES))
            out_ref[piece] = gated_ref[piece] * gain_ref[:, j : j + LANES]


def norm_kernel(channels_all, square_ref, more_ref, gained_ref, out_ref, scale):
    rows = out_ref.shape[0]
    start = pl.multiple_of(pl.program_id(0) * rows, rows)
    row = lax.rsqrt((square_ref[...] + more_ref[...]) / channels_all + 1e-05)
    scale[...] = jnp.broadcast_to(row, (LANES, rows)).T
    for r in range(0, rows, 16):
        part = scale[r : r + 16, :]
        for j in range(0, gained_ref.shape[1], LANES):
            gained = gained_ref[pl.ds(start + r, 16), j : j + LANES]
            out_ref[r : r + 16, j : j + LANES] = (gained * part).astype(BF16)


def chunk_of(total, most):
    wide = most
    while total % wide:
        wide -= LANES
    return wide


def whole(shape):
    return pl.BlockSpec(shape, lambda k, *_: (0,) * len(shape))


def in_hbm(*values):
    return [pltpu.with_memory_space_constraint(value, pltpu.HBM) for value in values]


SMEM = pl.BlockSpec(memory_space=pltpu.SMEM)
VMEM = pl.BlockSpec(memory_space=pltpu.VMEM)


def plan(chips, tiles):
    chunks = min(CHUNKS, tiles)
    size = -(-tiles // chunks)
    starts = tuple(min(c * size, tiles - size) for c in range(chunks))
    pieces = (tiles // 5,) * 5 if tiles % 10 == 0 else (tiles,)
    return starts, size, chunks + chips - 2, pieces


def on_device(
    token_values,
    gate_values,
    state_input,
    state_readout,
    step_raw,
    step_bias,
    decay_log,
    skip_gain,
    norm_gain,
    document_ids,
    live_blocks,
):
    length, channels = token_values.shape
    heads = step_raw.shape[0]
    width = channels // heads
    states = state_input.shape[1]
    half = states // 2
    count = length // BLOCK
    tiles = channels // LANES
    rows = -(-heads // 8) * 8
    scalars = -(-(2 * count + 2) // 16) * 16
    assert lax.axis_size("sub") == 2 and 2 * rows < LANES and states == LANES

    raw = step_raw
    if rows != heads:
        raw = jnp.pad(raw, ((0, rows - heads), (0, 0)))
    doc_row = document_ids.reshape(1, length)
    spot = jnp.stack([lax.axis_index("sub"), lax.axis_index("seq")]).astype(jnp.int32)
    head_of = np.arange(channels)[None, :] // width
    lanes = np.arange(LANES)[:, None]
    hot = jnp.asarray(lanes == head_of, dtype=BF16)
    hot_low = jnp.asarray(lanes == head_of + rows, dtype=BF16)
    tri = jnp.asarray(np.triu(np.ones((BLOCK, BLOCK))), dtype=BF16)

    chunk = chunk_of(channels, 512)
    per_chunk = chunk // LANES
    g, col, enter, own, sent, row = pl.pallas_call(
        functools.partial(state_kernel, heads),
        grid=(channels // chunk,),
        in_specs=[
            SMEM,
            SMEM,
            SMEM,
            whole((rows, length)),
            whole((1, heads)),
            whole((1, heads)),
            whole((1, heads)),
            whole((1, length)),
            whole((BLOCK, BLOCK)),
            pl.BlockSpec((LANES, chunk), lambda c: (0, c)),
            pl.BlockSpec((LANES, chunk), lambda c: (0, c)),
            pl.BlockSpec((length, chunk), lambda c: (0, c)),
            whole((length, states)),
        ],
        out_specs=[
            whole((rows, length)),
            whole((length, LANES)),
            pl.BlockSpec((count, states, chunk), lambda c: (0, 0, c)),
            pl.BlockSpec((per_chunk, half + 8, LANES), lambda c: (c, 0, 0)),
            pl.BlockSpec((per_chunk, half + 8, LANES), lambda c: (c, 0, 0)),
            pl.BlockSpec((scalars, chunk), lambda c: (0, c)),
        ],
        out_shape=[
            jax.ShapeDtypeStruct((rows, length), F32),
            jax.ShapeDtypeStruct((length, LANES), F32),
            jax.ShapeDtypeStruct((count, states, channels), BF16),
            jax.ShapeDtypeStruct((tiles, half + 8, LANES), F32),
            jax.ShapeDtypeStruct((tiles, half + 8, LANES), F32),
            jax.ShapeDtypeStruct((scalars, channels), F32),
        ],
        scratch_shapes=[
            pltpu.VMEM((LANES, length), F32),
            pltpu.VMEM((length, 2 * LANES), BF16),
            pltpu.VMEM((states, length), BF16),
            pltpu.VMEM((states, chunk), F32),
            pltpu.VMEM((scalars, LANES), F32),
        ],
        compiler_params=pltpu.CompilerParams(vmem_limit_bytes=EARLY_VMEM),
        name="shard_state",
    )(
        live_blocks,
        document_ids,
        spot,
        *in_hbm(
            raw,
            step_bias.reshape(1, heads),
            decay_log.reshape(1, heads),
            skip_gain.reshape(1, heads),
            doc_row,
            tri,
            hot,
            hot_low,
            token_values,
            state_input,
        ),
    )

    span = 2 if count % 2 == 0 else 1
    affinity, entry = pl.pallas_call(
        functools.partial(prepare_kernel, heads),
        grid=(count // span,),
        in_specs=[
            SMEM,
            pl.BlockSpec((span * BLOCK, states), lambda k: (k, 0)),
            pl.BlockSpec((span * BLOCK, states), lambda k: (k, 0)),
            pl.BlockSpec((span * BLOCK, LANES), lambda k: (k, 0)),
            pl.BlockSpec((1, span * BLOCK), lambda k: (0, k)),
        ],
        out_specs=[
            pl.BlockSpec((span, BLOCK, BLOCK), lambda k: (k, 0, 0)),
            pl.BlockSpec((span * BLOCK, 2 * LANES), lambda k: (k, 0)),
        ],
        out_shape=[
            jax.ShapeDtypeStruct((count, BLOCK, BLOCK), F32),
            jax.ShapeDtypeStruct((length, 2 * LANES), BF16),
        ],
        compiler_params=pltpu.CompilerParams(vmem_limit_bytes=EARLY_VMEM),
        name="prepare",
    )(document_ids, *in_hbm(state_input, state_readout), col, doc_row)

    pieces = plan(lax.axis_size("seq"), tiles)[3]
    group = 2 if tiles % 2 == 0 else 1
    ys, fs, at = [], [], 0
    x, z, readout, heads_hot = in_hbm(token_values, gate_values, state_readout, hot)
    inputs = (x, z, readout, g, col, affinity, entry, enter, row, heads_hot)
    for size in pieces:
        wide, first = size * LANES, at // size
        y, f = pl.pallas_call(
            functools.partial(inner_kernel, width, at, group, count),
            grid=(count,),
            in_specs=[
                SMEM,
                SMEM,
                pl.BlockSpec((BLOCK, wide), lambda k, q=first: (k, q)),
                pl.BlockSpec((BLOCK, wide), lambda k, q=first: (k, q)),
                pl.BlockSpec((BLOCK, states), lambda k: (k, 0)),
                pl.BlockSpec((rows, BLOCK), lambda k: (0, k)),
                pl.BlockSpec((BLOCK, LANES), lambda k: (k, 0)),
                pl.BlockSpec((1, BLOCK, BLOCK), lambda k: (k, 0, 0)),
                pl.BlockSpec((BLOCK, 2 * LANES), lambda k: (k, 0)),
                pl.BlockSpec((1, states, wide), lambda k, q=first: (k, 0, q)),
                pl.BlockSpec((scalars, wide), lambda k, q=first: (0, q)),
                pl.BlockSpec((LANES, wide), lambda k, q=first: (0, q)),
            ],
            out_specs=[pl.BlockSpec((BLOCK, wide), lambda k: (k, 0))] * 2,
            out_shape=[
                jax.ShapeDtypeStruct((length, wide), F32),
                jax.ShapeDtypeStruct((length, wide), F32),
            ],
            cost_estimate=pl.CostEstimate(
                flops=length * wide * 1200,
                bytes_accessed=length * wide * 10,
                transcendentals=0,
            ),
            compiler_params=pltpu.CompilerParams(vmem_limit_bytes=INNER_VMEM),
        )(live_blocks, document_ids, *inputs)
        ys.append(y)
        fs.append(f)
        at += size

    own, other = carry_in(own, sent, half)

    gated, squares = pl.pallas_call(
        join_kernel,
        in_specs=[SMEM] + [VMEM] * (3 + 2 * len(pieces)),
        out_specs=[VMEM, VMEM],
        out_shape=[
            jax.ShapeDtypeStruct((length, channels), F32),
            jax.ShapeDtypeStruct((1, length), F32),
        ],
        scratch_shapes=[pltpu.VMEM((length, LANES), F32)],
        compiler_params=pltpu.CompilerParams(vmem_limit_bytes=16 << 20),
        name="join",
    )(spot, own, other, state_readout, *ys, *fs)

    squares, more = summed(squares, "head")
    gained = pl.pallas_call(
        gain_kernel,
        in_specs=[VMEM, VMEM],
        out_specs=VMEM,
        out_shape=jax.ShapeDtypeStruct((length, channels), F32),
        input_output_aliases={1: 0},
        compiler_params=pltpu.CompilerParams(vmem_limit_bytes=16 << 20),
        name="gain",
    )(norm_gain.reshape(1, channels), gated)
    return pl.pallas_call(
        functools.partial(norm_kernel, channels * lax.axis_size("head")),
        grid=(count,),
        in_specs=[
            pl.BlockSpec((1, BLOCK), lambda k: (0, k)),
            pl.BlockSpec((1, BLOCK), lambda k: (0, k)),
            VMEM,
        ],
        out_specs=pl.BlockSpec((BLOCK, channels), lambda k: (k, 0)),
        out_shape=jax.ShapeDtypeStruct((length, channels), BF16),
        scratch_shapes=[pltpu.VMEM((BLOCK, LANES), F32)],
        compiler_params=pltpu.CompilerParams(vmem_limit_bytes=16 << 20),
        name="norm",
    )(squares, more, gained)


def summed(value, axis):
    size = lax.axis_size(axis)
    if size & (size - 1):
        total = value
        for shift in range(1, size):
            total = total + lax.ppermute(value, axis, [(i, (i + shift) % size) for i in range(size)])
        return total, jnp.zeros_like(value)
    more, shift = jnp.zeros_like(value), 1
    while shift < size:
        value = value + more if shift > 1 else value
        more = lax.ppermute(value, axis, [(i, i ^ shift) for i in range(size)])
        shift *= 2
    return value, more


def carry_in(own, sent, half):
    tiles = own.shape[0]
    chips = lax.axis_size("seq")
    second, place = own[0, half + 3] == 1.0, own[0, half + 4]
    got = lax.ppermute(sent, "sub", [(0, 1), (1, 0)])
    early = jnp.where(second, got, own)
    late = jnp.where(second, own, got)
    first, last = early[0, half + 1], late[0, half + 2]
    link = jnp.where(early[0, half + 2] == late[0, half + 1], 1.0, 0.0)
    early_decay, late_decay = early[:, half : half + 1], late[:, half : half + 1] * link
    early, late = early[:, :half], late[:, :half]
    chip_state = late_decay * early + late
    chip_decay = late_decay * early_decay

    starts, size, hops, _ = plan(chips, tiles)
    rows = size * half
    tail = jnp.broadcast_to(last, (8, LANES))

    def at(array, t):
        part = array[starts[0] : starts[0] + size]
        for c in range(1, len(starts)):
            part = jnp.where(place <= t - c, array[starts[c] : starts[c] + size], part)
        return part

    carry = jnp.zeros((size, half, LANES), F32)
    received = []
    for t in range(hops):
        send = at(chip_decay, t) * carry + at(chip_state, t)
        send = jnp.concatenate([send.reshape(rows, LANES), tail], axis=0)
        pairs = [(z, z + 1) for z in range(chips - 1) if 0 <= t - z < len(starts)]
        got = lax.ppermute(send, "seq", pairs)
        joined = jnp.where(got[rows] == first, 1.0, 0.0)
        carry = joined * got[:rows].reshape(size, half, LANES)
        received.append(carry)
    parts, done = [], 0
    for c, start in enumerate(starts):
        part = jnp.zeros((size, half, LANES), F32)
        for z in range(1, chips):
            part = jnp.where(place == z, received[c + z - 1], part)
        parts.append(part[done - start :])
        done = start + size
    entering = jnp.concatenate(parts, axis=0)
    onward = link * (early_decay * entering + early)
    mine = jnp.where(second, onward, entering)
    other = lax.ppermute(jnp.where(second, entering, onward), "sub", [(0, 1), (1, 0)])
    return mine, other


def solution(mesh):
    placed = (
        P(("groups", "seq", "sub"), "head"),
        P(("groups", "seq", "sub"), "head"),
        P(("groups", "seq", "sub"), None),
        P(("groups", "seq", "sub"), None),
        P("head", ("seq", "sub")),
        P("head"),
        P("head"),
        P("head"),
        P("head"),
        P(("groups", "seq", "sub")),
        P(("groups", "seq", "sub")),
    )

    return jax.shard_map(
        on_device,
        mesh=mesh,
        in_specs=placed,
        out_specs=P(("groups", "seq", "sub"), "head"),
        check_vma=False,
    )
```

```python
import functools
import math

import jax
import jax.numpy as jnp
import numpy as np
from jax import lax
from jax.experimental import pallas as pl
from jax.experimental.pallas import tpu as pltpu
from jax.sharding import PartitionSpec as P

BLOCK = 256
LANES = 128
LOG2E = math.log2(math.e)
CHUNKS = 2
INNER_VMEM = 16 << 20
EARLY_VMEM = 32 << 20
F32 = jnp.float32
BF16 = jnp.bfloat16


def dot(a, b, contract=((1,), (0,))):
    return lax.dot_general(a, b, (contract, ((), ())), preferred_element_type=F32)


def two_parts(value):
    high = value.astype(BF16)
    low = (value - high.astype(F32)).astype(BF16)
    return high, low


def pick_row(ref, base, count, k, cols):
    row = ref[base : base + 1, cols]
    for j in range(1, count):
        row = jnp.where(k == j, ref[base + j : base + j + 1, cols], row)
    return row


def softplus(v):
    u = jnp.exp(-jnp.abs(v))
    s = u / (2.0 + u)
    q = s * s
    series = jnp.full_like(q, 1.0 / 15.0)
    for odd in (13, 11, 9, 7, 5, 3, 1):
        series = series * q + 1.0 / odd
    return jnp.maximum(v, 0.0) + 2.0 * s * series


def state_kernel(
    heads,
    live_ref,
    docs_ref,
    spot_ref,
    raw_ref,
    bias_ref,
    decay_ref,
    skip_ref,
    doc_row_ref,
    tri_ref,
    hot_ref,
    hot_low_ref,
    x_ref,
    b_ref,
    cum_ref,
    step_ref,
    col_ref,
    enter_ref,
    own_ref,
    sent_ref,
    row_ref,
    pack,
    col_parts,
    inputs_t,
    state,
    scal,
):
    length = raw_ref.shape[0 + 1]
    rows = raw_ref.shape[0]
    count = length // BLOCK
    wide = x_ref.shape[1]
    ends = [docs_ref[j * BLOCK + BLOCK - 1] for j in range(count)]

    @pl.when(pl.program_id(0) == 0)
    def _():
        inputs_t[...] = b_ref[...].T
        pack[...] = jnp.zeros_like(pack)
        pack[0:1, 0:heads] = bias_ref[...]
        pack[1:2, 0:heads] = decay_ref[...]
        params = pack[0:LANES, 0:LANES].T
        lane = lax.broadcasted_iota(jnp.int32, (1, length), 1)
        step = softplus(raw_ref[...] + params[0:rows, 0:1])
        step = jnp.where(lane < live_ref[0] * BLOCK, step, 0.0)
        rate = (-LOG2E * jnp.exp(params[0:rows, 1:2])) * step
        high, _ = two_parts(rate)
        middle, low = two_parts(rate - high.astype(F32))
        tri = tri_ref[...]
        step_ref[...] = step
        for j in range(count):
            piece = slice(j * BLOCK, (j + 1) * BLOCK)
            cum = dot(high[:, piece], tri) + (dot(middle[:, piece], tri) + dot(low[:, piece], tri))
            cum_ref[:, piece] = cum
            same = doc_row_ref[:, piece] == ends[j]
            pack[0:rows, piece] = cum
            pack[rows : 2 * rows, piece] = jnp.where(
                same, step[:, piece] * jnp.exp2(cum[:, BLOCK - 1 :] - cum), 0.0
            )
        pack[LANES - 1 : LANES, :] = doc_row_ref[...].astype(F32)
        for j in range(count):
            piece = slice(j * BLOCK, (j + 1) * BLOCK)
            turned = pack[:, piece].T
            col_ref[piece, :] = turned
            high, low = two_parts(turned)
            col_parts[piece, 0:LANES] = high
            col_parts[piece, LANES:] = low
        head_lane = lax.broadcasted_iota(jnp.int32, (1, LANES), 1) < heads
        before = jnp.zeros((1, LANES), F32)
        scal[...] = jnp.zeros_like(scal)
        for j in range(count):
            end = jnp.where(head_lane, col_ref[(j + 1) * BLOCK - 1 : (j + 1) * BLOCK, :], 0.0)
            scal[j : j + 1, :] = jnp.where(head_lane, jnp.exp2(end), 0.0)
            scal[count + j : count + j + 1, :] = jnp.where(head_lane, jnp.exp2(before), 0.0)
            before = before + end
        scal[2 * count : 2 * count + 1, :] = jnp.where(head_lane, jnp.exp2(before), 0.0)
        scal[2 * count + 1 : 2 * count + 2, 0:heads] = skip_ref[...]

    hot = hot_ref[...]
    high, low = two_parts(scal[...])
    row = dot(high, hot) + dot(low, hot)
    row_ref[...] = row
    hot_low = jnp.concatenate([hot_low_ref[...]] * 2, axis=0)
    state[...] = jnp.zeros_like(state)
    scaled = (x_ref[...].astype(F32) * dot(col_parts[...], hot_low)).astype(BF16)
    for j in range(count):
        piece = slice(j * BLOCK, (j + 1) * BLOCK)
        prior = docs_ref[max(j * BLOCK - 1, 0)]
        passage = row[j : j + 1, :] * jnp.where(ends[j] == prior, 1.0, 0.0)
        old = state[...]
        enter_ref[j] = old.astype(BF16)
        state[...] = passage * old + dot(inputs_t[:, piece], scaled[piece])

    half = state.shape[0] // 2
    total = row[2 * count : 2 * count + 1, :] * jnp.where(ends[count - 1] == docs_ref[0], 1.0, 0.0)
    mine = pl.multiple_of(spot_ref[0] * half, half)
    theirs = pl.multiple_of((1 - spot_ref[0]) * half, half)
    line = lax.broadcasted_iota(jnp.int32, (8, LANES), 0)
    marks = jnp.zeros((8, LANES), F32)
    for at, mark in enumerate((docs_ref[0], docs_ref[length - 1], spot_ref[0], spot_ref[1])):
        marks = jnp.where(line == at + 1, mark.astype(F32), marks)
    for j in range(wide // LANES):
        cols = slice(j * LANES, (j + 1) * LANES)
        foot = jnp.where(line == 0, total[:, cols], marks)
        own_ref[j, 0:half, :] = state[pl.ds(mine, half), cols]
        sent_ref[j, 0:half, :] = state[pl.ds(theirs, half), cols]
        own_ref[j, half:, :] = foot
        sent_ref[j, half:, :] = foot


def prepare_kernel(heads, docs_ref, b_ref, c_ref, col_ref, doc_row_ref, affinity_ref, entry_ref):
    t = lax.broadcasted_iota(jnp.int32, (BLOCK, BLOCK), 0)
    s = lax.broadcasted_iota(jnp.int32, (BLOCK, BLOCK), 1)
    lane = lax.broadcasted_iota(jnp.int32, (1, LANES), 1)
    for j in range(affinity_ref.shape[0]):
        piece = slice(j * BLOCK, (j + 1) * BLOCK)
        block = pl.program_id(0) * affinity_ref.shape[0] + j
        columns = col_ref[piece, :]
        doc_col = columns[:, LANES - 1 :]
        doc_row = doc_row_ref[:, piece].astype(F32)
        affinity_ref[j] = jnp.where(
            (t >= s) & (doc_col == doc_row),
            dot(c_ref[piece, :], b_ref[piece, :], ((1,), (1,))),
            0.0,
        )
        prior_doc = docs_ref[jnp.maximum(block * BLOCK - 1, 0)].astype(F32)
        linked = (doc_col == prior_doc) & (lane < heads)
        high, low = two_parts(jnp.where(linked, jnp.exp2(columns), 0.0))
        entry_ref[piece, 0:LANES] = high
        entry_ref[piece, LANES:] = low


def inner_kernel(
    width,
    first_tile,
    group,
    count,
    live_ref,
    docs_ref,
    x_ref,
    z_ref,
    c_ref,
    cum_ref,
    step_ref,
    col_ref,
    affinity_ref,
    entry_ref,
    enter_ref,
    row_ref,
    hot_ref,
    *refs,
):
    y_ref, f_ref = refs[-2:]
    k = pl.program_id(0)
    half = BLOCK // 2
    per_tile = LANES // width

    @pl.when(k >= live_ref[0])
    def _():
        y_ref[...] = jnp.zeros_like(y_ref)
        f_ref[...] = jnp.zeros_like(f_ref)

    @pl.when(k < live_ref[0])
    def _():
        readout = c_ref[...]
        lane = lax.broadcasted_iota(jnp.int32, (1, LANES), 1)
        nothing = jnp.zeros((BLOCK, LANES), BF16)
        reaches = jnp.where(docs_ref[jnp.maximum(k * BLOCK - 1, 0)] == docs_ref[0], 1.0, 0.0)
        passed = pick_row(row_ref, count, count, k, slice(None)) * reaches
        for q in range(x_ref.shape[1] // (group * LANES)):
            cols = slice(q * group * LANES, (q + 1) * group * LANES)
            x = x_ref[:, cols]
            tops, bottoms, masked = [], [], []
            for u in range(group):
                part = x[:, u * LANES : (u + 1) * LANES]
                for i in range(per_tile):
                    h = (first_tile + q * group + u) * per_tile + i
                    cum = jnp.broadcast_to(col_ref[:, h : h + 1], (BLOCK, LANES))
                    left, right = cum_ref[h : h + 1, :half], cum_ref[h : h + 1, half:]
                    early, late = step_ref[h : h + 1, :half], step_ref[h : h + 1, half:]
                    top = jnp.exp2(jnp.minimum(cum[:half] - left, 0.0))
                    bottom = jnp.exp2(jnp.minimum(cum[half:] - left, 0.0))
                    corner = jnp.exp2(jnp.minimum(cum[half:] - right, 0.0))
                    tops.append((affinity_ref[0, :half, :half] * top * early).astype(BF16))
                    bottoms.append((affinity_ref[0, half:, :half] * bottom * early).astype(BF16))
                    bottoms.append((affinity_ref[0, half:, half:] * corner * late).astype(BF16))
                    mine = (lane >= i * width) & (lane < (i + 1) * width)
                    kept = part * jnp.where(mine, 1.0, 0.0).astype(BF16)
                    masked.append(
                        jnp.concatenate(
                            [kept if v == u else nothing for v in range(group)], axis=1
                        )
                    )
            upper = dot(
                jnp.concatenate(tops, axis=1),
                jnp.concatenate([m[:half] for m in masked], axis=0),
            )
            lower = dot(jnp.concatenate(bottoms, axis=1), jnp.concatenate(masked, axis=0))
            hot = jnp.concatenate([hot_ref[:, cols]] * 2, axis=0)
            enter = dot(entry_ref[...], hot)
            outer = dot(readout, enter_ref[0, :, cols])
            skip = row_ref[2 * count + 1 : 2 * count + 2, cols]
            y = jnp.concatenate([upper, lower], axis=0) + enter * outer + skip * x.astype(F32)
            z = z_ref[:, cols].astype(F32)
            gate = z / (1.0 + jnp.exp2(-LOG2E * z))
            y_ref[:, cols] = y * gate
            f_ref[:, cols] = enter * gate * passed[:, cols]


def join_kernel(spot_ref, own_ref, other_ref, c_ref, *refs):
    pieces = (len(refs) - 3) // 2
    gated_ref, square_ref, total = refs[2 * pieces :]
    length = c_ref.shape[0]
    second = spot_ref[0] == 1
    total[...] = jnp.zeros_like(total)
    tile = 0
    for y_ref, f_ref in zip(refs[:pieces], refs[pieces : 2 * pieces]):
        wide = chunk_of(y_ref.shape[1], 4 * LANES)
        for c in range(0, y_ref.shape[1], wide):
            parts = []
            for j in range(tile, tile + wide // LANES):
                own, other = own_ref[j].astype(BF16), other_ref[j].astype(BF16)
                parts.append(
                    jnp.concatenate(
                        [jnp.where(second, other, own), jnp.where(second, own, other)], axis=0
                    )
                )
            carry = jnp.concatenate(parts, axis=1)
            for r in range(0, length, BLOCK):
                rows = slice(r, r + BLOCK)
                outer = dot(c_ref[rows, :], carry)
                gated = y_ref[rows, c : c + wide] + f_ref[rows, c : c + wide] * outer
                gated_ref[rows, tile * LANES : tile * LANES + wide] = gated
                square = total[rows, :]
                for j in range(0, wide, LANES):
                    square = square + gated[:, j : j + LANES] * gated[:, j : j + LANES]
                total[rows, :] = square
            tile += wide // LANES
    square_ref[...] = jnp.sum(total[...].T, axis=0, keepdims=True)


def norm_kernel(channels_all, square_ref, more_ref, gain_ref, gated_ref, out_ref):
    rows = out_ref.shape[0]
    start = pl.multiple_of(pl.program_id(0) * rows, rows)
    scale = lax.rsqrt((square_ref[...] + more_ref[...]) / channels_all + 1e-05)
    scale = jnp.broadcast_to(scale, (LANES, rows)).T
    for j in range(gated_ref.shape[1] // LANES):
        cols = slice(j * LANES, (j + 1) * LANES)
        gated = gated_ref[pl.ds(start, rows), cols]
        out_ref[:, cols] = (gated * gain_ref[:, cols] * scale).astype(BF16)


def chunk_of(total, most):
    wide = most
    while total % wide:
        wide -= LANES
    return wide


def whole(shape):
    return pl.BlockSpec(shape, lambda k, *_: (0,) * len(shape))


def in_hbm(*values):
    return [pltpu.with_memory_space_constraint(value, pltpu.HBM) for value in values]


SMEM = pl.BlockSpec(memory_space=pltpu.SMEM)
VMEM = pl.BlockSpec(memory_space=pltpu.VMEM)


def plan(chips, tiles):
    chunks = min(CHUNKS, tiles)
    size = -(-tiles // chunks)
    starts = tuple(min(c * size, tiles - size) for c in range(chunks))
    pieces = (tiles,)
    if tiles % 10 == 0:
        pieces = (3 * tiles // 10,) * 2 + (tiles // 5,) * 2
    return starts, size, chunks + chips - 2, pieces


def on_device(
    token_values,
    gate_values,
    state_input,
    state_readout,
    step_raw,
    step_bias,
    decay_log,
    skip_gain,
    norm_gain,
    document_ids,
    live_blocks,
):
    length, channels = token_values.shape
    heads = step_raw.shape[0]
    width = channels // heads
    states = state_input.shape[1]
    half = states // 2
    count = length // BLOCK
    tiles = channels // LANES
    rows = -(-heads // 8) * 8
    scalars = -(-(2 * count + 2) // 16) * 16
    assert lax.axis_size("sub") == 2 and 2 * rows < LANES and states == LANES

    raw = step_raw
    if rows != heads:
        raw = jnp.pad(raw, ((0, rows - heads), (0, 0)))
    doc_row = document_ids.reshape(1, length)
    spot = jnp.stack([lax.axis_index("sub"), lax.axis_index("seq")]).astype(jnp.int32)
    head_of = np.arange(channels)[None, :] // width
    lanes = np.arange(LANES)[:, None]
    hot = jnp.asarray(lanes == head_of, dtype=BF16)
    hot_low = jnp.asarray(lanes == head_of + rows, dtype=BF16)
    tri = jnp.asarray(np.triu(np.ones((BLOCK, BLOCK))), dtype=BF16)

    chunk = chunk_of(channels, 512)
    per_chunk = chunk // LANES
    cum, step, col, enter, own, sent, row = pl.pallas_call(
        functools.partial(state_kernel, heads),
        grid=(channels // chunk,),
        in_specs=[
            SMEM,
            SMEM,
            SMEM,
            whole((rows, length)),
            whole((1, heads)),
            whole((1, heads)),
            whole((1, heads)),
            whole((1, length)),
            whole((BLOCK, BLOCK)),
            pl.BlockSpec((LANES, chunk), lambda c: (0, c)),
            pl.BlockSpec((LANES, chunk), lambda c: (0, c)),
            pl.BlockSpec((length, chunk), lambda c: (0, c)),
            whole((length, states)),
        ],
        out_specs=[
            whole((rows, length)),
            whole((rows, length)),
            whole((length, LANES)),
            pl.BlockSpec((count, states, chunk), lambda c: (0, 0, c)),
            pl.BlockSpec((per_chunk, half + 8, LANES), lambda c: (c, 0, 0)),
            pl.BlockSpec((per_chunk, half + 8, LANES), lambda c: (c, 0, 0)),
            pl.BlockSpec((scalars, chunk), lambda c: (0, c)),
        ],
        out_shape=[
            jax.ShapeDtypeStruct((rows, length), F32),
            jax.ShapeDtypeStruct((rows, length), F32),
            jax.ShapeDtypeStruct((length, LANES), F32),
            jax.ShapeDtypeStruct((count, states, channels), BF16),
            jax.ShapeDtypeStruct((tiles, half + 8, LANES), F32),
            jax.ShapeDtypeStruct((tiles, half + 8, LANES), F32),
            jax.ShapeDtypeStruct((scalars, channels), F32),
        ],
        scratch_shapes=[
            pltpu.VMEM((LANES, length), F32),
            pltpu.VMEM((length, 2 * LANES), BF16),
            pltpu.VMEM((states, length), BF16),
            pltpu.VMEM((states, chunk), F32),
            pltpu.VMEM((scalars, LANES), F32),
        ],
        compiler_params=pltpu.CompilerParams(vmem_limit_bytes=EARLY_VMEM),
        name="shard_state",
    )(
        live_blocks,
        document_ids,
        spot,
        *in_hbm(
            raw,
            step_bias.reshape(1, heads),
            decay_log.reshape(1, heads),
            skip_gain.reshape(1, heads),
            doc_row,
            tri,
            hot,
            hot_low,
            token_values,
            state_input,
        ),
    )

    span = 2 if count % 2 == 0 else 1
    affinity, entry = pl.pallas_call(
        functools.partial(prepare_kernel, heads),
        grid=(count // span,),
        in_specs=[
            SMEM,
            pl.BlockSpec((span * BLOCK, states), lambda k: (k, 0)),
            pl.BlockSpec((span * BLOCK, states), lambda k: (k, 0)),
            pl.BlockSpec((span * BLOCK, LANES), lambda k: (k, 0)),
            pl.BlockSpec((1, span * BLOCK), lambda k: (0, k)),
        ],
        out_specs=[
            pl.BlockSpec((span, BLOCK, BLOCK), lambda k: (k, 0, 0)),
            pl.BlockSpec((span * BLOCK, 2 * LANES), lambda k: (k, 0)),
        ],
        out_shape=[
            jax.ShapeDtypeStruct((count, BLOCK, BLOCK), F32),
            jax.ShapeDtypeStruct((length, 2 * LANES), BF16),
        ],
        compiler_params=pltpu.CompilerParams(vmem_limit_bytes=EARLY_VMEM),
        name="prepare",
    )(document_ids, *in_hbm(state_input, state_readout), col, doc_row)

    pieces = plan(lax.axis_size("seq"), tiles)[3]
    group = 2 if tiles % 2 == 0 else 1
    ys, fs, at = [], [], 0
    x, z, readout, heads_hot = in_hbm(token_values, gate_values, state_readout, hot)
    inputs = (x, z, readout, cum, step, col, affinity, entry, enter, row, heads_hot)
    for size in pieces:
        wide, first = size * LANES, at // size
        y, f = pl.pallas_call(
            functools.partial(inner_kernel, width, at, group, count),
            grid=(count,),
            in_specs=[
                SMEM,
                SMEM,
                pl.BlockSpec((BLOCK, wide), lambda k, q=first: (k, q)),
                pl.BlockSpec((BLOCK, wide), lambda k, q=first: (k, q)),
                pl.BlockSpec((BLOCK, states), lambda k: (k, 0)),
                pl.BlockSpec((rows, BLOCK), lambda k: (0, k)),
                pl.BlockSpec((rows, BLOCK), lambda k: (0, k)),
                pl.BlockSpec((BLOCK, LANES), lambda k: (k, 0)),
                pl.BlockSpec((1, BLOCK, BLOCK), lambda k: (k, 0, 0)),
                pl.BlockSpec((BLOCK, 2 * LANES), lambda k: (k, 0)),
                pl.BlockSpec((1, states, wide), lambda k, q=first: (k, 0, q)),
                pl.BlockSpec((scalars, wide), lambda k, q=first: (0, q)),
                pl.BlockSpec((LANES, wide), lambda k, q=first: (0, q)),
            ],
            out_specs=[pl.BlockSpec((BLOCK, wide), lambda k: (k, 0))] * 2,
            out_shape=[
                jax.ShapeDtypeStruct((length, wide), F32),
                jax.ShapeDtypeStruct((length, wide), F32),
            ],
            cost_estimate=pl.CostEstimate(
                flops=length * wide * 1200,
                bytes_accessed=length * wide * 10,
                transcendentals=0,
            ),
            compiler_params=pltpu.CompilerParams(vmem_limit_bytes=INNER_VMEM),
        )(live_blocks, document_ids, *inputs)
        ys.append(y)
        fs.append(f)
        at += size

    own, other = carry_in(own, sent, half)

    gated, squares = pl.pallas_call(
        join_kernel,
        in_specs=[SMEM] + [VMEM] * (3 + 2 * len(pieces)),
        out_specs=[VMEM, VMEM],
        out_shape=[
            jax.ShapeDtypeStruct((length, channels), F32),
            jax.ShapeDtypeStruct((1, length), F32),
        ],
        scratch_shapes=[pltpu.VMEM((length, LANES), F32)],
        compiler_params=pltpu.CompilerParams(vmem_limit_bytes=16 << 20),
        name="join",
    )(spot, own, other, state_readout, *ys, *fs)

    squares, more = summed(squares, "head")
    return pl.pallas_call(
        functools.partial(norm_kernel, channels * lax.axis_size("head")),
        grid=(count,),
        in_specs=[
            pl.BlockSpec((1, BLOCK), lambda k: (0, k)),
            pl.BlockSpec((1, BLOCK), lambda k: (0, k)),
            whole((1, channels)),
            VMEM,
        ],
        out_specs=pl.BlockSpec((BLOCK, channels), lambda k: (k, 0)),
        out_shape=jax.ShapeDtypeStruct((length, channels), BF16),
        compiler_params=pltpu.CompilerParams(vmem_limit_bytes=16 << 20),
        name="norm",
    )(squares, more, norm_gain.reshape(1, channels), gated)


def summed(value, axis):
    size = lax.axis_size(axis)
    if size & (size - 1):
        total = value
        for shift in range(1, size):
            total = total + lax.ppermute(value, axis, [(i, (i + shift) % size) for i in range(size)])
        return total, jnp.zeros_like(value)
    more, shift = jnp.zeros_like(value), 1
    while shift < size:
        value = value + more if shift > 1 else value
        more = lax.ppermute(value, axis, [(i, i ^ shift) for i in range(size)])
        shift *= 2
    return value, more


def carry_in(own, sent, half):
    tiles = own.shape[0]
    chips = lax.axis_size("seq")
    second, place = own[0, half + 3] == 1.0, own[0, half + 4]
    got = lax.ppermute(sent, "sub", [(0, 1), (1, 0)])
    early = jnp.where(second, got, own)
    late = jnp.where(second, own, got)
    first, last = early[0, half + 1], late[0, half + 2]
    link = jnp.where(early[0, half + 2] == late[0, half + 1], 1.0, 0.0)
    early_decay, late_decay = early[:, half : half + 1], late[:, half : half + 1] * link
    early, late = early[:, :half], late[:, :half]
    chip_state = late_decay * early + late
    chip_decay = late_decay * early_decay

    starts, size, hops, _ = plan(chips, tiles)
    rows = size * half
    tail = jnp.broadcast_to(last, (8, LANES))

    def at(array, t):
        part = array[starts[0] : starts[0] + size]
        for c in range(1, len(starts)):
            part = jnp.where(place <= t - c, array[starts[c] : starts[c] + size], part)
        return part

    carry = jnp.zeros((size, half, LANES), F32)
    received = []
    for t in range(hops):
        send = at(chip_decay, t) * carry + at(chip_state, t)
        send = jnp.concatenate([send.reshape(rows, LANES), tail], axis=0)
        pairs = [(z, z + 1) for z in range(chips - 1) if 0 <= t - z < len(starts)]
        got = lax.ppermute(send, "seq", pairs)
        joined = jnp.where(got[rows] == first, 1.0, 0.0)
        carry = joined * got[:rows].reshape(size, half, LANES)
        received.append(carry)
    parts, done = [], 0
    for c, start in enumerate(starts):
        part = jnp.zeros((size, half, LANES), F32)
        for z in range(1, chips):
            part = jnp.where(place == z, received[c + z - 1], part)
        parts.append(part[done - start :])
        done = start + size
    entering = jnp.concatenate(parts, axis=0)
    onward = link * (early_decay * entering + early)
    mine = jnp.where(second, onward, entering)
    other = lax.ppermute(jnp.where(second, entering, onward), "sub", [(0, 1), (1, 0)])
    return mine, other


def solution(mesh):
    placed = (
        P(("groups", "seq", "sub"), "head"),
        P(("groups", "seq", "sub"), "head"),
        P(("groups", "seq", "sub"), None),
        P(("groups", "seq", "sub"), None),
        P("head", ("seq", "sub")),
        P("head"),
        P("head"),
        P("head"),
        P("head"),
        P(("groups", "seq", "sub")),
        P(("groups", "seq", "sub")),
    )

    return jax.shard_map(
        on_device,
        mesh=mesh,
        in_specs=placed,
        out_specs=P(("groups", "seq", "sub"), "head"),
        check_vma=False,
    )
```

```python
import functools
import math

import jax
import jax.numpy as jnp
import numpy as np
from jax import lax
from jax.experimental import pallas as pl
from jax.experimental.pallas import tpu as pltpu
from jax.sharding import PartitionSpec as P

BLOCK = 256
LANES = 128
LOG2E = math.log2(math.e)
CHUNKS = 2
INNER_VMEM = 16 << 20
EARLY_VMEM = 32 << 20
F32 = jnp.float32
BF16 = jnp.bfloat16


def dot(a, b, contract=((1,), (0,))):
    return lax.dot_general(a, b, (contract, ((), ())), preferred_element_type=F32)


def two_parts(value):
    high = value.astype(BF16)
    low = (value - high.astype(F32)).astype(BF16)
    return high, low


def pick_row(ref, base, count, k, cols):
    row = ref[base : base + 1, cols]
    for j in range(1, count):
        row = jnp.where(k == j, ref[base + j : base + j + 1, cols], row)
    return row


def softplus(v):
    u = jnp.exp(-jnp.abs(v))
    s = u / (2.0 + u)
    q = s * s
    series = jnp.full_like(q, 1.0 / 15.0)
    for odd in (13, 11, 9, 7, 5, 3, 1):
        series = series * q + 1.0 / odd
    return jnp.maximum(v, 0.0) + 2.0 * s * series


def state_kernel(
    heads,
    live_ref,
    docs_ref,
    spot_ref,
    raw_ref,
    bias_ref,
    decay_ref,
    skip_ref,
    doc_row_ref,
    tri_ref,
    hot_ref,
    hot_low_ref,
    x_ref,
    b_ref,
    cum_ref,
    step_ref,
    col_ref,
    enter_ref,
    own_ref,
    sent_ref,
    row_ref,
    pack,
    col_parts,
    inputs_t,
    state,
    scal,
    x_parts,
    x_sems,
):
    rows, length = raw_ref.shape
    count = length // BLOCK
    wide = hot_ref.shape[1]
    step_at, slot = pl.program_id(0), lax.rem(pl.program_id(0), 2)

    def fetch(at, into):
        cols = pl.ds(pl.multiple_of(at * wide, LANES), wide)
        return pltpu.make_async_copy(x_ref.at[:, cols], x_parts.at[into], x_sems.at[into])

    @pl.when(step_at == 0)
    def _():
        fetch(0, 0).start()

    ends = [docs_ref[j * BLOCK + BLOCK - 1] for j in range(count)]

    @pl.when(pl.program_id(0) == 0)
    def _():
        inputs_t[...] = b_ref[...].T
        pack[...] = jnp.zeros_like(pack)
        pack[0:1, 0:heads] = bias_ref[...]
        pack[1:2, 0:heads] = decay_ref[...]
        params = pack[0:LANES, 0:LANES].T
        lane = lax.broadcasted_iota(jnp.int32, (1, length), 1)
        step = softplus(raw_ref[...] + params[0:rows, 0:1])
        step = jnp.where(lane < live_ref[0] * BLOCK, step, 0.0)
        rate = (-LOG2E * jnp.exp(params[0:rows, 1:2])) * step
        high, _ = two_parts(rate)
        middle, low = two_parts(rate - high.astype(F32))
        tri = tri_ref[...]
        step_ref[...] = step
        for j in range(count):
            piece = slice(j * BLOCK, (j + 1) * BLOCK)
            cum = dot(high[:, piece], tri) + (dot(middle[:, piece], tri) + dot(low[:, piece], tri))
            cum_ref[:, piece] = cum
            same = doc_row_ref[:, piece] == ends[j]
            pack[0:rows, piece] = cum
            pack[rows : 2 * rows, piece] = jnp.where(
                same, step[:, piece] * jnp.exp2(cum[:, BLOCK - 1 :] - cum), 0.0
            )
        pack[LANES - 1 : LANES, :] = doc_row_ref[...].astype(F32)
        for j in range(count):
            piece = slice(j * BLOCK, (j + 1) * BLOCK)
            turned = pack[:, piece].T
            col_ref[piece, :] = turned
            high, low = two_parts(turned)
            col_parts[piece, 0:LANES] = high
            col_parts[piece, LANES:] = low
        head_lane = lax.broadcasted_iota(jnp.int32, (1, LANES), 1) < heads
        before = jnp.zeros((1, LANES), F32)
        scal[...] = jnp.zeros_like(scal)
        for j in range(count):
            end = jnp.where(head_lane, col_ref[(j + 1) * BLOCK - 1 : (j + 1) * BLOCK, :], 0.0)
            scal[j : j + 1, :] = jnp.where(head_lane, jnp.exp2(end), 0.0)
            scal[count + j : count + j + 1, :] = jnp.where(head_lane, jnp.exp2(before), 0.0)
            before = before + end
        scal[2 * count : 2 * count + 1, :] = jnp.where(head_lane, jnp.exp2(before), 0.0)
        scal[2 * count + 1 : 2 * count + 2, 0:heads] = skip_ref[...]

    @pl.when(step_at + 1 < pl.num_programs(0))
    def _():
        fetch(step_at + 1, 1 - slot).start()

    hot = hot_ref[...]
    high, low = two_parts(scal[...])
    row = dot(high, hot) + dot(low, hot)
    row_ref[...] = row
    hot_low = jnp.concatenate([hot_low_ref[...]] * 2, axis=0)
    state[...] = jnp.zeros_like(state)
    fetch(step_at, slot).wait()
    scaled = (x_parts[slot].astype(F32) * dot(col_parts[...], hot_low)).astype(BF16)
    for j in range(count):
        piece = slice(j * BLOCK, (j + 1) * BLOCK)
        prior = docs_ref[max(j * BLOCK - 1, 0)]
        passage = row[j : j + 1, :] * jnp.where(ends[j] == prior, 1.0, 0.0)
        old = state[...]
        enter_ref[j] = old.astype(BF16)
        state[...] = passage * old + dot(inputs_t[:, piece], scaled[piece])

    half = state.shape[0] // 2
    total = row[2 * count : 2 * count + 1, :] * jnp.where(ends[count - 1] == docs_ref[0], 1.0, 0.0)
    mine = pl.multiple_of(spot_ref[0] * half, half)
    theirs = pl.multiple_of((1 - spot_ref[0]) * half, half)
    line = lax.broadcasted_iota(jnp.int32, (8, LANES), 0)
    marks = jnp.zeros((8, LANES), F32)
    for at, mark in enumerate((docs_ref[0], docs_ref[length - 1], spot_ref[0], spot_ref[1])):
        marks = jnp.where(line == at + 1, mark.astype(F32), marks)
    for j in range(wide // LANES):
        cols = slice(j * LANES, (j + 1) * LANES)
        foot = jnp.where(line == 0, total[:, cols], marks)
        own_ref[j, 0:half, :] = state[pl.ds(mine, half), cols]
        sent_ref[j, 0:half, :] = state[pl.ds(theirs, half), cols]
        own_ref[j, half:, :] = foot
        sent_ref[j, half:, :] = foot


def prepare_kernel(heads, docs_ref, b_ref, c_ref, col_ref, doc_row_ref, affinity_ref, entry_ref):
    t = lax.broadcasted_iota(jnp.int32, (BLOCK, BLOCK), 0)
    s = lax.broadcasted_iota(jnp.int32, (BLOCK, BLOCK), 1)
    lane = lax.broadcasted_iota(jnp.int32, (1, LANES), 1)
    for j in range(affinity_ref.shape[0]):
        piece = slice(j * BLOCK, (j + 1) * BLOCK)
        block = pl.program_id(0) * affinity_ref.shape[0] + j
        columns = col_ref[piece, :]
        doc_col = columns[:, LANES - 1 :]
        doc_row = doc_row_ref[:, piece].astype(F32)
        affinity_ref[j] = jnp.where(
            (t >= s) & (doc_col == doc_row),
            dot(c_ref[piece, :], b_ref[piece, :], ((1,), (1,))),
            0.0,
        )
        prior_doc = docs_ref[jnp.maximum(block * BLOCK - 1, 0)].astype(F32)
        linked = (doc_col == prior_doc) & (lane < heads)
        high, low = two_parts(jnp.where(linked, jnp.exp2(columns), 0.0))
        entry_ref[piece, 0:LANES] = high
        entry_ref[piece, LANES:] = low


def inner_kernel(
    width,
    first_tile,
    group,
    count,
    live_ref,
    docs_ref,
    x_ref,
    z_ref,
    c_ref,
    cum_ref,
    step_ref,
    col_ref,
    affinity_ref,
    entry_ref,
    enter_ref,
    row_ref,
    hot_ref,
    *refs,
):
    y_ref, f_ref = refs[-2:]
    k = pl.program_id(0)
    half = BLOCK // 2
    per_tile = LANES // width

    @pl.when(k >= live_ref[0])
    def _():
        y_ref[...] = jnp.zeros_like(y_ref)
        f_ref[...] = jnp.zeros_like(f_ref)

    @pl.when(k < live_ref[0])
    def _():
        readout = c_ref[...]
        lane = lax.broadcasted_iota(jnp.int32, (1, LANES), 1)
        nothing = jnp.zeros((BLOCK, LANES), BF16)
        reaches = jnp.where(docs_ref[jnp.maximum(k * BLOCK - 1, 0)] == docs_ref[0], 1.0, 0.0)
        passed = pick_row(row_ref, count, count, k, slice(None)) * reaches
        for q in range(x_ref.shape[1] // (group * LANES)):
            cols = slice(q * group * LANES, (q + 1) * group * LANES)
            x = x_ref[:, cols]
            tops, bottoms, masked = [], [], []
            for u in range(group):
                part = x[:, u * LANES : (u + 1) * LANES]
                for i in range(per_tile):
                    h = (first_tile + q * group + u) * per_tile + i
                    cum = jnp.broadcast_to(col_ref[:, h : h + 1], (BLOCK, LANES))
                    left, right = cum_ref[h : h + 1, :half], cum_ref[h : h + 1, half:]
                    early, late = step_ref[h : h + 1, :half], step_ref[h : h + 1, half:]
                    top = jnp.exp2(jnp.minimum(cum[:half] - left, 0.0))
                    bottom = jnp.exp2(jnp.minimum(cum[half:] - left, 0.0))
                    corner = jnp.exp2(jnp.minimum(cum[half:] - right, 0.0))
                    tops.append((affinity_ref[0, :half, :half] * top * early).astype(BF16))
                    bottoms.append((affinity_ref[0, half:, :half] * bottom * early).astype(BF16))
                    bottoms.append((affinity_ref[0, half:, half:] * corner * late).astype(BF16))
                    mine = (lane >= i * width) & (lane < (i + 1) * width)
                    kept = part * jnp.where(mine, 1.0, 0.0).astype(BF16)
                    masked.append(
                        jnp.concatenate(
                            [kept if v == u else nothing for v in range(group)], axis=1
                        )
                    )
            upper = dot(
                jnp.concatenate(tops, axis=1),
                jnp.concatenate([m[:half] for m in masked], axis=0),
            )
            lower = dot(jnp.concatenate(bottoms, axis=1), jnp.concatenate(masked, axis=0))
            hot = jnp.concatenate([hot_ref[:, cols]] * 2, axis=0)
            enter = dot(entry_ref[...], hot)
            outer = dot(readout, enter_ref[0, :, cols])
            skip = row_ref[2 * count + 1 : 2 * count + 2, cols]
            y = jnp.concatenate([upper, lower], axis=0) + enter * outer + skip * x.astype(F32)
            z = z_ref[:, cols].astype(F32)
            gate = z / (1.0 + jnp.exp2(-LOG2E * z))
            y_ref[:, cols] = y * gate
            f_ref[:, cols] = enter * gate * passed[:, cols]


def join_kernel(spot_ref, own_ref, other_ref, c_ref, *refs):
    pieces = (len(refs) - 3) // 2
    gated_ref, square_ref, total = refs[2 * pieces :]
    length = c_ref.shape[0]
    second = spot_ref[0] == 1
    total[...] = jnp.zeros_like(total)
    tile = 0
    for y_ref, f_ref in zip(refs[:pieces], refs[pieces : 2 * pieces]):
        wide = chunk_of(y_ref.shape[1], 4 * LANES)
        for c in range(0, y_ref.shape[1], wide):
            parts = []
            for j in range(tile, tile + wide // LANES):
                own, other = own_ref[j].astype(BF16), other_ref[j].astype(BF16)
                parts.append(
                    jnp.concatenate(
                        [jnp.where(second, other, own), jnp.where(second, own, other)], axis=0
                    )
                )
            carry = jnp.concatenate(parts, axis=1)
            for r in range(0, length, BLOCK):
                rows = slice(r, r + BLOCK)
                outer = dot(c_ref[rows, :], carry)
                gated = y_ref[rows, c : c + wide] + f_ref[rows, c : c + wide] * outer
                gated_ref[rows, tile * LANES : tile * LANES + wide] = gated
                square = total[rows, :]
                for j in range(0, wide, LANES):
                    square = square + gated[:, j : j + LANES] * gated[:, j : j + LANES]
                total[rows, :] = square
            tile += wide // LANES
    square_ref[...] = jnp.sum(total[...].T, axis=0, keepdims=True)


def norm_kernel(
    channels_all, square_ref, more_ref, gain_ref, gated_ref, out_ref, stage, scale, sems
):
    length = gated_ref.shape[0]
    row = lax.rsqrt((square_ref[...] + more_ref[...]) / channels_all + 1e-05)
    copies = []
    for b in range(length // LANES):
        block = slice(b * LANES, (b + 1) * LANES)
        scale[...] = jnp.broadcast_to(row[:, block], (LANES, LANES)).T
        for r in range(0, LANES, 16):
            rows = slice(b * LANES + r, b * LANES + r + 16)
            part = scale[r : r + 16, :]
            for j in range(0, gated_ref.shape[1], LANES):
                cols = slice(j, j + LANES)
                stage[rows, cols] = (gated_ref[rows, cols] * gain_ref[:, cols] * part).astype(BF16)
        copies.append(pltpu.make_async_copy(stage.at[block], out_ref.at[block], sems.at[b]))
        copies[-1].start()
    for copy in copies:
        copy.wait()


def chunk_of(total, most):
    wide = most
    while total % wide:
        wide -= LANES
    return wide


def whole(shape):
    return pl.BlockSpec(shape, lambda k, *_: (0,) * len(shape))


def in_hbm(*values):
    return [pltpu.with_memory_space_constraint(value, pltpu.HBM) for value in values]


SMEM = pl.BlockSpec(memory_space=pltpu.SMEM)
VMEM = pl.BlockSpec(memory_space=pltpu.VMEM)


def plan(chips, tiles):
    chunks = min(CHUNKS, tiles)
    size = -(-tiles // chunks)
    starts = tuple(min(c * size, tiles - size) for c in range(chunks))
    pieces = (tiles,)
    if tiles % 10 == 0:
        pieces = (3 * tiles // 10,) * 2 + (tiles // 5,) * 2
    return starts, size, chunks + chips - 2, pieces


def on_device(
    token_values,
    gate_values,
    state_input,
    state_readout,
    step_raw,
    step_bias,
    decay_log,
    skip_gain,
    norm_gain,
    document_ids,
    live_blocks,
):
    length, channels = token_values.shape
    heads = step_raw.shape[0]
    width = channels // heads
    states = state_input.shape[1]
    half = states // 2
    count = length // BLOCK
    tiles = channels // LANES
    rows = -(-heads // 8) * 8
    scalars = -(-(2 * count + 2) // 16) * 16
    assert lax.axis_size("sub") == 2 and 2 * rows < LANES and states == LANES

    raw = step_raw
    if rows != heads:
        raw = jnp.pad(raw, ((0, rows - heads), (0, 0)))
    doc_row = document_ids.reshape(1, length)
    spot = jnp.stack([lax.axis_index("sub"), lax.axis_index("seq")]).astype(jnp.int32)
    head_of = np.arange(channels)[None, :] // width
    lanes = np.arange(LANES)[:, None]
    hot = jnp.asarray(lanes == head_of, dtype=BF16)
    hot_low = jnp.asarray(lanes == head_of + rows, dtype=BF16)
    tri = jnp.asarray(np.triu(np.ones((BLOCK, BLOCK))), dtype=BF16)

    chunk = chunk_of(channels, 512)
    per_chunk = chunk // LANES
    cum, step, col, enter, own, sent, row = pl.pallas_call(
        functools.partial(state_kernel, heads),
        grid=(channels // chunk,),
        in_specs=[
            SMEM,
            SMEM,
            SMEM,
            whole((rows, length)),
            whole((1, heads)),
            whole((1, heads)),
            whole((1, heads)),
            whole((1, length)),
            whole((BLOCK, BLOCK)),
            pl.BlockSpec((LANES, chunk), lambda c: (0, c)),
            pl.BlockSpec((LANES, chunk), lambda c: (0, c)),
            pl.BlockSpec(memory_space=pl.ANY),
            whole((length, states)),
        ],
        out_specs=[
            whole((rows, length)),
            whole((rows, length)),
            whole((length, LANES)),
            pl.BlockSpec((count, states, chunk), lambda c: (0, 0, c)),
            pl.BlockSpec((per_chunk, half + 8, LANES), lambda c: (c, 0, 0)),
            pl.BlockSpec((per_chunk, half + 8, LANES), lambda c: (c, 0, 0)),
            pl.BlockSpec((scalars, chunk), lambda c: (0, c)),
        ],
        out_shape=[
            jax.ShapeDtypeStruct((rows, length), F32),
            jax.ShapeDtypeStruct((rows, length), F32),
            jax.ShapeDtypeStruct((length, LANES), F32),
            jax.ShapeDtypeStruct((count, states, channels), BF16),
            jax.ShapeDtypeStruct((tiles, half + 8, LANES), F32),
            jax.ShapeDtypeStruct((tiles, half + 8, LANES), F32),
            jax.ShapeDtypeStruct((scalars, channels), F32),
        ],
        scratch_shapes=[
            pltpu.VMEM((LANES, length), F32),
            pltpu.VMEM((length, 2 * LANES), BF16),
            pltpu.VMEM((states, length), BF16),
            pltpu.VMEM((states, chunk), F32),
            pltpu.VMEM((scalars, LANES), F32),
            pltpu.VMEM((2, length, chunk), BF16),
            pltpu.SemaphoreType.DMA((2,)),
        ],
        compiler_params=pltpu.CompilerParams(vmem_limit_bytes=EARLY_VMEM),
        name="shard_state",
    )(
        live_blocks,
        document_ids,
        spot,
        *in_hbm(
            raw,
            step_bias.reshape(1, heads),
            decay_log.reshape(1, heads),
            skip_gain.reshape(1, heads),
            doc_row,
            tri,
            hot,
            hot_low,
            token_values,
            state_input,
        ),
    )

    span = 2 if count % 2 == 0 else 1
    affinity, entry = pl.pallas_call(
        functools.partial(prepare_kernel, heads),
        grid=(count // span,),
        in_specs=[
            SMEM,
            pl.BlockSpec((span * BLOCK, states), lambda k: (k, 0)),
            pl.BlockSpec((span * BLOCK, states), lambda k: (k, 0)),
            pl.BlockSpec((span * BLOCK, LANES), lambda k: (k, 0)),
            pl.BlockSpec((1, span * BLOCK), lambda k: (0, k)),
        ],
        out_specs=[
            pl.BlockSpec((span, BLOCK, BLOCK), lambda k: (k, 0, 0)),
            pl.BlockSpec((span * BLOCK, 2 * LANES), lambda k: (k, 0)),
        ],
        out_shape=[
            jax.ShapeDtypeStruct((count, BLOCK, BLOCK), F32),
            jax.ShapeDtypeStruct((length, 2 * LANES), BF16),
        ],
        compiler_params=pltpu.CompilerParams(vmem_limit_bytes=EARLY_VMEM),
        name="prepare",
    )(document_ids, *in_hbm(state_input, state_readout), col, doc_row)

    pieces = plan(lax.axis_size("seq"), tiles)[3]
    group = 2 if tiles % 2 == 0 else 1
    ys, fs, at = [], [], 0
    x, z, readout, heads_hot = in_hbm(token_values, gate_values, state_readout, hot)
    inputs = (x, z, readout, cum, step, col, affinity, entry, enter, row, heads_hot)
    for size in pieces:
        wide, first = size * LANES, at // size
        y, f = pl.pallas_call(
            functools.partial(inner_kernel, width, at, group, count),
            grid=(count,),
            in_specs=[
                SMEM,
                SMEM,
                pl.BlockSpec((BLOCK, wide), lambda k, q=first: (k, q)),
                pl.BlockSpec((BLOCK, wide), lambda k, q=first: (k, q)),
                pl.BlockSpec((BLOCK, states), lambda k: (k, 0)),
                pl.BlockSpec((rows, BLOCK), lambda k: (0, k)),
                pl.BlockSpec((rows, BLOCK), lambda k: (0, k)),
                pl.BlockSpec((BLOCK, LANES), lambda k: (k, 0)),
                pl.BlockSpec((1, BLOCK, BLOCK), lambda k: (k, 0, 0)),
                pl.BlockSpec((BLOCK, 2 * LANES), lambda k: (k, 0)),
                pl.BlockSpec((1, states, wide), lambda k, q=first: (k, 0, q)),
                pl.BlockSpec((scalars, wide), lambda k, q=first: (0, q)),
                pl.BlockSpec((LANES, wide), lambda k, q=first: (0, q)),
            ],
            out_specs=[pl.BlockSpec((BLOCK, wide), lambda k: (k, 0))] * 2,
            out_shape=[
                jax.ShapeDtypeStruct((length, wide), F32),
                jax.ShapeDtypeStruct((length, wide), F32),
            ],
            cost_estimate=pl.CostEstimate(
                flops=length * wide * 1200,
                bytes_accessed=length * wide * 10,
                transcendentals=0,
            ),
            compiler_params=pltpu.CompilerParams(vmem_limit_bytes=INNER_VMEM),
        )(live_blocks, document_ids, *inputs)
        ys.append(y)
        fs.append(f)
        at += size

    own, other = carry_in(own, sent, half)

    gated, squares = pl.pallas_call(
        join_kernel,
        in_specs=[SMEM] + [VMEM] * (3 + 2 * len(pieces)),
        out_specs=[VMEM, VMEM],
        out_shape=[
            jax.ShapeDtypeStruct((length, channels), F32),
            jax.ShapeDtypeStruct((1, length), F32),
        ],
        scratch_shapes=[pltpu.VMEM((length, LANES), F32)],
        compiler_params=pltpu.CompilerParams(vmem_limit_bytes=16 << 20),
        name="join",
    )(spot, own, other, state_readout, *ys, *fs)

    squares, more = summed(squares, "head")
    return pl.pallas_call(
        functools.partial(norm_kernel, channels * lax.axis_size("head")),
        in_specs=[VMEM] * 4,
        out_specs=pl.BlockSpec(memory_space=pl.ANY),
        out_shape=jax.ShapeDtypeStruct((length, channels), BF16),
        scratch_shapes=[
            pltpu.VMEM((length, channels), BF16),
            pltpu.VMEM((LANES, LANES), F32),
            pltpu.SemaphoreType.DMA((length // LANES,)),
        ],
        compiler_params=pltpu.CompilerParams(vmem_limit_bytes=16 << 20),
        name="norm",
    )(squares, more, norm_gain.reshape(1, channels), gated)


def summed(value, axis):
    size = lax.axis_size(axis)
    if size & (size - 1):
        total = value
        for shift in range(1, size):
            total = total + lax.ppermute(value, axis, [(i, (i + shift) % size) for i in range(size)])
        return total, jnp.zeros_like(value)
    more, shift = jnp.zeros_like(value), 1
    while shift < size:
        value = value + more if shift > 1 else value
        more = lax.ppermute(value, axis, [(i, i ^ shift) for i in range(size)])
        shift *= 2
    return value, more


def carry_in(own, sent, half):
    tiles = own.shape[0]
    chips = lax.axis_size("seq")
    second, place = own[0, half + 3] == 1.0, own[0, half + 4]
    got = lax.ppermute(sent, "sub", [(0, 1), (1, 0)])
    early = jnp.where(second, got, own)
    late = jnp.where(second, own, got)
    first, last = early[0, half + 1], late[0, half + 2]
    link = jnp.where(early[0, half + 2] == late[0, half + 1], 1.0, 0.0)
    early_decay, late_decay = early[:, half : half + 1], late[:, half : half + 1] * link
    early, late = early[:, :half], late[:, :half]
    chip_state = late_decay * early + late
    chip_decay = late_decay * early_decay

    starts, size, hops, _ = plan(chips, tiles)
    rows = size * half
    tail = jnp.broadcast_to(last, (8, LANES))

    def at(array, t):
        part = array[starts[0] : starts[0] + size]
        for c in range(1, len(starts)):
            part = jnp.where(place <= t - c, array[starts[c] : starts[c] + size], part)
        return part

    carry = jnp.zeros((size, half, LANES), F32)
    received = []
    for t in range(hops):
        send = at(chip_decay, t) * carry + at(chip_state, t)
        send = jnp.concatenate([send.reshape(rows, LANES), tail], axis=0)
        pairs = [(z, z + 1) for z in range(chips - 1) if 0 <= t - z < len(starts)]
        got = lax.ppermute(send, "seq", pairs)
        joined = jnp.where(got[rows] == first, 1.0, 0.0)
        carry = joined * got[:rows].reshape(size, half, LANES)
        received.append(carry)
    parts, done = [], 0
    for c, start in enumerate(starts):
        part = jnp.zeros((size, half, LANES), F32)
        for z in range(1, chips):
            part = jnp.where(place == z, received[c + z - 1], part)
        parts.append(part[done - start :])
        done = start + size
    entering = jnp.concatenate(parts, axis=0)
    onward = link * (early_decay * entering + early)
    mine = jnp.where(second, onward, entering)
    other = lax.ppermute(jnp.where(second, entering, onward), "sub", [(0, 1), (1, 0)])
    return mine, other


def solution(mesh):
    placed = (
        P(("groups", "seq", "sub"), "head"),
        P(("groups", "seq", "sub"), "head"),
        P(("groups", "seq", "sub"), None),
        P(("groups", "seq", "sub"), None),
        P("head", ("seq", "sub")),
        P("head"),
        P("head"),
        P("head"),
        P("head"),
        P(("groups", "seq", "sub")),
        P(("groups", "seq", "sub")),
    )

    return jax.shard_map(
        on_device,
        mesh=mesh,
        in_specs=placed,
        out_specs=P(("groups", "seq", "sub"), "head"),
        check_vma=False,
    )
```

```python
import functools
import math

import jax
import jax.numpy as jnp
import numpy as np
from jax import lax
from jax.experimental import pallas as pl
from jax.experimental.pallas import tpu as pltpu
from jax.sharding import PartitionSpec as P

BLOCK = 256
LANES = 128
LOG2E = math.log2(math.e)
CHUNKS = 2
INNER_VMEM = 16 << 20
EARLY_VMEM = 32 << 20
F32 = jnp.float32
BF16 = jnp.bfloat16


def dot(a, b, contract=((1,), (0,))):
    return lax.dot_general(a, b, (contract, ((), ())), preferred_element_type=F32)


def two_parts(value):
    high = value.astype(BF16)
    low = (value - high.astype(F32)).astype(BF16)
    return high, low


def pick_row(ref, base, count, k, cols):
    row = ref[base : base + 1, cols]
    for j in range(1, count):
        row = jnp.where(k == j, ref[base + j : base + j + 1, cols], row)
    return row


def softplus(v):
    u = jnp.exp(-jnp.abs(v))
    s = u / (2.0 + u)
    q = s * s
    series = jnp.full_like(q, 1.0 / 15.0)
    for odd in (13, 11, 9, 7, 5, 3, 1):
        series = series * q + 1.0 / odd
    return jnp.maximum(v, 0.0) + 2.0 * s * series


def state_kernel(
    heads,
    live_ref,
    docs_ref,
    spot_ref,
    raw_ref,
    bias_ref,
    decay_ref,
    skip_ref,
    doc_row_ref,
    tri_ref,
    hot_ref,
    hot_low_ref,
    x_ref,
    b_ref,
    cum_ref,
    step_ref,
    col_ref,
    enter_ref,
    own_ref,
    sent_ref,
    row_ref,
    pack,
    col_parts,
    inputs_t,
    state,
    scal,
):
    length = raw_ref.shape[0 + 1]
    rows = raw_ref.shape[0]
    count = length // BLOCK
    wide = x_ref.shape[1]
    ends = [docs_ref[j * BLOCK + BLOCK - 1] for j in range(count)]

    @pl.when(pl.program_id(0) == 0)
    def _():
        inputs_t[...] = b_ref[...].T
        pack[...] = jnp.zeros_like(pack)
        pack[0:1, 0:heads] = bias_ref[...]
        pack[1:2, 0:heads] = decay_ref[...]
        params = pack[0:LANES, 0:LANES].T
        lane = lax.broadcasted_iota(jnp.int32, (1, length), 1)
        step = softplus(raw_ref[...] + params[0:rows, 0:1])
        step = jnp.where(lane < live_ref[0] * BLOCK, step, 0.0)
        rate = (-LOG2E * jnp.exp(params[0:rows, 1:2])) * step
        high, _ = two_parts(rate)
        middle, low = two_parts(rate - high.astype(F32))
        tri = tri_ref[...]
        step_ref[...] = step
        for j in range(count):
            piece = slice(j * BLOCK, (j + 1) * BLOCK)
            cum = dot(high[:, piece], tri) + (dot(middle[:, piece], tri) + dot(low[:, piece], tri))
            cum_ref[:, piece] = cum
            same = doc_row_ref[:, piece] == ends[j]
            pack[0:rows, piece] = cum
            pack[rows : 2 * rows, piece] = jnp.where(
                same, step[:, piece] * jnp.exp2(cum[:, BLOCK - 1 :] - cum), 0.0
            )
        pack[LANES - 1 : LANES, :] = doc_row_ref[...].astype(F32)
        for j in range(count):
            piece = slice(j * BLOCK, (j + 1) * BLOCK)
            turned = pack[:, piece].T
            col_ref[piece, :] = turned
            high, low = two_parts(turned)
            col_parts[piece, 0:LANES] = high
            col_parts[piece, LANES:] = low
        head_lane = lax.broadcasted_iota(jnp.int32, (1, LANES), 1) < heads
        before = jnp.zeros((1, LANES), F32)
        scal[...] = jnp.zeros_like(scal)
        for j in range(count):
            end = jnp.where(head_lane, col_ref[(j + 1) * BLOCK - 1 : (j + 1) * BLOCK, :], 0.0)
            scal[j : j + 1, :] = jnp.where(head_lane, jnp.exp2(end), 0.0)
            scal[count + j : count + j + 1, :] = jnp.where(head_lane, jnp.exp2(before), 0.0)
            before = before + end
        scal[2 * count : 2 * count + 1, :] = jnp.where(head_lane, jnp.exp2(before), 0.0)
        scal[2 * count + 1 : 2 * count + 2, 0:heads] = skip_ref[...]

    hot = hot_ref[...]
    high, low = two_parts(scal[...])
    row = dot(high, hot) + dot(low, hot)
    row_ref[...] = row
    hot_low = jnp.concatenate([hot_low_ref[...]] * 2, axis=0)
    state[...] = jnp.zeros_like(state)
    scaled = (x_ref[...].astype(F32) * dot(col_parts[...], hot_low)).astype(BF16)
    for j in range(count):
        piece = slice(j * BLOCK, (j + 1) * BLOCK)
        prior = docs_ref[max(j * BLOCK - 1, 0)]
        passage = row[j : j + 1, :] * jnp.where(ends[j] == prior, 1.0, 0.0)
        old = state[...]
        enter_ref[j] = old.astype(BF16)
        state[...] = passage * old + dot(inputs_t[:, piece], scaled[piece])

    half = state.shape[0] // 2
    total = row[2 * count : 2 * count + 1, :] * jnp.where(ends[count - 1] == docs_ref[0], 1.0, 0.0)
    mine = pl.multiple_of(spot_ref[0] * half, half)
    theirs = pl.multiple_of((1 - spot_ref[0]) * half, half)
    line = lax.broadcasted_iota(jnp.int32, (8, LANES), 0)
    marks = jnp.zeros((8, LANES), F32)
    for at, mark in enumerate((docs_ref[0], docs_ref[length - 1], spot_ref[0], spot_ref[1])):
        marks = jnp.where(line == at + 1, mark.astype(F32), marks)
    for j in range(wide // LANES):
        cols = slice(j * LANES, (j + 1) * LANES)
        foot = jnp.where(line == 0, total[:, cols], marks)
        own_ref[j, 0:half, :] = state[pl.ds(mine, half), cols]
        sent_ref[j, 0:half, :] = state[pl.ds(theirs, half), cols]
        own_ref[j, half:, :] = foot
        sent_ref[j, half:, :] = foot


def prepare_kernel(heads, docs_ref, b_ref, c_ref, col_ref, doc_row_ref, affinity_ref, entry_ref):
    t = lax.broadcasted_iota(jnp.int32, (BLOCK, BLOCK), 0)
    s = lax.broadcasted_iota(jnp.int32, (BLOCK, BLOCK), 1)
    lane = lax.broadcasted_iota(jnp.int32, (1, LANES), 1)
    for j in range(affinity_ref.shape[0]):
        piece = slice(j * BLOCK, (j + 1) * BLOCK)
        block = pl.program_id(0) * affinity_ref.shape[0] + j
        columns = col_ref[piece, :]
        doc_col = columns[:, LANES - 1 :]
        doc_row = doc_row_ref[:, piece].astype(F32)
        affinity_ref[j] = jnp.where(
            (t >= s) & (doc_col == doc_row),
            dot(c_ref[piece, :], b_ref[piece, :], ((1,), (1,))),
            0.0,
        )
        prior_doc = docs_ref[jnp.maximum(block * BLOCK - 1, 0)].astype(F32)
        linked = (doc_col == prior_doc) & (lane < heads)
        high, low = two_parts(jnp.where(linked, jnp.exp2(columns), 0.0))
        entry_ref[piece, 0:LANES] = high
        entry_ref[piece, LANES:] = low


def inner_kernel(
    width,
    first_tile,
    group,
    count,
    live_ref,
    docs_ref,
    x_ref,
    z_ref,
    c_ref,
    cum_ref,
    step_ref,
    col_ref,
    affinity_ref,
    entry_ref,
    enter_ref,
    row_ref,
    hot_ref,
    *refs,
):
    y_ref, f_ref = refs[-2:]
    k = pl.program_id(0)
    half = BLOCK // 2
    per_tile = LANES // width

    @pl.when(k >= live_ref[0])
    def _():
        y_ref[...] = jnp.zeros_like(y_ref)
        f_ref[...] = jnp.zeros_like(f_ref)

    @pl.when(k < live_ref[0])
    def _():
        readout = c_ref[...]
        lane = lax.broadcasted_iota(jnp.int32, (1, LANES), 1)
        nothing = jnp.zeros((BLOCK, LANES), BF16)
        reaches = jnp.where(docs_ref[jnp.maximum(k * BLOCK - 1, 0)] == docs_ref[0], 1.0, 0.0)
        passed = pick_row(row_ref, count, count, k, slice(None)) * reaches
        for q in range(x_ref.shape[1] // (group * LANES)):
            cols = slice(q * group * LANES, (q + 1) * group * LANES)
            x = x_ref[:, cols]
            tops, bottoms, masked = [], [], []
            for u in range(group):
                part = x[:, u * LANES : (u + 1) * LANES]
                for i in range(per_tile):
                    h = (first_tile + q * group + u) * per_tile + i
                    cum = jnp.broadcast_to(col_ref[:, h : h + 1], (BLOCK, LANES))
                    left, right = cum_ref[h : h + 1, :half], cum_ref[h : h + 1, half:]
                    early, late = step_ref[h : h + 1, :half], step_ref[h : h + 1, half:]
                    top = jnp.exp2(jnp.minimum(cum[:half] - left, 0.0))
                    bottom = jnp.exp2(jnp.minimum(cum[half:] - left, 0.0))
                    corner = jnp.exp2(jnp.minimum(cum[half:] - right, 0.0))
                    tops.append((affinity_ref[0, :half, :half] * top * early).astype(BF16))
                    bottoms.append((affinity_ref[0, half:, :half] * bottom * early).astype(BF16))
                    bottoms.append((affinity_ref[0, half:, half:] * corner * late).astype(BF16))
                    mine = (lane >= i * width) & (lane < (i + 1) * width)
                    kept = part * jnp.where(mine, 1.0, 0.0).astype(BF16)
                    masked.append(
                        jnp.concatenate(
                            [kept if v == u else nothing for v in range(group)], axis=1
                        )
                    )
            upper = dot(
                jnp.concatenate(tops, axis=1),
                jnp.concatenate([m[:half] for m in masked], axis=0),
            )
            lower = dot(jnp.concatenate(bottoms, axis=1), jnp.concatenate(masked, axis=0))
            hot = jnp.concatenate([hot_ref[:, cols]] * 2, axis=0)
            enter = dot(entry_ref[...], hot)
            outer = dot(readout, enter_ref[0, :, cols])
            skip = row_ref[2 * count + 1 : 2 * count + 2, cols]
            y = jnp.concatenate([upper, lower], axis=0) + enter * outer + skip * x.astype(F32)
            z = z_ref[:, cols].astype(F32)
            gate = z / (1.0 + jnp.exp2(-LOG2E * z))
            y_ref[:, cols] = y * gate
            f_ref[:, cols] = enter * gate * passed[:, cols]


def join_kernel(spot_ref, own_ref, other_ref, c_ref, *refs):
    pieces = (len(refs) - 3) // 2
    gated_ref, square_ref, total = refs[2 * pieces :]
    second = spot_ref[0] == 1
    total[...] = jnp.zeros_like(total)
    tile = 0
    for y_ref, f_ref in zip(refs[:pieces], refs[pieces : 2 * pieces]):
        wide = chunk_of(y_ref.shape[1], 2 * LANES)
        for c in range(0, y_ref.shape[1], wide):
            parts = []
            for j in range(tile, tile + wide // LANES):
                own, other = own_ref[j].astype(BF16), other_ref[j].astype(BF16)
                parts.append(
                    jnp.concatenate(
                        [jnp.where(second, other, own), jnp.where(second, own, other)], axis=0
                    )
                )
            outer = dot(c_ref[...], jnp.concatenate(parts, axis=1))
            gated = y_ref[:, c : c + wide] + f_ref[:, c : c + wide] * outer
            gated_ref[:, tile * LANES : tile * LANES + wide] = gated
            square = total[...]
            for j in range(0, wide, LANES):
                square = square + gated[:, j : j + LANES] * gated[:, j : j + LANES]
            total[...] = square
            tile += wide // LANES
    square_ref[...] = jnp.sum(total[...].T, axis=0, keepdims=True)


def norm_kernel(
    channels_all, square_ref, more_ref, gain_ref, gated_ref, out_ref, stage, scale, sems
):
    length = gated_ref.shape[0]
    row = lax.rsqrt((square_ref[...] + more_ref[...]) / channels_all + 1e-05)
    copies = []
    for b in range(length // LANES):
        block = slice(b * LANES, (b + 1) * LANES)
        scale[...] = jnp.broadcast_to(row[:, block], (LANES, LANES)).T
        for r in range(0, LANES, 16):
            rows = slice(b * LANES + r, b * LANES + r + 16)
            part = scale[r : r + 16, :]
            for j in range(0, gated_ref.shape[1], LANES):
                cols = slice(j, j + LANES)
                stage[rows, cols] = (gated_ref[rows, cols] * gain_ref[:, cols] * part).astype(BF16)
        copies.append(pltpu.make_async_copy(stage.at[block], out_ref.at[block], sems.at[b]))
        copies[-1].start()
    for copy in copies:
        copy.wait()


def chunk_of(total, most):
    wide = most
    while total % wide:
        wide -= LANES
    return wide


def whole(shape):
    return pl.BlockSpec(shape, lambda k, *_: (0,) * len(shape))


def in_hbm(*values):
    return [pltpu.with_memory_space_constraint(value, pltpu.HBM) for value in values]


SMEM = pl.BlockSpec(memory_space=pltpu.SMEM)
VMEM = pl.BlockSpec(memory_space=pltpu.VMEM)


def plan(chips, tiles):
    chunks = min(CHUNKS, tiles)
    size = -(-tiles // chunks)
    starts = tuple(min(c * size, tiles - size) for c in range(chunks))
    pieces = (tiles,)
    if tiles % 10 == 0:
        pieces = (3 * tiles // 10,) * 2 + (tiles // 5,) * 2
    return starts, size, chunks + chips - 2, pieces


def on_device(
    token_values,
    gate_values,
    state_input,
    state_readout,
    step_raw,
    step_bias,
    decay_log,
    skip_gain,
    norm_gain,
    document_ids,
    live_blocks,
):
    length, channels = token_values.shape
    heads = step_raw.shape[0]
    width = channels // heads
    states = state_input.shape[1]
    half = states // 2
    count = length // BLOCK
    tiles = channels // LANES
    rows = -(-heads // 8) * 8
    scalars = -(-(2 * count + 2) // 16) * 16
    assert lax.axis_size("sub") == 2 and 2 * rows < LANES and states == LANES

    raw = step_raw
    if rows != heads:
        raw = jnp.pad(raw, ((0, rows - heads), (0, 0)))
    doc_row = document_ids.reshape(1, length)
    spot = jnp.stack([lax.axis_index("sub"), lax.axis_index("seq")]).astype(jnp.int32)
    head_of = np.arange(channels)[None, :] // width
    lanes = np.arange(LANES)[:, None]
    hot = jnp.asarray(lanes == head_of, dtype=BF16)
    hot_low = jnp.asarray(lanes == head_of + rows, dtype=BF16)
    tri = jnp.asarray(np.triu(np.ones((BLOCK, BLOCK))), dtype=BF16)

    chunk = chunk_of(channels, 512)
    per_chunk = chunk // LANES
    cum, step, col, enter, own, sent, row = pl.pallas_call(
        functools.partial(state_kernel, heads),
        grid=(channels // chunk,),
        in_specs=[
            SMEM,
            SMEM,
            SMEM,
            whole((rows, length)),
            whole((1, heads)),
            whole((1, heads)),
            whole((1, heads)),
            whole((1, length)),
            whole((BLOCK, BLOCK)),
            pl.BlockSpec((LANES, chunk), lambda c: (0, c)),
            pl.BlockSpec((LANES, chunk), lambda c: (0, c)),
            pl.BlockSpec((length, chunk), lambda c: (0, c)),
            whole((length, states)),
        ],
        out_specs=[
            whole((rows, length)),
            whole((rows, length)),
            whole((length, LANES)),
            pl.BlockSpec((count, states, chunk), lambda c: (0, 0, c)),
            pl.BlockSpec((per_chunk, half + 8, LANES), lambda c: (c, 0, 0)),
            pl.BlockSpec((per_chunk, half + 8, LANES), lambda c: (c, 0, 0)),
            pl.BlockSpec((scalars, chunk), lambda c: (0, c)),
        ],
        out_shape=[
            jax.ShapeDtypeStruct((rows, length), F32),
            jax.ShapeDtypeStruct((rows, length), F32),
            jax.ShapeDtypeStruct((length, LANES), F32),
            jax.ShapeDtypeStruct((count, states, channels), BF16),
            jax.ShapeDtypeStruct((tiles, half + 8, LANES), F32),
            jax.ShapeDtypeStruct((tiles, half + 8, LANES), F32),
            jax.ShapeDtypeStruct((scalars, channels), F32),
        ],
        scratch_shapes=[
            pltpu.VMEM((LANES, length), F32),
            pltpu.VMEM((length, 2 * LANES), BF16),
            pltpu.VMEM((states, length), BF16),
            pltpu.VMEM((states, chunk), F32),
            pltpu.VMEM((scalars, LANES), F32),
        ],
        compiler_params=pltpu.CompilerParams(vmem_limit_bytes=EARLY_VMEM),
        name="shard_state",
    )(
        live_blocks,
        document_ids,
        spot,
        *in_hbm(
            raw,
            step_bias.reshape(1, heads),
            decay_log.reshape(1, heads),
            skip_gain.reshape(1, heads),
            doc_row,
            tri,
            hot,
            hot_low,
            token_values,
            state_input,
        ),
    )

    span = 2 if count % 2 == 0 else 1
    affinity, entry = pl.pallas_call(
        functools.partial(prepare_kernel, heads),
        grid=(count // span,),
        in_specs=[
            SMEM,
            pl.BlockSpec((span * BLOCK, states), lambda k: (k, 0)),
            pl.BlockSpec((span * BLOCK, states), lambda k: (k, 0)),
            pl.BlockSpec((span * BLOCK, LANES), lambda k: (k, 0)),
            pl.BlockSpec((1, span * BLOCK), lambda k: (0, k)),
        ],
        out_specs=[
            pl.BlockSpec((span, BLOCK, BLOCK), lambda k: (k, 0, 0)),
            pl.BlockSpec((span * BLOCK, 2 * LANES), lambda k: (k, 0)),
        ],
        out_shape=[
            jax.ShapeDtypeStruct((count, BLOCK, BLOCK), F32),
            jax.ShapeDtypeStruct((length, 2 * LANES), BF16),
        ],
        compiler_params=pltpu.CompilerParams(vmem_limit_bytes=EARLY_VMEM),
        name="prepare",
    )(document_ids, *in_hbm(state_input, state_readout), col, doc_row)

    pieces = plan(lax.axis_size("seq"), tiles)[3]
    group = 2 if tiles % 2 == 0 else 1
    ys, fs, at = [], [], 0
    x, z, readout, heads_hot = in_hbm(token_values, gate_values, state_readout, hot)
    inputs = (x, z, readout, cum, step, col, affinity, entry, enter, row, heads_hot)
    for size in pieces:
        wide, first = size * LANES, at // size
        y, f = pl.pallas_call(
            functools.partial(inner_kernel, width, at, group, count),
            grid=(count,),
            in_specs=[
                SMEM,
                SMEM,
                pl.BlockSpec((BLOCK, wide), lambda k, q=first: (k, q)),
                pl.BlockSpec((BLOCK, wide), lambda k, q=first: (k, q)),
                pl.BlockSpec((BLOCK, states), lambda k: (k, 0)),
                pl.BlockSpec((rows, BLOCK), lambda k: (0, k)),
                pl.BlockSpec((rows, BLOCK), lambda k: (0, k)),
                pl.BlockSpec((BLOCK, LANES), lambda k: (k, 0)),
                pl.BlockSpec((1, BLOCK, BLOCK), lambda k: (k, 0, 0)),
                pl.BlockSpec((BLOCK, 2 * LANES), lambda k: (k, 0)),
                pl.BlockSpec((1, states, wide), lambda k, q=first: (k, 0, q)),
                pl.BlockSpec((scalars, wide), lambda k, q=first: (0, q)),
                pl.BlockSpec((LANES, wide), lambda k, q=first: (0, q)),
            ],
            out_specs=[pl.BlockSpec((BLOCK, wide), lambda k: (k, 0))] * 2,
            out_shape=[
                jax.ShapeDtypeStruct((length, wide), F32),
                jax.ShapeDtypeStruct((length, wide), F32),
            ],
            cost_estimate=pl.CostEstimate(
                flops=length * wide * 1200,
                bytes_accessed=length * wide * 10,
                transcendentals=0,
            ),
            compiler_params=pltpu.CompilerParams(vmem_limit_bytes=INNER_VMEM),
        )(live_blocks, document_ids, *inputs)
        ys.append(y)
        fs.append(f)
        at += size

    own, other = carry_in(own, sent, half)

    gated, squares = pl.pallas_call(
        join_kernel,
        in_specs=[SMEM] + [VMEM] * (3 + 2 * len(pieces)),
        out_specs=[VMEM, VMEM],
        out_shape=[
            jax.ShapeDtypeStruct((length, channels), F32),
            jax.ShapeDtypeStruct((1, length), F32),
        ],
        scratch_shapes=[pltpu.VMEM((length, LANES), F32)],
        compiler_params=pltpu.CompilerParams(vmem_limit_bytes=16 << 20),
        name="join",
    )(spot, own, other, state_readout, *ys, *fs)

    squares, more = summed(squares, "head")
    return pl.pallas_call(
        functools.partial(norm_kernel, channels * lax.axis_size("head")),
        in_specs=[VMEM] * 4,
        out_specs=pl.BlockSpec(memory_space=pl.ANY),
        out_shape=jax.ShapeDtypeStruct((length, channels), BF16),
        scratch_shapes=[
            pltpu.VMEM((length, channels), BF16),
            pltpu.VMEM((LANES, LANES), F32),
            pltpu.SemaphoreType.DMA((length // LANES,)),
        ],
        compiler_params=pltpu.CompilerParams(vmem_limit_bytes=16 << 20),
        name="norm",
    )(squares, more, norm_gain.reshape(1, channels), gated)


def summed(value, axis):
    size = lax.axis_size(axis)
    if size & (size - 1):
        total = value
        for shift in range(1, size):
            total = total + lax.ppermute(value, axis, [(i, (i + shift) % size) for i in range(size)])
        return total, jnp.zeros_like(value)
    more, shift = jnp.zeros_like(value), 1
    while shift < size:
        value = value + more if shift > 1 else value
        more = lax.ppermute(value, axis, [(i, i ^ shift) for i in range(size)])
        shift *= 2
    return value, more


def carry_in(own, sent, half):
    tiles = own.shape[0]
    chips = lax.axis_size("seq")
    second, place = own[0, half + 3] == 1.0, own[0, half + 4]
    got = lax.ppermute(sent, "sub", [(0, 1), (1, 0)])
    early = jnp.where(second, got, own)
    late = jnp.where(second, own, got)
    first, last = early[0, half + 1], late[0, half + 2]
    link = jnp.where(early[0, half + 2] == late[0, half + 1], 1.0, 0.0)
    early_decay, late_decay = early[:, half : half + 1], late[:, half : half + 1] * link
    early, late = early[:, :half], late[:, :half]
    chip_state = late_decay * early + late
    chip_decay = late_decay * early_decay

    starts, size, hops, _ = plan(chips, tiles)
    rows = size * half
    tail = jnp.broadcast_to(last, (8, LANES))

    def at(array, t):
        part = array[starts[0] : starts[0] + size]
        for c in range(1, len(starts)):
            part = jnp.where(place <= t - c, array[starts[c] : starts[c] + size], part)
        return part

    carry = jnp.zeros((size, half, LANES), F32)
    received = []
    for t in range(hops):
        send = at(chip_decay, t) * carry + at(chip_state, t)
        send = jnp.concatenate([send.reshape(rows, LANES), tail], axis=0)
        pairs = [(z, z + 1) for z in range(chips - 1) if 0 <= t - z < len(starts)]
        got = lax.ppermute(send, "seq", pairs)
        joined = jnp.where(got[rows] == first, 1.0, 0.0)
        carry = joined * got[:rows].reshape(size, half, LANES)
        received.append(carry)
    parts, done = [], 0
    for c, start in enumerate(starts):
        part = jnp.zeros((size, half, LANES), F32)
        for z in range(1, chips):
            part = jnp.where(place == z, received[c + z - 1], part)
        parts.append(part[done - start :])
        done = start + size
    entering = jnp.concatenate(parts, axis=0)
    onward = link * (early_decay * entering + early)
    mine = jnp.where(second, onward, entering)
    other = lax.ppermute(jnp.where(second, entering, onward), "sub", [(0, 1), (1, 0)])
    return mine, other


def solution(mesh):
    placed = (
        P(("groups", "seq", "sub"), "head"),
        P(("groups", "seq", "sub"), "head"),
        P(("groups", "seq", "sub"), None),
        P(("groups", "seq", "sub"), None),
        P("head", ("seq", "sub")),
        P("head"),
        P("head"),
        P("head"),
        P("head"),
        P(("groups", "seq", "sub")),
        P(("groups", "seq", "sub")),
    )

    return jax.shard_map(
        on_device,
        mesh=mesh,
        in_specs=placed,
        out_specs=P(("groups", "seq", "sub"), "head"),
        check_vma=False,
    )
```
